32 devices in a mesh: gs: 8 (over z, y), img: 4 (over x, core).
Axes of the slice: x: 2, y: 2, z: 4, core: 2. Of those that a mesh axis runs over, the one named last changes fastest.
Arguments:
- gaussians: float32 [59, 40960], P(None, ('gs', 'img')), may hold values from -6 to 2048, as said below
- send_slots: int32 [32, 2560], P(('gs', 'img')), may hold values from 0 to 1279, as said below
- tile_lists: int32 [32, 128, 512], P('img', 'gs'), may hold values from -1 to 2559, as said below
- truth: float32 [3, 512, 2048], P(None, 'img', 'gs'), may hold values from 0 to 1
Outputs:
- rendered: float32 [3, 512, 2048], P(None, 'img', 'gs')
- pixel_loss: float32 [512, 2048], P('img', 'gs')
The draws below stay inside these ranges and needn't reach their ends.
Inputs may be any that keep to these rules, and one draw needn't show every extreme that they name: `gaussians`: rows 0 and 1 are pixel positions, row 2 a depth of 10 to 60, rows 3 to 5 log scales, rows 6 to 9 a quaternion whose first component is at least 0.5, row 10 an opacity logit, rows 11 to 58 colour harmonics, 16 for each channel. `send_slots`: row s lists, for each destination device in order, 80 indices of source s's own Gaussians. `tile_lists`: live entries (0 or more) name distinct slots of the owning device's received Gaussians and come first, ordered by increasing depth (row 2) of the Gaussians they name; the rest are -1.
All inputs are finite; a program needn't handle non-finite values.
Results may differ from the reference program's by a relative error of at most 0.0003.
Values sent between devices are 32-bit elements; how exact they have to be, the bound alone decides.
No kernel may reach another device: no remote copies, remote signals or barrier semaphores. Data moves between devices by JAX's collectives and lax.ppermute only.
A program may use at most 64 MiB of HBM per device.

```python
import math
import jax
import jax.numpy as jnp
from jax import lax

TILE = 16
LIST = 512
TC = 16
TR = 8
HOME = 40
G_DEV = 1280
CAP = 80
SLOTS = 2560
HEIGHT = 512
WIDTH = 2048
N_GS = 8
N_IMG = 4
DEVICES = 32


def home_perms(key):
    subkeys = jax.random.split(jax.random.fold_in(key, 7), DEVICES)

    def shuffle(subkey):
        return jax.random.permutation(subkey, G_DEV)
    return jax.vmap(shuffle)(subkeys).astype(jnp.int32)


def column_fields(key):
    permuted = home_perms(key)
    home_ids = (jnp.argsort(permuted, axis=1) // HOME).reshape(DEVICES * G_DEV).astype(jnp.int32)
    amount = DEVICES * G_DEV
    subkeys = jax.random.split(jax.random.fold_in(key, 5), 4)
    place_x = home_ids // N_IMG * (TILE * TC) + jax.random.randint(subkeys[0], (amount,), 0, TILE * TC)
    place_y = home_ids % N_IMG * (TILE * TR) + jax.random.randint(subkeys[1], (amount,), 0, TILE * TR)
    size_class = jax.random.randint(subkeys[2], (amount,), 0, 5)
    depth_rank = jax.random.permutation(subkeys[3], amount).astype(jnp.int32)
    return (place_x.astype(jnp.int32), place_y.astype(jnp.int32), size_class.astype(jnp.int32), depth_rank)


def draw_send_slots(key, part):
    permuted = home_perms(key)
    targets = jnp.arange(DEVICES, dtype=jnp.int32)
    left_ids = (targets // N_IMG - 1) % N_GS * N_IMG + targets % N_IMG
    home_ids = jnp.stack([targets, left_ids], axis=1)
    picked = (home_ids[:, :, None] * HOME + jnp.arange(HOME, dtype=jnp.int32)[None, None, :]).reshape(DEVICES * CAP)
    return permuted[:, picked]


def draw_gaussians(key, part):
    place_x, place_y, size_class, depth_rank = column_fields(key)
    amount = DEVICES * G_DEV
    subkeys = jax.random.split(jax.random.fold_in(key, 3), 9)
    mean_x = place_x.astype(jnp.float32) + jax.random.uniform(subkeys[0], (amount,))
    mean_y = place_y.astype(jnp.float32) + jax.random.uniform(subkeys[1], (amount,))
    mean_z = 10.0 + 50.0 * (depth_rank.astype(jnp.float32) + jax.random.uniform(subkeys[2], (amount,))) / float(amount)
    top = math.log(8.0) + size_class.astype(jnp.float32) * math.log(2.0)
    log_scales = top[None, :] - jax.random.uniform(subkeys[3], (3, amount), minval=0.0, maxval=math.log(2.0))
    quat_w = jax.random.uniform(subkeys[4], (1, amount), minval=0.5, maxval=1.0)
    quat_rest = jax.random.uniform(subkeys[5], (3, amount), minval=-1.0, maxval=1.0)
    logits = jax.random.uniform(subkeys[6], (1, amount), minval=-6.0, maxval=-2.0)
    lowest = 0.5 * jax.random.truncated_normal(subkeys[7], -3.0, 3.0, (3, 1, amount))
    higher = 0.2 * jax.random.truncated_normal(subkeys[8], -3.0, 3.0, (3, 15, amount))
    harmonics = jnp.concatenate([lowest, higher], axis=1).reshape(48, amount)
    return jnp.concatenate([mean_x[None], mean_y[None], mean_z[None], log_scales, quat_w, quat_rest, logits, harmonics], axis=0)


def draw_tile_lists(key, part):
    place_x, place_y, size_class, depth_rank = column_fields(key)
    reach_table = jnp.array([26, 50, 98, 194, 386], dtype=jnp.int32)
    reach = reach_table[size_class]
    send = draw_send_slots(key, part)
    routed = send.reshape(DEVICES, DEVICES, CAP) + (jnp.arange(DEVICES, dtype=jnp.int32) * G_DEV)[:, None, None]
    received = jnp.transpose(routed, (1, 0, 2)).reshape(DEVICES, SLOTS)
    subkeys = jax.random.split(jax.random.fold_in(key, 11), 2)
    tile_rows = TR * N_IMG
    tile_cols = TC * N_GS
    dense = jax.random.randint(subkeys[0], (tile_rows, tile_cols), 0, 8) == 0
    wanted = jnp.where(dense, LIST, jax.random.randint(subkeys[1], (tile_rows, tile_cols), 32, 129)).astype(jnp.int32)
    cols = jnp.arange(tile_cols, dtype=jnp.int32)
    slot_pos = jnp.arange(SLOTS, dtype=jnp.int32)
    position = jnp.arange(LIST, dtype=jnp.int32)

    def one_row(inputs):
        row_number, wanted_row = inputs
        owners = cols // TC * N_IMG + row_number // TR
        columns = received[owners]
        gauss_x = place_x[columns]
        gauss_y = place_y[columns]
        gauss_reach = reach[columns]
        left_x = (cols * TILE)[:, None]
        top_y = row_number * TILE
        gap_x = jnp.maximum(jnp.maximum(left_x - gauss_x, gauss_x - (left_x + TILE)), 0)
        gap_y = jnp.maximum(jnp.maximum(top_y - gauss_y, gauss_y - (top_y + TILE)), 0)
        candidate = (gap_x <= gauss_reach) & (gap_y <= gauss_reach)
        order_key = jnp.where(candidate, depth_rank[columns], DEVICES * G_DEV + slot_pos[None, :])
        order = jnp.argsort(order_key, axis=1, stable=True).astype(jnp.int32)
        if SLOTS >= LIST:
            order = order[:, :LIST]
        else:
            order = jnp.pad(order, ((0, 0), (0, LIST - SLOTS)))
        live_count = jnp.minimum(jnp.sum(candidate.astype(jnp.int32), axis=1), wanted_row)
        return jnp.where(position[None, :] < live_count[:, None], order, -1).astype(jnp.int32)
    return lax.map(one_row, (jnp.arange(tile_rows, dtype=jnp.int32), wanted))


def steps_of(key, shape, pieces, smallest, high):
    loudness = 1.0
    for dim, shards_of in pieces:
        steps = jax.random.uniform(jax.random.fold_in(jax.random.fold_in(key, 6), dim), (shards_of,), jnp.float32, smallest / len(pieces), high / len(pieces))
        loudness = loudness * jnp.repeat(jnp.exp(steps), shape[dim] // shards_of).reshape((-1,) + (1,) * (len(shape) - 1 - dim))
    return loudness


def setup_inputs(seed: int = 0) -> dict:
    key_of = jax.random.split(jax.random.key(seed), 5)
    return {
        "gaussians": draw_gaussians(jax.random.fold_in(key_of[4], 71), 0),
        "send_slots": draw_send_slots(jax.random.fold_in(key_of[4], 71), 0),
        "tile_lists": draw_tile_lists(jax.random.fold_in(key_of[4], 71), 0),
        "truth": jnp.clip(1.0 * jax.random.uniform(key_of[3], (3, HEIGHT, WIDTH), jnp.float32) ** steps_of(key_of[3], (3, HEIGHT, WIDTH), ((1, 4), (2, 8)), -0.2, 0.2), 0.0, 1.0),
    }


coef_zero = 0.28209479177387814
coef_one = 0.4886025119029199
coef_two = [1.0925484305920792, -1.0925484305920792, 0.31539156525252005, -1.0925484305920792, 0.5462742152960396]
coef_three = [-0.5900435899266435, 2.890611442640554, -0.4570457994644658, 0.3731763325901154, -0.4570457994644658, 1.445305721320277, -0.5900435899266435]
camera_z = -3000.0
ssim_share = 0.2
stable_one = 0.0001
stable_two = 0.0009

def project(gauss):
    mean_x, mean_y, mean_z = (gauss[0], gauss[1], gauss[2])
    squared = jnp.exp(2.0 * gauss[3:6])
    rotation = gauss[6:10] / jnp.sqrt(lax.optimization_barrier(jnp.sum(gauss[6:10] * gauss[6:10], axis=0)))
    quat_w, quat_x, quat_y, quat_z = (rotation[0], rotation[1], rotation[2], rotation[3])
    first_a = 1.0 - 2.0 * (quat_y * quat_y + quat_z * quat_z)
    first_b = 2.0 * (quat_x * quat_y - quat_w * quat_z)
    first_c = 2.0 * (quat_x * quat_z + quat_w * quat_y)
    second_a = 2.0 * (quat_x * quat_y + quat_w * quat_z)
    second_b = 1.0 - 2.0 * (quat_x * quat_x + quat_z * quat_z)
    second_c = 2.0 * (quat_y * quat_z - quat_w * quat_x)
    cov_xx = first_a * first_a * squared[0] + first_b * first_b * squared[1] + first_c * first_c * squared[2] + 0.3
    cov_xy = first_a * second_a * squared[0] + first_b * second_b * squared[1] + first_c * second_c * squared[2]
    cov_yy = second_a * second_a * squared[0] + second_b * second_b * squared[1] + second_c * second_c * squared[2] + 0.3
    determinant = cov_xx * cov_yy - cov_xy * cov_xy
    opacity = jax.nn.sigmoid(gauss[10])
    delta_z = mean_z - camera_z
    length = jnp.sqrt(mean_x * mean_x + mean_y * mean_y + delta_z * delta_z)
    dir_x, dir_y, dir_z = (mean_x / length, mean_y / length, delta_z / length)
    sq_x, sq_y, sq_z = (dir_x * dir_x, dir_y * dir_y, dir_z * dir_z)
    prod_xy, prod_yz, prod_xz = (dir_x * dir_y, dir_y * dir_z, dir_x * dir_z)
    harmonic_basis = jnp.stack([coef_zero * jnp.ones_like(dir_x), -coef_one * dir_y, coef_one * dir_z, -coef_one * dir_x, coef_two[0] * prod_xy, coef_two[1] * prod_yz, coef_two[2] * (2.0 * sq_z - sq_x - sq_y), coef_two[3] * prod_xz, coef_two[4] * (sq_x - sq_y), coef_three[0] * dir_y * (3.0 * sq_x - sq_y), coef_three[1] * prod_xy * dir_z, coef_three[2] * dir_y * (4.0 * sq_z - sq_x - sq_y), coef_three[3] * dir_z * (2.0 * sq_z - 3.0 * sq_x - 3.0 * sq_y), coef_three[4] * dir_x * (4.0 * sq_z - sq_x - sq_y), coef_three[5] * dir_z * (sq_x - sq_y), coef_three[6] * dir_x * (sq_x - 3.0 * sq_y)])
    harmonics = gauss[11:59].reshape(3, 16, gauss.shape[1])
    colour = jnp.maximum(lax.optimization_barrier(jnp.sum(harmonics * harmonic_basis[None], axis=1)) + 0.5, 0.0)
    return jnp.stack([mean_x, mean_y, cov_yy / determinant, -cov_xy / determinant, cov_xx / determinant, opacity, colour[0], colour[1], colour[2]])

def splat_alpha(params, live_mask, pix_x, pix_y):
    delta_x = pix_x[:, :, None] - params[0][:, None, :]
    delta_y = pix_y[:, :, None] - params[1][:, None, :]
    power = -0.5 * (params[2][:, None, :] * delta_x * delta_x + params[4][:, None, :] * delta_y * delta_y)
    power = power - params[3][:, None, :] * delta_x * delta_y
    return jnp.where(live_mask[:, None, :], params[5][:, None, :] * jnp.exp(power), 0.0)

def window():
    offsets = jnp.arange(11, dtype=jnp.float32) - 5.0
    weights = jnp.exp(-offsets * offsets / 4.5)
    return weights / jnp.sum(weights)

def loss_from(filtered, rendered, truth):
    mean_r, mean_t = (filtered[0:3], filtered[3:6])
    variance_r = filtered[6:9] - mean_r * mean_r
    variance_t = filtered[9:12] - mean_t * mean_t
    covariance = filtered[12:15] - mean_r * mean_t
    similarity = (2.0 * mean_r * mean_t + stable_one) * (2.0 * covariance + stable_two) / ((mean_r * mean_r + mean_t * mean_t + stable_one) * (variance_r + variance_t + stable_two))
    return (1.0 - ssim_share) * lax.optimization_barrier(jnp.mean(jnp.abs(rendered - truth), axis=0)) + ssim_share * (1.0 - lax.optimization_barrier(jnp.mean(similarity, axis=0)))

def reference(gaussians, send_slots, tile_lists, truth):
    splats = project(gaussians)
    sources = jnp.arange(DEVICES, dtype=jnp.int32)
    routed = send_slots.reshape(DEVICES, DEVICES, CAP) + (sources * G_DEV)[:, None, None]
    slot_ids = jnp.transpose(routed, (1, 0, 2)).reshape(DEVICES, DEVICES * CAP)
    tile_rows, tile_cols = (tile_lists.shape[0], tile_lists.shape[1])
    row_index = jnp.arange(tile_rows, dtype=jnp.int32)
    col_index = jnp.arange(tile_cols, dtype=jnp.int32)
    owners = (col_index // TC)[None, :] * N_IMG + (row_index // TR)[:, None]
    pixels = jnp.arange(TILE * TILE, dtype=jnp.int32)

    def render_row(inputs):
        lists_row, owner_row, row_number = inputs
        live_mask = lists_row >= 0
        chosen = slot_ids[owner_row[:, None], jnp.maximum(lists_row, 0)]
        params = splats[:, chosen]
        pix_x = (col_index[:, None] * TILE + pixels[None, :] % TILE).astype(jnp.float32) + 0.5
        pix_y = jnp.broadcast_to((row_number * TILE + pixels // TILE).astype(jnp.float32) + 0.5, pix_x.shape)
        alphas = splat_alpha(params, live_mask, pix_x, pix_y)
        log_keep = jnp.log1p(-alphas)
        before = jnp.cumsum(log_keep, axis=2) - log_keep
        weight = jnp.exp(before) * alphas
        return jnp.einsum('qpk,cqk->cqp', weight, params[6:9], precision=lax.Precision.HIGHEST)
    colours = lax.map(render_row, (tile_lists, owners, row_index))
    rendered = colours.reshape(tile_rows, 3, tile_cols, TILE, TILE).transpose(1, 0, 3, 2, 4)
    rendered = rendered.reshape(3, tile_rows * TILE, tile_cols * TILE)
    quantities = jnp.concatenate([rendered, truth, rendered * rendered, truth * truth, rendered * truth])
    padded = jnp.pad(quantities, ((0, 0), (5, 5), (5, 5)))
    img_height, img_width = (rendered.shape[1], rendered.shape[2])
    weights = window()
    row_filtered = jnp.zeros((15, img_height, img_width + 10), jnp.float32)
    for offset in range(11):
        row_filtered = row_filtered + weights[offset] * padded[:, offset:offset + img_height, :]
    filtered = jnp.zeros((15, img_height, img_width), jnp.float32)
    for offset in range(11):
        filtered = filtered + weights[offset] * row_filtered[:, :, offset:offset + img_width]
    return (rendered, loss_from(filtered, rendered, truth))
```

```python
import functools

import jax
import jax.numpy as jnp
import numpy as np
from jax import lax
from jax.experimental import pallas as pl
from jax.experimental.pallas import tpu as pltpu
from jax.sharding import PartitionSpec as P

TILE = 16
LANES = 128
SUBS = 8
PARAMS = 9
LOG2E = 1.4426950408889634

coef_zero = 0.28209479177387814
coef_one = 0.4886025119029199
coef_two = [
    1.0925484305920792,
    -1.0925484305920792,
    0.31539156525252005,
    -1.0925484305920792,
    0.5462742152960396,
]
coef_three = [
    -0.5900435899266435,
    2.890611442640554,
    -0.4570457994644658,
    0.3731763325901154,
    -0.4570457994644658,
    1.445305721320277,
    -0.5900435899266435,
]
camera_z = -3000.0
ssim_share = 0.2
stable_one = 0.0001
stable_two = 0.0009


def extended(value, sides, width):
    for axis, dim in sides:
        size, length = (lax.axis_size(axis), value.shape[dim])
        up = [(i, (i + 1) % size) for i in range(size - 1)]
        down = [(j, i) for i, j in up]
        last = lax.slice_in_dim(value, length - width, length, axis=dim)
        first = lax.slice_in_dim(value, 0, width, axis=dim)
        before = lax.ppermute(last, axis, up)
        after = lax.ppermute(first, axis, down)
        value = jnp.concatenate([before, value, after], axis=dim)
    return value


def window():
    offsets = jnp.arange(11, dtype=jnp.float32) - 5.0
    weights = jnp.exp(-offsets * offsets / 4.5)
    return weights / jnp.sum(weights)


def band_matrix(outputs, inputs_len, sign):
    difference = sign * (
        jnp.arange(inputs_len, dtype=jnp.int32)[None, :]
        - jnp.arange(outputs, dtype=jnp.int32)[:, None]
    )
    offsets = jnp.arange(11, dtype=jnp.int32)
    return jnp.sum(
        jnp.where(difference[:, :, None] == offsets[None, None, :], window()[None, None, :], 0.0),
        axis=2,
    )


def loss_from(filtered, rendered, truth):
    mean_r, mean_t = (filtered[0:3], filtered[3:6])
    variance_r = filtered[6:9] - mean_r * mean_r
    variance_t = filtered[9:12] - mean_t * mean_t
    covariance = filtered[12:15] - mean_r * mean_t
    similarity = (
        (2.0 * mean_r * mean_t + stable_one)
        * (2.0 * covariance + stable_two)
        / (
            (mean_r * mean_r + mean_t * mean_t + stable_one)
            * (variance_r + variance_t + stable_two)
        )
    )
    return (1.0 - ssim_share) * jnp.mean(jnp.abs(rendered - truth), axis=0) + ssim_share * (
        1.0 - jnp.mean(similarity, axis=0)
    )


def iota(shape, dim):
    return lax.broadcasted_iota(jnp.int32, shape, dim)


def lane_take(values, index):
    return jnp.take_along_axis(values, index, axis=1, mode="promise_in_bounds")


def sublane_take(values, index):
    return jnp.take_along_axis(values, index, axis=0, mode="promise_in_bounds")


def as_bf16(value):
    return value.astype(jnp.bfloat16).astype(jnp.float32)


def three_parts(value):
    high = as_bf16(value)
    rest = value - high
    middle = as_bf16(rest)
    return high, middle, rest - middle


def project(row):
    mean_x, mean_y, mean_z = row(0), row(1), row(2)
    squared = [jnp.exp(2.0 * row(3 + k)) for k in range(3)]
    quat = [row(6 + k) for k in range(4)]
    norm = jnp.sqrt(quat[0] * quat[0] + quat[1] * quat[1] + quat[2] * quat[2] + quat[3] * quat[3])
    quat_w, quat_x, quat_y, quat_z = [part / norm for part in quat]
    first = [
        1.0 - 2.0 * (quat_y * quat_y + quat_z * quat_z),
        2.0 * (quat_x * quat_y - quat_w * quat_z),
        2.0 * (quat_x * quat_z + quat_w * quat_y),
    ]
    second = [
        2.0 * (quat_x * quat_y + quat_w * quat_z),
        1.0 - 2.0 * (quat_x * quat_x + quat_z * quat_z),
        2.0 * (quat_y * quat_z - quat_w * quat_x),
    ]

    def weighted(left, right):
        return (
            left[0] * right[0] * squared[0]
            + left[1] * right[1] * squared[1]
            + left[2] * right[2] * squared[2]
        )

    cov_xx = weighted(first, first) + 0.3
    cov_xy = weighted(first, second)
    cov_yy = weighted(second, second) + 0.3
    determinant = cov_xx * cov_yy - cov_xy * cov_xy
    log_opacity = -LOG2E * jnp.log(1.0 + jnp.exp(-row(10)))
    delta_z = mean_z - camera_z
    length = jnp.sqrt(mean_x * mean_x + mean_y * mean_y + delta_z * delta_z)
    dir_x, dir_y, dir_z = (mean_x / length, mean_y / length, delta_z / length)
    sq_x, sq_y, sq_z = (dir_x * dir_x, dir_y * dir_y, dir_z * dir_z)
    prod_xy, prod_yz, prod_xz = (dir_x * dir_y, dir_y * dir_z, dir_x * dir_z)
    basis = [
        coef_zero * jnp.ones_like(dir_x),
        -coef_one * dir_y,
        coef_one * dir_z,
        -coef_one * dir_x,
        coef_two[0] * prod_xy,
        coef_two[1] * prod_yz,
        coef_two[2] * (2.0 * sq_z - sq_x - sq_y),
        coef_two[3] * prod_xz,
        coef_two[4] * (sq_x - sq_y),
        coef_three[0] * dir_y * (3.0 * sq_x - sq_y),
        coef_three[1] * prod_xy * dir_z,
        coef_three[2] * dir_y * (4.0 * sq_z - sq_x - sq_y),
        coef_three[3] * dir_z * (2.0 * sq_z - 3.0 * sq_x - 3.0 * sq_y),
        coef_three[4] * dir_x * (4.0 * sq_z - sq_x - sq_y),
        coef_three[5] * dir_z * (sq_x - sq_y),
        coef_three[6] * dir_x * (sq_x - 3.0 * sq_y),
    ]
    colours = []
    for channel in range(3):
        total = row(11 + 16 * channel) * basis[0]
        for k in range(1, 16):
            total = total + row(11 + 16 * channel + k) * basis[k]
        colours.append(jnp.maximum(total + 0.5, 0.0))
    return [
        mean_x,
        mean_y,
        (-0.5 * LOG2E) * (cov_yy / determinant),
        LOG2E * (cov_xy / determinant),
        (-0.5 * LOG2E) * (cov_xx / determinant),
        log_opacity,
    ] + colours


def pack_kernel(cap, gauss_ref, send_ref, out_ref, table_ref, index_ref):
    targets = out_ref.shape[0]
    chunks = gauss_ref.shape[1] // LANES
    spare = LANES - cap
    rows = project(lambda k: gauss_ref[k : k + 1, :])
    for k in range(PARAMS):
        table_ref[k : k + 1, :] = rows[k]
    lane = iota((SUBS, LANES), 1)
    sub = iota((SUBS, LANES), 0)
    send_chunks = send_ref.shape[1] // LANES
    for target in range(targets):
        chunk, shift = divmod(target * cap, LANES)

        def piece(c):
            c = min(c, send_chunks - 1)
            return jnp.broadcast_to(send_ref[0:1, c * LANES : (c + 1) * LANES], (SUBS, LANES))

        index = piece(chunk)
        if shift:
            index = jnp.where(
                lane < LANES - shift,
                pltpu.roll(index, LANES - shift, axis=1),
                pltpu.roll(piece(chunk + 1), LANES - shift, axis=1),
            )
        result = index
        for r in range(-(-cap // spare)):
            moved = pltpu.roll(index, (cap - r * spare) % LANES, axis=1)
            result = jnp.where((lane >= cap) & (sub == r), moved, result)
        index_ref[target] = result

    def one(target, carry):
        index = index_ref[target]
        low, high = index & (LANES - 1), index >> 7
        left = jnp.zeros((SUBS, LANES), jnp.float32)
        right = left
        for c in range(chunks):
            hit = high == c
            part = lane_take(table_ref[0:SUBS, c * LANES : (c + 1) * LANES], low)
            left = jnp.where(hit, part, left)
            last = jnp.broadcast_to(
                table_ref[SUBS : SUBS + 1, c * LANES : (c + 1) * LANES], (SUBS, LANES)
            )
            right = jnp.where(hit, lane_take(last, low), right)
        out_ref[target] = jnp.where(lane < cap, left, right)
        return carry

    lax.fori_loop(0, targets, one, 0)


def sort_kernel(cols_here, lists_ref, index_ref, meta_ref, centre_ref):
    tiles, length = lists_ref.shape
    lists = lists_ref[...]
    live = jnp.sum((lists >= 0).astype(jnp.float32), axis=1, keepdims=True)
    live = jnp.broadcast_to(live, (tiles, tiles))
    down, across = iota((tiles, tiles), 0), iota((tiles, tiles), 1)
    live_row = jnp.sum(jnp.where(down == across, live, 0.0), axis=0, keepdims=True)
    ahead = (live > live_row) | ((live == live_row) & (down < across))
    rank_row = jnp.sum(ahead.astype(jnp.float32), axis=0, keepdims=True)
    behind = (live_row > live) | ((live_row == live) & (across < down))
    rank = jnp.sum(behind.astype(jnp.float32), axis=1, keepdims=True)
    select = (rank_row == down.astype(jnp.float32)).astype(jnp.float32)
    placed = (rank == across.astype(jnp.float32)).astype(jnp.float32)
    live_sorted = jnp.sum(placed * live, axis=0, keepdims=True)
    tile_sorted = jnp.sum(placed * down.astype(jnp.float32), axis=0, keepdims=True)
    meta_ref[0:1, :] = live_sorted.astype(jnp.int32)
    meta_ref[1:2, :] = tile_sorted.astype(jnp.int32)
    tile = jnp.sum(select * across.astype(jnp.float32), axis=1, keepdims=True).astype(jnp.int32)
    tile = jnp.broadcast_to(tile, (tiles, tiles))
    tile_row = lax.div(tile, cols_here)
    tile_col = tile - tile_row * cols_here
    tile_row = tile_row + lax.axis_index("img") * (tiles // cols_here)
    tile_col = tile_col + lax.axis_index("gs") * cols_here
    centre_ref[0] = (tile_col * TILE + TILE // 2).astype(jnp.float32)
    centre_ref[1] = (tile_row * TILE + TILE // 2).astype(jnp.float32)
    high = (lists >> 7).astype(jnp.float32).astype(jnp.bfloat16)
    low = (lists & (LANES - 1)).astype(jnp.float32).astype(jnp.bfloat16)
    select = select.astype(jnp.bfloat16)
    high = jnp.dot(select, high, preferred_element_type=jnp.float32)
    low = jnp.dot(select, low, preferred_element_type=jnp.float32)
    index_ref[...] = high.astype(jnp.int32) * LANES + low.astype(jnp.int32)


def basis_matrix():
    local = np.arange(TILE) - 7.5
    kinds = [[(0, local**0), (1, local), (2, local**2)], [(3, local**0), (4, local)]]
    kinds += [[(k, local**0)] for k in range(5, 9)]
    matrix = np.zeros((2 * LANES, len(kinds) * LANES), np.float32)
    for kind, terms in enumerate(kinds):
        for coefficient, values in terms:
            for part in range(3):
                for t in range(SUBS):
                    start = kind * LANES + t * TILE
                    matrix[(coefficient * 3 + part) * SUBS + t, start : start + TILE] = values
    return jnp.asarray(matrix, jnp.bfloat16)


def render_kernel(
    cap, cols_here, meta_ref, recv_ref, index_ref, centre_ref, basis_ref, out_ref, table_ref, rows_ref
):
    sources = recv_ref.shape[0]
    tiles, list_len = index_ref.shape
    chunks = table_ref.shape[1] // LANES
    spare = LANES - cap
    lane = iota((SUBS, LANES), 1)
    sub = iota((SUBS, LANES), 0)
    for source in range(sources):
        value = recv_ref[source]
        last = jnp.zeros((SUBS, LANES), jnp.float32)
        for r in range(-(-cap // spare)):
            row = jnp.broadcast_to(value[r : r + 1, :], (SUBS, LANES))
            moved = pltpu.roll(row, (r * spare - cap) % LANES, axis=1)
            last = jnp.where((lane >= r * spare) & (lane < (r + 1) * spare), moved, last)
        chunk, shift = divmod(source * cap, LANES)
        here = min(cap, LANES - shift)
        if shift:
            value = pltpu.roll(value, shift, axis=1)
            last = pltpu.roll(last, shift, axis=1)
        for c, start, end, lo in ((chunk, shift, shift + here, 0), (chunk + 1, 0, cap - here, 1)):
            if end > start:
                table_ref[0:SUBS, c * LANES + start : c * LANES + end] = value[:, start:end]
                table_ref[SUBS : SUBS + 1, c * LANES + start : c * LANES + end] = last[0:1, start:end]

    up = (sub.astype(jnp.float32) + 0.5)
    up_squared = up * up
    flip = (SUBS - 1) - sub
    zero = jnp.zeros((SUBS, LANES), jnp.float32)

    def group(g, carry):
        start = pl.multiple_of(g * SUBS, SUBS)
        count = meta_ref[0, g * SUBS]
        centre_x = centre_ref[0, pl.ds(start, SUBS), :]
        centre_y = centre_ref[1, pl.ds(start, SUBS), :]

        def block(b, state):
            index = index_ref[pl.ds(start, SUBS), pl.ds(pl.multiple_of(b * LANES, LANES), LANES)]
            live = index >= 0
            safe = jnp.maximum(index, 0)
            low, high = safe & (LANES - 1), safe >> 7

            def chunk(c, params):
                hit = high == c
                at = pl.ds(pl.multiple_of(c * LANES, LANES), LANES)
                return tuple(
                    jnp.where(
                        hit,
                        lane_take(jnp.broadcast_to(table_ref[p : p + 1, at], (SUBS, LANES)), low),
                        params[p],
                    )
                    for p in range(PARAMS)
                )

            params = lax.fori_loop(0, chunks, chunk, (zero,) * PARAMS, unroll=4)
            u = params[0] - centre_x
            v = params[1] - centre_y
            quad_x, quad_xy, quad_y = params[2:5]
            slope_x = quad_x * u
            slope_y = quad_y * v
            constant = params[5] + slope_x * u + slope_y * v + quad_xy * u * v
            coefficients = [
                jnp.where(live, constant, -1e5),
                jnp.where(live, -2.0 * slope_x - quad_xy * v, 0.0),
                jnp.where(live, quad_x, 0.0),
                jnp.where(live, -2.0 * slope_y - quad_xy * u, 0.0),
                jnp.where(live, quad_xy, 0.0),
                jnp.where(live, quad_y, 0.0),
            ] + list(params[6:9])
            parts = [part for value in coefficients for part in three_parts(value)]
            parts += [zero] * (2 * LANES // SUBS - len(parts))
            stacked = jnp.concatenate(parts, axis=0).T.astype(jnp.bfloat16)
            for kind in range(6):
                rows_ref[kind, 0:LANES, :] = jnp.dot(
                    stacked,
                    basis_ref[:, kind * LANES : (kind + 1) * LANES],
                    preferred_element_type=jnp.float32,
                )
            steps = (jnp.minimum(count - b * LANES, LANES) + SUBS - 1) >> 3

            def eight(s, state):
                left_a, left_b, ra, ga, ba, rb, gb, bb = state
                for q in range(SUBS):
                    def row(kind):
                        return rows_ref[kind, pl.ds(s * SUBS + q, SUBS, stride=0), :]

                    even = row(0) + up_squared * row(2)
                    odd = up * row(1)
                    alpha_a = jnp.exp2(even - odd)
                    alpha_b = jnp.exp2(even + odd)
                    weight_a = left_a * alpha_a
                    weight_b = left_b * alpha_b
                    left_a = left_a - weight_a
                    left_b = left_b - weight_b
                    red, green, blue = row(3), row(4), row(5)
                    ra, ga, ba = ra + weight_a * red, ga + weight_a * green, ba + weight_a * blue
                    rb, gb, bb = rb + weight_b * red, gb + weight_b * green, bb + weight_b * blue
                return left_a, left_b, ra, ga, ba, rb, gb, bb

            return lax.fori_loop(0, steps, eight, state)

        one = jnp.ones((SUBS, LANES), jnp.float32)
        state = lax.fori_loop(
            0, (count + LANES - 1) >> 7, block, (one, one) + (zero,) * 6
        )
        halves = [sublane_take(value, flip) for value in state[2:5]] + list(state[5:8])
        for t in range(SUBS):
            tile = meta_ref[1, g * SUBS + t]
            tile_row = tile // cols_here
            column = (tile - tile_row * cols_here) * TILE
            shift = column & (LANES - 1)
            at = pl.ds(pl.multiple_of(column - shift, LANES), LANES)
            mask = (lane >= shift) & (lane < shift + TILE)
            for half in range(2):
                to = pl.ds(pl.multiple_of(tile_row * TILE + half * SUBS, SUBS), SUBS)
                for channel in range(3):
                    moved = pltpu.roll(
                        halves[half * 3 + channel], (shift - t * TILE) & (LANES - 1), axis=1
                    )
                    pltpu.store(out_ref.at[channel, to, at], moved, mask=mask)
        return carry

    lax.fori_loop(0, tiles // SUBS, group, 0)


VMEM = pl.BlockSpec(memory_space=pltpu.VMEM)
SMEM = pl.BlockSpec(memory_space=pltpu.SMEM)


def on_device(gaussians, send_slots, tile_lists, truth):
    axes = ("gs", "img")
    devices = lax.axis_size(axes)
    cap = send_slots.shape[1] // devices
    count = gaussians.shape[1]
    rows_here, cols_here, list_len = tile_lists.shape
    tiles = rows_here * cols_here
    slots = send_slots.shape[1]
    packed = pl.pallas_call(
        functools.partial(pack_kernel, cap),
        out_shape=jax.ShapeDtypeStruct((devices, SUBS, LANES), jnp.float32),
        in_specs=[VMEM, VMEM],
        out_specs=VMEM,
        scratch_shapes=[
            pltpu.VMEM((2 * SUBS, count), jnp.float32),
            pltpu.VMEM((devices, SUBS, LANES), jnp.int32),
        ],
        name="pack",
    )(gaussians, send_slots)
    arrived = lax.all_to_all(packed, axes, split_axis=0, concat_axis=0, tiled=True)
    index, meta, centre = pl.pallas_call(
        functools.partial(sort_kernel, cols_here),
        out_shape=(
            jax.ShapeDtypeStruct((tiles, list_len), jnp.int32),
            jax.ShapeDtypeStruct((SUBS, tiles), jnp.int32),
            jax.ShapeDtypeStruct((2, tiles, LANES), jnp.float32),
        ),
        in_specs=[VMEM],
        out_specs=(VMEM, VMEM, VMEM),
        name="order",
    )(tile_lists.reshape(tiles, list_len))
    height, width = rows_here * TILE, cols_here * TILE
    rendered = pl.pallas_call(
        functools.partial(render_kernel, cap, cols_here),
        out_shape=jax.ShapeDtypeStruct((3, height, width), jnp.float32),
        in_specs=[SMEM, VMEM, VMEM, VMEM, VMEM],
        out_specs=VMEM,
        scratch_shapes=[
            pltpu.VMEM((2 * SUBS, -(-slots // LANES) * LANES), jnp.float32),
            pltpu.VMEM((6, LANES + SUBS, LANES), jnp.float32),
        ],
        name="render",
    )(meta, arrived, index, centre, basis_matrix())
    stacked = jnp.concatenate([rendered, truth])
    padded = extended(stacked, (("gs", 2), ("img", 1)), 5)
    rim_r, rim_t = (padded[0:3], padded[3:6])
    quantities = jnp.concatenate([rim_r, rim_t, rim_r * rim_r, rim_t * rim_t, rim_r * rim_t])
    band_rows = band_matrix(height, height + 10, 1)
    band_cols = band_matrix(width, width + 10, 1).T
    filtered = jnp.einsum("ij,cjw->ciw", band_rows, quantities, precision=lax.Precision.HIGHEST)
    filtered = jnp.einsum("ciw,wv->civ", filtered, band_cols, precision=lax.Precision.HIGHEST)
    return (rendered, loss_from(filtered, rendered, truth))


def solution(mesh):
    return jax.shard_map(
        on_device,
        mesh=mesh,
        in_specs=(
            P(None, ("gs", "img")),
            P(("gs", "img"), None),
            P("img", "gs", None),
            P(None, "img", "gs"),
        ),
        out_specs=(P(None, "img", "gs"), P("img", "gs")),
        check_vma=False,
    )
```

```python
import functools

import jax
import jax.numpy as jnp
import numpy as np
from jax import lax
from jax.experimental import pallas as pl
from jax.experimental.pallas import tpu as pltpu
from jax.sharding import PartitionSpec as P

TILE = 16
LANES = 128
SUBS = 8
PARAMS = 9
UNROLL = 16
LOG2E = 1.4426950408889634

coef_zero = 0.28209479177387814
coef_one = 0.4886025119029199
coef_two = [
    1.0925484305920792,
    -1.0925484305920792,
    0.31539156525252005,
    -1.0925484305920792,
    0.5462742152960396,
]
coef_three = [
    -0.5900435899266435,
    2.890611442640554,
    -0.4570457994644658,
    0.3731763325901154,
    -0.4570457994644658,
    1.445305721320277,
    -0.5900435899266435,
]
camera_z = -3000.0
ssim_share = 0.2
stable_one = 0.0001
stable_two = 0.0009


def iota(shape, dim):
    return lax.broadcasted_iota(jnp.int32, shape, dim)


def lane_take(values, index):
    return jnp.take_along_axis(values, index, axis=1, mode="promise_in_bounds")


def sublane_take(values, index):
    return jnp.take_along_axis(values, index, axis=0, mode="promise_in_bounds")


def as_bf16(value):
    return value.astype(jnp.bfloat16).astype(jnp.float32)


def three_parts(value):
    high = as_bf16(value)
    rest = value - high
    middle = as_bf16(rest)
    return high, middle, rest - middle


def project(row):
    mean_x, mean_y, mean_z = row(0), row(1), row(2)
    squared = [jnp.exp(2.0 * row(3 + k)) for k in range(3)]
    quat = [row(6 + k) for k in range(4)]
    norm = jnp.sqrt(quat[0] * quat[0] + quat[1] * quat[1] + quat[2] * quat[2] + quat[3] * quat[3])
    quat_w, quat_x, quat_y, quat_z = [part / norm for part in quat]
    first = [
        1.0 - 2.0 * (quat_y * quat_y + quat_z * quat_z),
        2.0 * (quat_x * quat_y - quat_w * quat_z),
        2.0 * (quat_x * quat_z + quat_w * quat_y),
    ]
    second = [
        2.0 * (quat_x * quat_y + quat_w * quat_z),
        1.0 - 2.0 * (quat_x * quat_x + quat_z * quat_z),
        2.0 * (quat_y * quat_z - quat_w * quat_x),
    ]

    def weighted(left, right):
        return (
            left[0] * right[0] * squared[0]
            + left[1] * right[1] * squared[1]
            + left[2] * right[2] * squared[2]
        )

    cov_xx = weighted(first, first) + 0.3
    cov_xy = weighted(first, second)
    cov_yy = weighted(second, second) + 0.3
    determinant = cov_xx * cov_yy - cov_xy * cov_xy
    log_opacity = -LOG2E * jnp.log(1.0 + jnp.exp(-row(10)))
    delta_z = mean_z - camera_z
    length = jnp.sqrt(mean_x * mean_x + mean_y * mean_y + delta_z * delta_z)
    dir_x, dir_y, dir_z = (mean_x / length, mean_y / length, delta_z / length)
    sq_x, sq_y, sq_z = (dir_x * dir_x, dir_y * dir_y, dir_z * dir_z)
    prod_xy, prod_yz, prod_xz = (dir_x * dir_y, dir_y * dir_z, dir_x * dir_z)
    basis = [
        coef_zero * jnp.ones_like(dir_x),
        -coef_one * dir_y,
        coef_one * dir_z,
        -coef_one * dir_x,
        coef_two[0] * prod_xy,
        coef_two[1] * prod_yz,
        coef_two[2] * (2.0 * sq_z - sq_x - sq_y),
        coef_two[3] * prod_xz,
        coef_two[4] * (sq_x - sq_y),
        coef_three[0] * dir_y * (3.0 * sq_x - sq_y),
        coef_three[1] * prod_xy * dir_z,
        coef_three[2] * dir_y * (4.0 * sq_z - sq_x - sq_y),
        coef_three[3] * dir_z * (2.0 * sq_z - 3.0 * sq_x - 3.0 * sq_y),
        coef_three[4] * dir_x * (4.0 * sq_z - sq_x - sq_y),
        coef_three[5] * dir_z * (sq_x - sq_y),
        coef_three[6] * dir_x * (sq_x - 3.0 * sq_y),
    ]
    colours = []
    for channel in range(3):
        total = row(11 + 16 * channel) * basis[0]
        for k in range(1, 16):
            total = total + row(11 + 16 * channel + k) * basis[k]
        colours.append(jnp.maximum(total + 0.5, 0.0))
    return [
        mean_x,
        mean_y,
        (-0.5 * LOG2E) * (cov_yy / determinant),
        LOG2E * (cov_xy / determinant),
        (-0.5 * LOG2E) * (cov_xx / determinant),
        log_opacity,
    ] + colours


def pack_kernel(cap, gauss_ref, send_ref, out_ref, table_ref, index_ref):
    targets = out_ref.shape[0]
    chunks = gauss_ref.shape[1] // LANES
    spare = LANES - cap
    rows = project(lambda k: gauss_ref[k : k + 1, :])
    for k in range(PARAMS):
        table_ref[k : k + 1, :] = rows[k]
    lane = iota((SUBS, LANES), 1)
    sub = iota((SUBS, LANES), 0)
    send_chunks = send_ref.shape[1] // LANES
    for target in range(targets):
        chunk, shift = divmod(target * cap, LANES)

        def piece(c):
            c = min(c, send_chunks - 1)
            return jnp.broadcast_to(send_ref[0:1, c * LANES : (c + 1) * LANES], (SUBS, LANES))

        index = piece(chunk)
        if shift:
            index = jnp.where(
                lane < LANES - shift,
                pltpu.roll(index, LANES - shift, axis=1),
                pltpu.roll(piece(chunk + 1), LANES - shift, axis=1),
            )
        result = index
        for r in range(-(-cap // spare)):
            moved = pltpu.roll(index, (cap - r * spare) % LANES, axis=1)
            result = jnp.where((lane >= cap) & (sub == r), moved, result)
        index_ref[target] = result

    def one(target, carry):
        index = index_ref[target]
        low, high = index & (LANES - 1), index >> 7
        left = jnp.zeros((SUBS, LANES), jnp.float32)
        right = left
        for c in range(chunks):
            hit = high == c
            part = lane_take(table_ref[0:SUBS, c * LANES : (c + 1) * LANES], low)
            left = jnp.where(hit, part, left)
            last = jnp.broadcast_to(
                table_ref[SUBS : SUBS + 1, c * LANES : (c + 1) * LANES], (SUBS, LANES)
            )
            right = jnp.where(hit, lane_take(last, low), right)
        out_ref[target] = jnp.where(lane < cap, left, right)
        return carry

    lax.fori_loop(0, targets, one, 0)


def sort_kernel(cols_here, lists_ref, index_ref, meta_ref, centre_ref):
    tiles, length = lists_ref.shape
    lists = lists_ref[...]
    live = jnp.sum((lists >= 0).astype(jnp.float32), axis=1, keepdims=True)
    live = jnp.broadcast_to(live, (tiles, tiles))
    down, across = iota((tiles, tiles), 0), iota((tiles, tiles), 1)
    live_row = jnp.sum(jnp.where(down == across, live, 0.0), axis=0, keepdims=True)
    ahead = (live > live_row) | ((live == live_row) & (down < across))
    rank_row = jnp.sum(ahead.astype(jnp.float32), axis=0, keepdims=True)
    behind = (live_row > live) | ((live_row == live) & (across < down))
    rank = jnp.sum(behind.astype(jnp.float32), axis=1, keepdims=True)
    select = (rank_row == down.astype(jnp.float32)).astype(jnp.float32)
    placed = (rank == across.astype(jnp.float32)).astype(jnp.float32)
    live_sorted = jnp.sum(placed * live, axis=0, keepdims=True)
    tile_sorted = jnp.sum(placed * down.astype(jnp.float32), axis=0, keepdims=True)
    tile_id = tile_sorted.astype(jnp.int32)
    row_of = lax.div(tile_id, cols_here)
    column = (tile_id - row_of * cols_here) * TILE
    busy = jnp.sum((live > (LANES * across).astype(jnp.float32)).astype(jnp.int32), axis=0, keepdims=True)
    meta_ref[0:1, :] = live_sorted.astype(jnp.int32)
    meta_ref[1:2, :] = row_of * (TILE // SUBS * (cols_here * TILE // LANES)) + (column >> 7)
    meta_ref[2:3, :] = column & (LANES - 1)
    meta_ref[4:5, :] = (busy + (2 * SUBS - 1)) >> 4
    tile = jnp.sum(select * across.astype(jnp.float32), axis=1, keepdims=True).astype(jnp.int32)
    tile = jnp.broadcast_to(tile, (tiles, tiles))
    tile_row = lax.div(tile, cols_here)
    tile_col = tile - tile_row * cols_here
    tile_row = tile_row + lax.axis_index("img") * (tiles // cols_here)
    tile_col = tile_col + lax.axis_index("gs") * cols_here
    centre_ref[0] = (tile_col * TILE + TILE // 2).astype(jnp.float32)
    centre_ref[1] = (tile_row * TILE + TILE // 2).astype(jnp.float32)
    high = (lists >> 7).astype(jnp.float32).astype(jnp.bfloat16)
    low = (lists & (LANES - 1)).astype(jnp.float32).astype(jnp.bfloat16)
    select = select.astype(jnp.bfloat16)
    high = jnp.dot(select, high, preferred_element_type=jnp.float32)
    low = jnp.dot(select, low, preferred_element_type=jnp.float32)
    index_ref[...] = high.astype(jnp.int32) * LANES + low.astype(jnp.int32)


def basis_matrix():
    local = np.arange(TILE) - 7.5
    kinds = [[(0, local**0), (1, local), (2, local**2)], [(3, local**0), (4, local)]]
    kinds += [[(k, local**0)] for k in range(5, 9)]
    matrix = np.zeros((2 * LANES, len(kinds) * LANES), np.float32)
    for kind, terms in enumerate(kinds):
        for coefficient, values in terms:
            for part in range(3):
                for t in range(SUBS):
                    start = kind * LANES + t * TILE
                    matrix[(coefficient * 3 + part) * SUBS + t, start : start + TILE] = values
    return jnp.asarray(matrix, jnp.bfloat16)


def render_kernel(
    cap,
    meta_ref,
    recv_ref,
    index_ref,
    centre_ref,
    basis_ref,
    truth_ref,
    out_ref,
    top_ref,
    bottom_ref,
    table_ref,
    rows_ref,
    image_ref,
):
    wide = out_ref.shape[2] // LANES
    sources = recv_ref.shape[0]
    tiles, list_len = index_ref.shape
    chunks = table_ref.shape[1] // LANES
    spare = LANES - cap
    lane = iota((SUBS, LANES), 1)
    sub = iota((SUBS, LANES), 0)
    for source in range(sources):
        value = recv_ref[source]
        last = jnp.zeros((SUBS, LANES), jnp.float32)
        for r in range(-(-cap // spare)):
            row = jnp.broadcast_to(value[r : r + 1, :], (SUBS, LANES))
            moved = pltpu.roll(row, (r * spare - cap) % LANES, axis=1)
            last = jnp.where((lane >= r * spare) & (lane < (r + 1) * spare), moved, last)
        chunk, shift = divmod(source * cap, LANES)
        here = min(cap, LANES - shift)
        if shift:
            value = pltpu.roll(value, shift, axis=1)
            last = pltpu.roll(last, shift, axis=1)
        for c, start, end, lo in ((chunk, shift, shift + here, 0), (chunk + 1, 0, cap - here, 1)):
            if end > start:
                table_ref[0:SUBS, c * LANES + start : c * LANES + end] = value[:, start:end]
                table_ref[SUBS : SUBS + 1, c * LANES + start : c * LANES + end] = last[0:1, start:end]

    zero = jnp.zeros((SUBS, LANES), jnp.float32)

    def coefficients_of(g, b):
        start = pl.multiple_of(g * SUBS, SUBS)
        index = index_ref[pl.ds(start, SUBS), pl.ds(pl.multiple_of(b * LANES, LANES), LANES)]
        live = index >= 0
        safe = jnp.maximum(index, 0)
        low, high = safe & (LANES - 1), safe >> 7
        params = [zero] * PARAMS
        for c in range(chunks):
            hit = high == c
            for p in range(PARAMS):
                row = table_ref[p : p + 1, c * LANES : (c + 1) * LANES]
                part = lane_take(jnp.broadcast_to(row, (SUBS, LANES)), low)
                params[p] = jnp.where(hit, part, params[p])
        u = params[0] - centre_ref[0, pl.ds(start, SUBS), :]
        v = params[1] - centre_ref[1, pl.ds(start, SUBS), :]
        quad_x, quad_xy, quad_y = params[2:5]
        slope_x = quad_x * u
        slope_y = quad_y * v
        constant = params[5] + slope_x * u + slope_y * v + quad_xy * u * v
        values = [
            jnp.where(live, constant, -1e5),
            jnp.where(live, -2.0 * slope_x - quad_xy * v, 0.0),
            jnp.where(live, quad_x, 0.0),
            jnp.where(live, -2.0 * slope_y - quad_xy * u, 0.0),
            jnp.where(live, quad_xy, 0.0),
            jnp.where(live, quad_y, 0.0),
        ] + params[6:9]
        parts = [part for value in values for part in three_parts(value)]
        parts += [zero] * (2 * LANES // SUBS - len(parts))
        return jnp.concatenate(parts, axis=0).T.astype(jnp.bfloat16)

    def block(b, carry):
        def pair(p, inner):
            both = [coefficients_of(2 * p + k, b) for k in range(2)]
            result = jnp.dot(
                jnp.concatenate(both, axis=0), basis_ref[...], preferred_element_type=jnp.float32
            )
            for k in range(2):
                to = pl.ds(pl.multiple_of((2 * p + k) * list_len + b * LANES, LANES), LANES)
                for kind in range(6):
                    rows_ref[kind, to, :] = result[
                        k * LANES : (k + 1) * LANES, kind * LANES : (kind + 1) * LANES
                    ]
            return inner

        return lax.fori_loop(0, meta_ref[4, b], pair, carry)

    lax.fori_loop(0, list_len // LANES, block, 0)

    up = sub.astype(jnp.float32) + 0.5
    up_squared = up * up
    flip = (SUBS - 1) - sub
    one = jnp.ones((SUBS, LANES), jnp.float32)

    def group(g, carry):
        steps = (meta_ref[0, g * SUBS] + UNROLL - 1) // UNROLL
        first = g * list_len

        def many(s, state):
            left_a, left_b, ra, ga, ba, rb, gb, bb = state
            for q in range(UNROLL):
                def row(kind):
                    return rows_ref[kind, pl.ds(first + s * UNROLL + q, SUBS, stride=0), :]

                even = row(0) + up_squared * row(2)
                odd = up * row(1)
                alpha_a = jnp.exp2(even - odd)
                alpha_b = jnp.exp2(even + odd)
                weight_a = left_a * alpha_a
                weight_b = left_b * alpha_b
                left_a = left_a - weight_a
                left_b = left_b - weight_b
                red, green, blue = row(3), row(4), row(5)
                ra, ga, ba = ra + weight_a * red, ga + weight_a * green, ba + weight_a * blue
                rb, gb, bb = rb + weight_b * red, gb + weight_b * green, bb + weight_b * blue
            return left_a, left_b, ra, ga, ba, rb, gb, bb

        state = lax.fori_loop(0, steps, many, (one, one) + (zero,) * 6)
        halves = [sublane_take(value, flip) for value in state[2:5]] + list(state[5:8])
        for t in range(SUBS):
            place, shift = meta_ref[1, g * SUBS + t], meta_ref[2, g * SUBS + t]
            mask = (lane >= shift) & (lane < shift + TILE)
            for half in range(2):
                for channel in range(3):
                    moved = pltpu.roll(
                        halves[half * 3 + channel], (shift - t * TILE) & (LANES - 1), axis=1
                    )
                    pltpu.store(image_ref.at[channel, place + half * wide], moved, mask=mask)
        return carry

    lax.fori_loop(0, tiles // SUBS, group, 0)

    height = out_ref.shape[1]
    for channel in range(3):
        for r in range(height // SUBS):
            for c in range(wide):
                value = image_ref[channel, r * wide + c]
                rows, columns = slice(r * SUBS, (r + 1) * SUBS), slice(c * LANES, (c + 1) * LANES)
                out_ref[channel, rows, columns] = value
                if r == 0:
                    top_ref[channel, :, columns] = value
                if r == height // SUBS - 1:
                    bottom_ref[channel, :, columns] = value
    top_ref[3:6] = truth_ref[:, 0:SUBS, :]
    bottom_ref[3:6] = truth_ref[:, height - SUBS : height, :]


def window():
    offsets = np.arange(11) - 5.0
    weights = np.exp(-offsets * offsets / 4.5)
    return [float(weight) for weight in weights / weights.sum()]


def filtered(load):
    weights = window()
    total = load(5) * weights[5]
    for k in range(5):
        total = total + (load(k) + load(10 - k)) * weights[k]
    return total


def products(image, truth):
    return [image, truth, image * image, truth * truth, image * truth]


def down_kernel(image_ref, truth_ref, out_ref, values_ref):
    _, height, width = image_ref.shape
    wide = width // LANES
    for channel in range(3):
        for c in range(wide):
            columns = slice(c * LANES, (c + 1) * LANES)
            parts = products(image_ref[channel, :, columns], truth_ref[channel, :, columns])
            for kind, part in enumerate(parts):
                values_ref[(kind * 3 + channel) * wide + c] = part

    def one(slot, carry):
        for r in range(1, height // SUBS - 1):
            out_ref[slot, r * SUBS : (r + 1) * SUBS, :] = filtered(
                lambda k: values_ref[slot, r * SUBS - 5 + k : r * SUBS + 3 + k, :]
            )
        return carry

    lax.fori_loop(0, out_ref.shape[0], one, 0)


def turn_kernel(
    image_ref, truth_ref, above_ref, below_ref, down_ref, out_ref, first_ref, last_ref, values_ref
):
    _, height, width = image_ref.shape
    wide = width // LANES
    for channel in range(3):
        for c in range(wide):
            columns = slice(c * LANES, (c + 1) * LANES)

            def cut(ref, which, rows):
                return ref[which, rows, columns]

            near, far = slice(0, 2 * SUBS), slice(height - 2 * SUBS, height)
            every = slice(0, SUBS)
            top = products(
                *(
                    jnp.concatenate([cut(above_ref, k, every), cut(ref, channel, near)])
                    for ref, k in ((image_ref, channel), (truth_ref, channel + 3))
                )
            )
            bottom = products(
                *(
                    jnp.concatenate([cut(ref, channel, far), cut(below_ref, k, every)])
                    for ref, k in ((image_ref, channel), (truth_ref, channel + 3))
                )
            )
            for kind in range(5):
                quantity = kind * 3 + channel
                values_ref[0] = top[kind]
                values_ref[1] = bottom[kind]
                ends = [
                    filtered(lambda k: values_ref[side, 3 + k : 3 + k + SUBS, :]) for side in range(2)
                ]
                middle = down_ref[quantity * wide + c, SUBS : height - SUBS, :]
                turned = jnp.concatenate([ends[0], middle, ends[1]], axis=0).T
                out_ref[quantity, columns, :] = turned
                if c == 0:
                    first_ref[quantity] = turned[0:SUBS]
                if c == wide - 1:
                    last_ref[quantity] = turned[LANES - SUBS : LANES]


def similarity(parts):
    mean_r, mean_t, square_r, square_t, product = parts
    both, squares = mean_r * mean_t, mean_r * mean_r + mean_t * mean_t
    return (
        (2.0 * both + stable_one)
        * (2.0 * (product - both) + stable_two)
        / ((squares + stable_one) * (square_r + square_t - squares + stable_two))
    )


def across_kernel(turned_ref, out_ref):
    tiles = turned_ref.shape[1] // SUBS
    out_ref[...] = jnp.zeros_like(out_ref)

    def one(channel, carry):
        for r in range(1, tiles - 1):
            parts = [
                filtered(
                    lambda k: turned_ref[
                        kind * 3 + channel, r * SUBS - 5 + k : r * SUBS + 3 + k, :
                    ]
                )
                for kind in range(5)
            ]
            rows = slice(r * SUBS, (r + 1) * SUBS)
            out_ref[rows, :] = out_ref[rows, :] + similarity(parts)
        return carry

    lax.fori_loop(0, 3, one, 0)


def loss_kernel(
    turned_ref, before_ref, after_ref, sum_ref, image_ref, truth_ref, out_ref, values_ref
):
    length = turned_ref.shape[1]
    ends = []
    for side in range(2):
        total = None
        for channel in range(3):
            parts = []
            for kind in range(5):
                quantity = kind * 3 + channel
                if side == 0:
                    values_ref[0:SUBS] = before_ref[quantity]
                    values_ref[SUBS : 3 * SUBS] = turned_ref[quantity, 0 : 2 * SUBS, :]
                else:
                    values_ref[0 : 2 * SUBS] = turned_ref[quantity, length - 2 * SUBS : length, :]
                    values_ref[2 * SUBS : 3 * SUBS] = after_ref[quantity]
                parts.append(filtered(lambda k: values_ref[3 + k : 3 + k + SUBS, :]))
            value = similarity(parts)
            total = value if total is None else total + value
        ends.append(total)
    sums = jnp.concatenate([ends[0], sum_ref[SUBS : length - SUBS, :], ends[1]], axis=0)
    for c in range(length // LANES):
        columns = slice(c * LANES, (c + 1) * LANES)
        mean = sums[columns].T * (1.0 / 3.0)
        apart = [jnp.abs(image_ref[k, :, columns] - truth_ref[k, :, columns]) for k in range(3)]
        distance = (apart[0] + apart[1] + apart[2]) * (1.0 / 3.0)
        out_ref[:, columns] = (1.0 - ssim_share) * distance + ssim_share * (1.0 - mean)


def exchanged(low, high, axis):
    size = lax.axis_size(axis)
    up = [(i, i + 1) for i in range(size - 1)]
    down = [(j, i) for i, j in up]
    return lax.ppermute(high, axis, up), lax.ppermute(low, axis, down)


VMEM = pl.BlockSpec(memory_space=pltpu.VMEM)
SMEM = pl.BlockSpec(memory_space=pltpu.SMEM)


def on_device(gaussians, send_slots, tile_lists, truth):
    axes = ("gs", "img")
    devices = lax.axis_size(axes)
    cap = send_slots.shape[1] // devices
    count = gaussians.shape[1]
    rows_here, cols_here, list_len = tile_lists.shape
    tiles = rows_here * cols_here
    slots = send_slots.shape[1]
    packed = pl.pallas_call(
        functools.partial(pack_kernel, cap),
        out_shape=jax.ShapeDtypeStruct((devices, SUBS, LANES), jnp.float32),
        in_specs=[VMEM, VMEM],
        out_specs=VMEM,
        scratch_shapes=[
            pltpu.VMEM((2 * SUBS, count), jnp.float32),
            pltpu.VMEM((devices, SUBS, LANES), jnp.int32),
        ],
        name="pack",
    )(gaussians, send_slots)
    arrived = lax.all_to_all(packed, axes, split_axis=0, concat_axis=0, tiled=True)
    index, meta, centre = pl.pallas_call(
        functools.partial(sort_kernel, cols_here),
        out_shape=(
            jax.ShapeDtypeStruct((tiles, list_len), jnp.int32),
            jax.ShapeDtypeStruct((SUBS, tiles), jnp.int32),
            jax.ShapeDtypeStruct((2, tiles, LANES), jnp.float32),
        ),
        in_specs=[VMEM],
        out_specs=(VMEM, VMEM, VMEM),
        name="order",
    )(tile_lists.reshape(tiles, list_len))
    height, width = rows_here * TILE, cols_here * TILE
    wide = width // LANES

    def arrays(*shapes):
        return tuple(jax.ShapeDtypeStruct(shape, jnp.float32) for shape in shapes)

    def call(kernel, name, inputs, outputs, scratch):
        return pl.pallas_call(
            kernel,
            out_shape=outputs if len(outputs) > 1 else outputs[0],
            in_specs=[VMEM] * inputs,
            out_specs=(VMEM,) * len(outputs) if len(outputs) > 1 else VMEM,
            scratch_shapes=[pltpu.VMEM(shape, jnp.float32) for shape in scratch],
            name=name,
        )

    rendered, top, bottom = pl.pallas_call(
        functools.partial(render_kernel, cap),
        out_shape=arrays((3, height, width), (6, SUBS, width), (6, SUBS, width)),
        in_specs=[SMEM] + [VMEM] * 5,
        out_specs=(VMEM,) * 3,
        scratch_shapes=[
            pltpu.VMEM((2 * SUBS, -(-slots // LANES) * LANES), jnp.float32),
            pltpu.VMEM((6, tiles // SUBS * list_len + SUBS, LANES), jnp.float32),
            pltpu.VMEM((3, height // SUBS * wide, SUBS, LANES), jnp.float32),
        ],
        name="render",
    )(meta, arrived, index, centre, basis_matrix(), truth)
    above, below = exchanged(top, bottom, "img")
    sums = call(
        down_kernel, "down", 2, arrays((15 * wide, height, LANES)), [(15 * wide, height, LANES)]
    )(rendered, truth)
    turned, first, last = call(
        turn_kernel,
        "turn",
        5,
        arrays((15, width, height), (15, SUBS, height), (15, SUBS, height)),
        [(2, 3 * SUBS, LANES)],
    )(rendered, truth, above, below, sums)
    before, after = exchanged(first, last, "gs")
    similar = call(across_kernel, "across", 1, arrays((width, height)), [])(turned)
    loss = call(loss_kernel, "loss", 6, arrays((height, width)), [(3 * SUBS, height)])(
        turned, before, after, similar, rendered, truth
    )
    return rendered, loss


def solution(mesh):
    return jax.shard_map(
        on_device,
        mesh=mesh,
        in_specs=(
            P(None, ("gs", "img")),
            P(("gs", "img"), None),
            P("img", "gs", None),
            P(None, "img", "gs"),
        ),
        out_specs=(P(None, "img", "gs"), P("img", "gs")),
        check_vma=False,
    )
```

```python
import functools

import jax
import jax.numpy as jnp
import numpy as np
from jax import lax
from jax.experimental import pallas as pl
from jax.experimental.pallas import tpu as pltpu
from jax.sharding import PartitionSpec as P

TILE = 16
LANES = 128
SUBS = 8
PARAMS = 9
UNROLL = 16
LOG2E = 1.4426950408889634

coef_zero = 0.28209479177387814
coef_one = 0.4886025119029199
coef_two = [
    1.0925484305920792,
    -1.0925484305920792,
    0.31539156525252005,
    -1.0925484305920792,
    0.5462742152960396,
]
coef_three = [
    -0.5900435899266435,
    2.890611442640554,
    -0.4570457994644658,
    0.3731763325901154,
    -0.4570457994644658,
    1.445305721320277,
    -0.5900435899266435,
]
camera_z = -3000.0
ssim_share = 0.2
stable_one = 0.0001
stable_two = 0.0009


def iota(shape, dim):
    return lax.broadcasted_iota(jnp.int32, shape, dim)


def lane_take(values, index):
    return jnp.take_along_axis(values, index, axis=1, mode="promise_in_bounds")


def sublane_take(values, index):
    return jnp.take_along_axis(values, index, axis=0, mode="promise_in_bounds")


def as_bf16(value):
    return value.astype(jnp.bfloat16).astype(jnp.float32)


def three_parts(value):
    high = as_bf16(value)
    rest = value - high
    middle = as_bf16(rest)
    return high, middle, rest - middle


def project(row):
    mean_x, mean_y, mean_z = row(0), row(1), row(2)
    squared = [jnp.exp(2.0 * row(3 + k)) for k in range(3)]
    quat = [row(6 + k) for k in range(4)]
    norm = jnp.sqrt(quat[0] * quat[0] + quat[1] * quat[1] + quat[2] * quat[2] + quat[3] * quat[3])
    quat_w, quat_x, quat_y, quat_z = [part / norm for part in quat]
    first = [
        1.0 - 2.0 * (quat_y * quat_y + quat_z * quat_z),
        2.0 * (quat_x * quat_y - quat_w * quat_z),
        2.0 * (quat_x * quat_z + quat_w * quat_y),
    ]
    second = [
        2.0 * (quat_x * quat_y + quat_w * quat_z),
        1.0 - 2.0 * (quat_x * quat_x + quat_z * quat_z),
        2.0 * (quat_y * quat_z - quat_w * quat_x),
    ]

    def weighted(left, right):
        return (
            left[0] * right[0] * squared[0]
            + left[1] * right[1] * squared[1]
            + left[2] * right[2] * squared[2]
        )

    cov_xx = weighted(first, first) + 0.3
    cov_xy = weighted(first, second)
    cov_yy = weighted(second, second) + 0.3
    determinant = cov_xx * cov_yy - cov_xy * cov_xy
    log_opacity = -LOG2E * jnp.log(1.0 + jnp.exp(-row(10)))
    delta_z = mean_z - camera_z
    length = jnp.sqrt(mean_x * mean_x + mean_y * mean_y + delta_z * delta_z)
    dir_x, dir_y, dir_z = (mean_x / length, mean_y / length, delta_z / length)
    sq_x, sq_y, sq_z = (dir_x * dir_x, dir_y * dir_y, dir_z * dir_z)
    prod_xy, prod_yz, prod_xz = (dir_x * dir_y, dir_y * dir_z, dir_x * dir_z)
    basis = [
        coef_zero * jnp.ones_like(dir_x),
        -coef_one * dir_y,
        coef_one * dir_z,
        -coef_one * dir_x,
        coef_two[0] * prod_xy,
        coef_two[1] * prod_yz,
        coef_two[2] * (2.0 * sq_z - sq_x - sq_y),
        coef_two[3] * prod_xz,
        coef_two[4] * (sq_x - sq_y),
        coef_three[0] * dir_y * (3.0 * sq_x - sq_y),
        coef_three[1] * prod_xy * dir_z,
        coef_three[2] * dir_y * (4.0 * sq_z - sq_x - sq_y),
        coef_three[3] * dir_z * (2.0 * sq_z - 3.0 * sq_x - 3.0 * sq_y),
        coef_three[4] * dir_x * (4.0 * sq_z - sq_x - sq_y),
        coef_three[5] * dir_z * (sq_x - sq_y),
        coef_three[6] * dir_x * (sq_x - 3.0 * sq_y),
    ]
    colours = []
    for channel in range(3):
        total = row(11 + 16 * channel) * basis[0]
        for k in range(1, 16):
            total = total + row(11 + 16 * channel + k) * basis[k]
        colours.append(jnp.maximum(total + 0.5, 0.0))
    return [
        mean_x,
        mean_y,
        (-0.5 * LOG2E) * (cov_yy / determinant),
        LOG2E * (cov_xy / determinant),
        (-0.5 * LOG2E) * (cov_xx / determinant),
        log_opacity,
    ] + colours


def pack_kernel(cap, gauss_ref, send_ref, out_ref, table_ref, index_ref):
    targets = out_ref.shape[0]
    chunks = gauss_ref.shape[1] // LANES
    spare = LANES - cap
    rows = project(lambda k: gauss_ref[k : k + 1, :])
    for k in range(PARAMS):
        table_ref[k : k + 1, :] = rows[k]
    lane = iota((SUBS, LANES), 1)
    sub = iota((SUBS, LANES), 0)
    send_chunks = send_ref.shape[1] // LANES
    for target in range(targets):
        chunk, shift = divmod(target * cap, LANES)

        def piece(c):
            c = min(c, send_chunks - 1)
            return jnp.broadcast_to(send_ref[0:1, c * LANES : (c + 1) * LANES], (SUBS, LANES))

        index = piece(chunk)
        if shift:
            index = jnp.where(
                lane < LANES - shift,
                pltpu.roll(index, LANES - shift, axis=1),
                pltpu.roll(piece(chunk + 1), LANES - shift, axis=1),
            )
        result = index
        for r in range(-(-cap // spare)):
            moved = pltpu.roll(index, (cap - r * spare) % LANES, axis=1)
            result = jnp.where((lane >= cap) & (sub == r), moved, result)
        index_ref[target] = result

    def one(target, carry):
        index = index_ref[target]
        low, high = index & (LANES - 1), index >> 7
        left = jnp.zeros((SUBS, LANES), jnp.float32)
        right = left
        for c in range(chunks):
            hit = high == c
            part = lane_take(table_ref[0:SUBS, c * LANES : (c + 1) * LANES], low)
            left = jnp.where(hit, part, left)
            last = jnp.broadcast_to(
                table_ref[SUBS : SUBS + 1, c * LANES : (c + 1) * LANES], (SUBS, LANES)
            )
            right = jnp.where(hit, lane_take(last, low), right)
        out_ref[target] = jnp.where(lane < cap, left, right)
        return carry

    lax.fori_loop(0, targets, one, 0)


def sort_kernel(
    cols_here,
    lists_ref,
    basis_in,
    truth_in,
    index_ref,
    meta_ref,
    centre_ref,
    basis_ref,
    truth_ref,
    sems,
):
    copies = [
        pltpu.make_async_copy(basis_in, basis_ref, sems.at[0]),
        pltpu.make_async_copy(truth_in, truth_ref, sems.at[1]),
    ]
    for copy in copies:
        copy.start()
    tiles, length = lists_ref.shape
    lists = lists_ref[...]
    live = jnp.sum((lists >= 0).astype(jnp.float32), axis=1, keepdims=True)
    live = jnp.broadcast_to(live, (tiles, tiles))
    down, across = iota((tiles, tiles), 0), iota((tiles, tiles), 1)
    live_row = jnp.sum(jnp.where(down == across, live, 0.0), axis=0, keepdims=True)
    ahead = (live > live_row) | ((live == live_row) & (down < across))
    rank_row = jnp.sum(ahead.astype(jnp.float32), axis=0, keepdims=True)
    behind = (live_row > live) | ((live_row == live) & (across < down))
    rank = jnp.sum(behind.astype(jnp.float32), axis=1, keepdims=True)
    select = (rank_row == down.astype(jnp.float32)).astype(jnp.float32)
    placed = (rank == across.astype(jnp.float32)).astype(jnp.float32)
    live_sorted = jnp.sum(placed * live, axis=0, keepdims=True)
    tile_sorted = jnp.sum(placed * down.astype(jnp.float32), axis=0, keepdims=True)
    tile_id = tile_sorted.astype(jnp.int32)
    row_of = lax.div(tile_id, cols_here)
    column = (tile_id - row_of * cols_here) * TILE
    busy = jnp.sum((live > (LANES * across).astype(jnp.float32)).astype(jnp.int32), axis=0, keepdims=True)
    meta_ref[0:1, :] = live_sorted.astype(jnp.int32)
    meta_ref[1:2, :] = row_of * (TILE // SUBS * (cols_here * TILE // LANES)) + (column >> 7)
    meta_ref[2:3, :] = column & (LANES - 1)
    meta_ref[4:5, :] = (busy + (2 * SUBS - 1)) >> 4
    tile = jnp.sum(select * across.astype(jnp.float32), axis=1, keepdims=True).astype(jnp.int32)
    tile = jnp.broadcast_to(tile, (tiles, tiles))
    tile_row = lax.div(tile, cols_here)
    tile_col = tile - tile_row * cols_here
    tile_row = tile_row + lax.axis_index("img") * (tiles // cols_here)
    tile_col = tile_col + lax.axis_index("gs") * cols_here
    centre_ref[0] = (tile_col * TILE + TILE // 2).astype(jnp.float32)
    centre_ref[1] = (tile_row * TILE + TILE // 2).astype(jnp.float32)
    high = (lists >> 7).astype(jnp.float32).astype(jnp.bfloat16)
    low = (lists & (LANES - 1)).astype(jnp.float32).astype(jnp.bfloat16)
    select = select.astype(jnp.bfloat16)
    high = jnp.dot(select, high, preferred_element_type=jnp.float32)
    low = jnp.dot(select, low, preferred_element_type=jnp.float32)
    index_ref[...] = high.astype(jnp.int32) * LANES + low.astype(jnp.int32)
    for copy in copies:
        copy.wait()


def basis_matrix():
    local = np.arange(TILE) - 7.5
    kinds = [[(0, local**0), (1, local), (2, local**2)], [(3, local**0), (4, local)]]
    kinds += [[(k, local**0)] for k in range(5, 9)]
    matrix = np.zeros((2 * LANES, len(kinds) * LANES), np.float32)
    for kind, terms in enumerate(kinds):
        for coefficient, values in terms:
            for part in range(3):
                for t in range(SUBS):
                    start = kind * LANES + t * TILE
                    matrix[(coefficient * 3 + part) * SUBS + t, start : start + TILE] = values
    return jnp.asarray(matrix, jnp.bfloat16)


def render_kernel(
    cap,
    meta_ref,
    recv_ref,
    index_ref,
    centre_ref,
    basis_ref,
    truth_ref,
    out_ref,
    near_ref,
    far_ref,
    table_ref,
    rows_ref,
    image_ref,
):
    wide = out_ref.shape[2] // LANES
    sources = recv_ref.shape[0]
    tiles, list_len = index_ref.shape
    chunks = table_ref.shape[1] // LANES
    spare = LANES - cap
    lane = iota((SUBS, LANES), 1)
    sub = iota((SUBS, LANES), 0)
    for source in range(sources):
        value = recv_ref[source]
        last = jnp.zeros((SUBS, LANES), jnp.float32)
        for r in range(-(-cap // spare)):
            row = jnp.broadcast_to(value[r : r + 1, :], (SUBS, LANES))
            moved = pltpu.roll(row, (r * spare - cap) % LANES, axis=1)
            last = jnp.where((lane >= r * spare) & (lane < (r + 1) * spare), moved, last)
        chunk, shift = divmod(source * cap, LANES)
        here = min(cap, LANES - shift)
        if shift:
            value = pltpu.roll(value, shift, axis=1)
            last = pltpu.roll(last, shift, axis=1)
        for c, start, end, lo in ((chunk, shift, shift + here, 0), (chunk + 1, 0, cap - here, 1)):
            if end > start:
                table_ref[0:SUBS, c * LANES + start : c * LANES + end] = value[:, start:end]
                table_ref[SUBS : SUBS + 1, c * LANES + start : c * LANES + end] = last[0:1, start:end]

    zero = jnp.zeros((SUBS, LANES), jnp.float32)

    def coefficients_of(g, b):
        start = pl.multiple_of(g * SUBS, SUBS)
        index = index_ref[pl.ds(start, SUBS), pl.ds(pl.multiple_of(b * LANES, LANES), LANES)]
        live = index >= 0
        safe = jnp.maximum(index, 0)
        low, high = safe & (LANES - 1), safe >> 7
        params = [zero] * PARAMS
        for c in range(chunks):
            hit = high == c
            for p in range(PARAMS):
                row = table_ref[p : p + 1, c * LANES : (c + 1) * LANES]
                part = lane_take(jnp.broadcast_to(row, (SUBS, LANES)), low)
                params[p] = jnp.where(hit, part, params[p])
        u = params[0] - centre_ref[0, pl.ds(start, SUBS), :]
        v = params[1] - centre_ref[1, pl.ds(start, SUBS), :]
        quad_x, quad_xy, quad_y = params[2:5]
        slope_x = quad_x * u
        slope_y = quad_y * v
        constant = params[5] + slope_x * u + slope_y * v + quad_xy * u * v
        values = [
            jnp.where(live, constant, -1e5),
            jnp.where(live, -2.0 * slope_x - quad_xy * v, 0.0),
            jnp.where(live, quad_x, 0.0),
            jnp.where(live, -2.0 * slope_y - quad_xy * u, 0.0),
            jnp.where(live, quad_xy, 0.0),
            jnp.where(live, quad_y, 0.0),
        ] + params[6:9]
        parts = [part for value in values for part in three_parts(value)]
        parts += [zero] * (2 * LANES // SUBS - len(parts))
        return jnp.concatenate(parts, axis=0).T.astype(jnp.bfloat16)

    def block(b, carry):
        def pair(p, inner):
            both = [coefficients_of(2 * p + k, b) for k in range(2)]
            result = jnp.dot(
                jnp.concatenate(both, axis=0), basis_ref[...], preferred_element_type=jnp.float32
            )
            for k in range(2):
                to = pl.ds(pl.multiple_of((2 * p + k) * list_len + b * LANES, LANES), LANES)
                for kind in range(6):
                    rows_ref[kind, to, :] = result[
                        k * LANES : (k + 1) * LANES, kind * LANES : (kind + 1) * LANES
                    ]
            return inner

        return lax.fori_loop(0, meta_ref[4, b], pair, carry)

    lax.fori_loop(0, list_len // LANES, block, 0)

    up = sub.astype(jnp.float32) + 0.5
    up_squared = up * up
    flip = (SUBS - 1) - sub
    one = jnp.ones((SUBS, LANES), jnp.float32)

    def group(g, carry):
        steps = (meta_ref[0, g * SUBS] + UNROLL - 1) // UNROLL
        first = g * list_len

        def many(s, state):
            left_a, left_b, ra, ga, ba, rb, gb, bb = state
            for q in range(UNROLL):
                def row(kind):
                    return rows_ref[kind, pl.ds(first + s * UNROLL + q, SUBS, stride=0), :]

                even = row(0) + up_squared * row(2)
                odd = up * row(1)
                alpha_a = jnp.exp2(even - odd)
                alpha_b = jnp.exp2(even + odd)
                weight_a = left_a * alpha_a
                weight_b = left_b * alpha_b
                left_a = left_a - weight_a
                left_b = left_b - weight_b
                red, green, blue = row(3), row(4), row(5)
                ra, ga, ba = ra + weight_a * red, ga + weight_a * green, ba + weight_a * blue
                rb, gb, bb = rb + weight_b * red, gb + weight_b * green, bb + weight_b * blue
            return left_a, left_b, ra, ga, ba, rb, gb, bb

        state = lax.fori_loop(0, steps, many, (one, one) + (zero,) * 6)
        halves = [sublane_take(value, flip) for value in state[2:5]] + list(state[5:8])
        for t in range(SUBS):
            place, shift = meta_ref[1, g * SUBS + t], meta_ref[2, g * SUBS + t]
            mask = (lane >= shift) & (lane < shift + TILE)
            for half in range(2):
                for channel in range(3):
                    moved = pltpu.roll(
                        halves[half * 3 + channel], (shift - t * TILE) & (LANES - 1), axis=1
                    )
                    pltpu.store(image_ref.at[channel, place + half * wide], moved, mask=mask)
        return carry

    lax.fori_loop(0, tiles // SUBS, group, 0)

    height = out_ref.shape[1]
    for channel in range(3):
        for r in range(height // SUBS):
            for c in range(wide):
                rows, columns = slice(r * SUBS, (r + 1) * SUBS), slice(c * LANES, (c + 1) * LANES)
                out_ref[channel, rows, columns] = image_ref[channel, r * wide + c]
    sides = [
        jnp.concatenate([out_ref[:, rows, :], truth_ref[:, rows, :]])
        for rows in (slice(0, SUBS), slice(height - SUBS, height))
    ]
    near_ref[...], far_ref[...] = by_parity("img", sides[1], sides[0])


def by_parity(axis, first, second):
    even = lax.axis_index(axis) & 1 == 0
    return jnp.where(even, first, second), jnp.where(even, second, first)


def arrived_sides(axis, near, far):
    index, size = lax.axis_index(axis), lax.axis_size(axis)
    before, after = by_parity(axis, far, near)
    return (
        jnp.where(index == 0, 0.0, before),
        jnp.where(index == size - 1, 0.0, after),
    )


def window():
    offsets = np.arange(11) - 5.0
    weights = np.exp(-offsets * offsets / 4.5)
    return [float(weight) for weight in weights / weights.sum()]


def filtered(load):
    weights = window()
    total = load(5) * weights[5]
    for k in range(5):
        total = total + (load(k) + load(10 - k)) * weights[k]
    return total


def products(image, truth):
    return [image, truth, image * image, truth * truth, image * truth]


def down_kernel(image_ref, truth_ref, out_ref, copy_ref, values_ref, sem):
    copy = pltpu.make_async_copy(image_ref, copy_ref, sem)
    copy.start()
    _, height, width = image_ref.shape
    wide = width // LANES
    for channel in range(3):
        for c in range(wide):
            columns = slice(c * LANES, (c + 1) * LANES)
            parts = products(image_ref[channel, :, columns], truth_ref[channel, :, columns])
            for kind, part in enumerate(parts):
                values_ref[(kind * 3 + channel) * wide + c] = part

    def one(slot, carry):
        for r in range(1, height // SUBS - 1):
            out_ref[slot, r * SUBS : (r + 1) * SUBS, :] = filtered(
                lambda k: values_ref[slot, r * SUBS - 5 + k : r * SUBS + 3 + k, :]
            )
        return carry

    lax.fori_loop(0, out_ref.shape[0], one, 0)
    copy.wait()


def turn_kernel(
    image_ref, truth_ref, near_in, far_in, down_ref, out_ref, near_ref, far_ref, values_ref
):
    _, height, width = image_ref.shape
    wide = width // LANES
    above, below = arrived_sides("img", near_in[...], far_in[...])
    for channel in range(3):
        for c in range(wide):
            columns = slice(c * LANES, (c + 1) * LANES)

            def cut(ref, which, rows):
                return ref[which, rows, columns]

            near, far = slice(0, 2 * SUBS), slice(height - 2 * SUBS, height)
            top = products(
                *(
                    jnp.concatenate([above[k, :, columns], cut(ref, channel, near)])
                    for ref, k in ((image_ref, channel), (truth_ref, channel + 3))
                )
            )
            bottom = products(
                *(
                    jnp.concatenate([cut(ref, channel, far), below[k, :, columns]])
                    for ref, k in ((image_ref, channel), (truth_ref, channel + 3))
                )
            )
            for kind in range(5):
                quantity = kind * 3 + channel
                values_ref[0] = top[kind]
                values_ref[1] = bottom[kind]
                ends = [
                    filtered(lambda k: values_ref[side, 3 + k : 3 + k + SUBS, :]) for side in range(2)
                ]
                middle = down_ref[quantity * wide + c, SUBS : height - SUBS, :]
                turned = jnp.concatenate([ends[0], middle, ends[1]], axis=0).T
                out_ref[quantity, columns, :] = turned


    near_ref[...], far_ref[...] = by_parity(
        "gs", out_ref[:, width - SUBS : width, :], out_ref[:, 0:SUBS, :]
    )


def similarity(parts):
    mean_r, mean_t, square_r, square_t, product = parts
    both, squares = mean_r * mean_t, mean_r * mean_r + mean_t * mean_t
    return (
        (2.0 * both + stable_one)
        * (2.0 * (product - both) + stable_two)
        / ((squares + stable_one) * (square_r + square_t - squares + stable_two))
    )


def across_kernel(turned_ref, out_ref):
    tiles = turned_ref.shape[1] // SUBS
    out_ref[...] = jnp.zeros_like(out_ref)

    def one(channel, carry):
        for r in range(1, tiles - 1):
            parts = [
                filtered(
                    lambda k: turned_ref[
                        kind * 3 + channel, r * SUBS - 5 + k : r * SUBS + 3 + k, :
                    ]
                )
                for kind in range(5)
            ]
            rows = slice(r * SUBS, (r + 1) * SUBS)
            out_ref[rows, :] = out_ref[rows, :] + similarity(parts)
        return carry

    lax.fori_loop(0, 3, one, 0)


def loss_kernel(
    turned_ref, near_in, far_in, sum_ref, image_ref, truth_ref, out_ref, values_ref
):
    length = turned_ref.shape[1]
    before, after = arrived_sides("gs", near_in[...], far_in[...])
    ends = []
    for side in range(2):
        total = None
        for channel in range(3):
            parts = []
            for kind in range(5):
                quantity = kind * 3 + channel
                if side == 0:
                    values_ref[0:SUBS] = before[quantity]
                    values_ref[SUBS : 3 * SUBS] = turned_ref[quantity, 0 : 2 * SUBS, :]
                else:
                    values_ref[0 : 2 * SUBS] = turned_ref[quantity, length - 2 * SUBS : length, :]
                    values_ref[2 * SUBS : 3 * SUBS] = after[quantity]
                parts.append(filtered(lambda k: values_ref[3 + k : 3 + k + SUBS, :]))
            value = similarity(parts)
            total = value if total is None else total + value
        ends.append(total)
    sums = jnp.concatenate([ends[0], sum_ref[SUBS : length - SUBS, :], ends[1]], axis=0)
    for c in range(length // LANES):
        columns = slice(c * LANES, (c + 1) * LANES)
        mean = sums[columns].T * (1.0 / 3.0)
        apart = [jnp.abs(image_ref[k, :, columns] - truth_ref[k, :, columns]) for k in range(3)]
        distance = (apart[0] + apart[1] + apart[2]) * (1.0 / 3.0)
        out_ref[:, columns] = (1.0 - ssim_share) * distance + ssim_share * (1.0 - mean)


def exchanged(near, far, axis, spare):
    axes = ("gs", "img")
    sizes = {name: lax.axis_size(name) for name in axes}
    size = sizes[axis]

    def flat(place):
        return place["gs"] * sizes["img"] + place["img"]

    pairs = [[], []]
    for along in range(size):
        for other in range(sizes[spare]):
            source = {axis: along, spare: other}
            pairs[0].append((flat(source), flat({axis: along ^ 1, spare: other})))
            if 0 < along < size - 1:
                target = {axis: ((along + 1) ^ 1) - 1, spare: other}
            else:
                target = {axis: along, spare: other ^ 1}
            pairs[1].append((flat(source), flat(target)))
    return lax.ppermute(near, axes, pairs[0]), lax.ppermute(far, axes, pairs[1])


def grant(mebibytes):
    return pltpu.CompilerParams(vmem_limit_bytes=mebibytes << 20)


VMEM = pl.BlockSpec(memory_space=pltpu.VMEM)
SMEM = pl.BlockSpec(memory_space=pltpu.SMEM)
ANY = pl.BlockSpec(memory_space=pl.ANY)


def on_device(gaussians, send_slots, tile_lists, truth):
    axes = ("gs", "img")
    devices = lax.axis_size(axes)
    cap = send_slots.shape[1] // devices
    count = gaussians.shape[1]
    rows_here, cols_here, list_len = tile_lists.shape
    tiles = rows_here * cols_here
    slots = send_slots.shape[1]
    packed = pl.pallas_call(
        functools.partial(pack_kernel, cap),
        out_shape=jax.ShapeDtypeStruct((devices, SUBS, LANES), jnp.float32),
        in_specs=[VMEM, VMEM],
        out_specs=VMEM,
        scratch_shapes=[
            pltpu.VMEM((2 * SUBS, count), jnp.float32),
            pltpu.VMEM((devices, SUBS, LANES), jnp.int32),
        ],
        compiler_params=grant(6),
        name="pack",
    )(gaussians, send_slots)
    arrived = lax.all_to_all(packed, axes, split_axis=0, concat_axis=0, tiled=True)
    basis = basis_matrix()
    index, meta, centre, basis, truth = pl.pallas_call(
        functools.partial(sort_kernel, cols_here),
        out_shape=(
            jax.ShapeDtypeStruct((tiles, list_len), jnp.int32),
            jax.ShapeDtypeStruct((SUBS, tiles), jnp.int32),
            jax.ShapeDtypeStruct((2, tiles, LANES), jnp.float32),
            jax.ShapeDtypeStruct(basis.shape, basis.dtype),
            jax.ShapeDtypeStruct(truth.shape, jnp.float32),
        ),
        in_specs=[VMEM, ANY, ANY],
        out_specs=(VMEM,) * 5,
        scratch_shapes=[pltpu.SemaphoreType.DMA((2,))],
        compiler_params=grant(6),
        name="order",
    )(tile_lists.reshape(tiles, list_len), basis, truth)
    height, width = rows_here * TILE, cols_here * TILE
    wide = width // LANES

    def arrays(*shapes):
        return tuple(jax.ShapeDtypeStruct(shape, jnp.float32) for shape in shapes)

    def call(kernel, name, inputs, outputs, scratch):
        return pl.pallas_call(
            kernel,
            out_shape=outputs if len(outputs) > 1 else outputs[0],
            in_specs=[VMEM] * inputs,
            out_specs=(VMEM,) * len(outputs) if len(outputs) > 1 else VMEM,
            scratch_shapes=[pltpu.VMEM(shape, jnp.float32) for shape in scratch],
            compiler_params=grant(9),
            name=name,
        )

    image, near, far = pl.pallas_call(
        functools.partial(render_kernel, cap),
        out_shape=arrays((3, height, width), (6, SUBS, width), (6, SUBS, width)),
        in_specs=[SMEM] + [VMEM] * 5,
        out_specs=(VMEM,) * 3,
        scratch_shapes=[
            pltpu.VMEM((2 * SUBS, -(-slots // LANES) * LANES), jnp.float32),
            pltpu.VMEM((6, tiles // SUBS * list_len + SUBS, LANES), jnp.float32),
            pltpu.VMEM((3, height // SUBS * wide, SUBS, LANES), jnp.float32),
        ],
        compiler_params=grant(34),
        name="render",
    )(meta, arrived, index, centre, basis, truth)
    near, far = exchanged(near, far, "img", "gs")
    sums, rendered = pl.pallas_call(
        down_kernel,
        out_shape=arrays((15 * wide, height, LANES), (3, height, width)),
        in_specs=[VMEM, VMEM],
        out_specs=(VMEM, ANY),
        scratch_shapes=[
            pltpu.VMEM((15 * wide, height, LANES), jnp.float32),
            pltpu.SemaphoreType.DMA,
        ],
        compiler_params=grant(9),
        name="down",
    )(image, truth)
    turned, near, far = call(
        turn_kernel,
        "turn",
        5,
        arrays((15, width, height), (15, SUBS, height), (15, SUBS, height)),
        [(2, 3 * SUBS, LANES)],
    )(image, truth, near, far, sums)
    near, far = exchanged(near, far, "gs", "img")
    similar = call(across_kernel, "across", 1, arrays((width, height)), [])(turned)
    loss = call(loss_kernel, "loss", 6, arrays((height, width)), [(3 * SUBS, height)])(
        turned, near, far, similar, image, truth
    )
    return rendered, loss


def solution(mesh):
    return jax.shard_map(
        on_device,
        mesh=mesh,
        in_specs=(
            P(None, ("gs", "img")),
            P(("gs", "img"), None),
            P("img", "gs", None),
            P(None, "img", "gs"),
        ),
        out_specs=(P(None, "img", "gs"), P("img", "gs")),
        check_vma=False,
    )
```

```python
import functools

import jax
import jax.numpy as jnp
import numpy as np
from jax import lax
from jax.experimental import pallas as pl
from jax.experimental.pallas import tpu as pltpu
from jax.sharding import PartitionSpec as P

TILE = 16
LANES = 128
SUBS = 8
PARAMS = 9
UNROLL = 16
FUSED = 64
LOG2E = 1.4426950408889634

coef_zero = 0.28209479177387814
coef_one = 0.4886025119029199
coef_two = [
    1.0925484305920792,
    -1.0925484305920792,
    0.31539156525252005,
    -1.0925484305920792,
    0.5462742152960396,
]
coef_three = [
    -0.5900435899266435,
    2.890611442640554,
    -0.4570457994644658,
    0.3731763325901154,
    -0.4570457994644658,
    1.445305721320277,
    -0.5900435899266435,
]
camera_z = -3000.0
ssim_share = 0.2
stable_one = 0.0001
stable_two = 0.0009


def iota(shape, dim):
    return lax.broadcasted_iota(jnp.int32, shape, dim)


def lane_take(values, index):
    return jnp.take_along_axis(values, index, axis=1, mode="promise_in_bounds")


def sublane_take(values, index):
    return jnp.take_along_axis(values, index, axis=0, mode="promise_in_bounds")


def as_bf16(value):
    return value.astype(jnp.bfloat16).astype(jnp.float32)


def three_parts(value):
    high = as_bf16(value)
    rest = value - high
    middle = as_bf16(rest)
    return high, middle, rest - middle


def project(row):
    mean_x, mean_y, mean_z = row(0), row(1), row(2)
    squared = [jnp.exp(2.0 * row(3 + k)) for k in range(3)]
    quat = [row(6 + k) for k in range(4)]
    norm = jnp.sqrt(quat[0] * quat[0] + quat[1] * quat[1] + quat[2] * quat[2] + quat[3] * quat[3])
    quat_w, quat_x, quat_y, quat_z = [part / norm for part in quat]
    first = [
        1.0 - 2.0 * (quat_y * quat_y + quat_z * quat_z),
        2.0 * (quat_x * quat_y - quat_w * quat_z),
        2.0 * (quat_x * quat_z + quat_w * quat_y),
    ]
    second = [
        2.0 * (quat_x * quat_y + quat_w * quat_z),
        1.0 - 2.0 * (quat_x * quat_x + quat_z * quat_z),
        2.0 * (quat_y * quat_z - quat_w * quat_x),
    ]

    def weighted(left, right):
        return (
            left[0] * right[0] * squared[0]
            + left[1] * right[1] * squared[1]
            + left[2] * right[2] * squared[2]
        )

    cov_xx = weighted(first, first) + 0.3
    cov_xy = weighted(first, second)
    cov_yy = weighted(second, second) + 0.3
    determinant = cov_xx * cov_yy - cov_xy * cov_xy
    log_opacity = -LOG2E * jnp.log(1.0 + jnp.exp(-row(10)))
    delta_z = mean_z - camera_z
    length = jnp.sqrt(mean_x * mean_x + mean_y * mean_y + delta_z * delta_z)
    dir_x, dir_y, dir_z = (mean_x / length, mean_y / length, delta_z / length)
    sq_x, sq_y, sq_z = (dir_x * dir_x, dir_y * dir_y, dir_z * dir_z)
    prod_xy, prod_yz, prod_xz = (dir_x * dir_y, dir_y * dir_z, dir_x * dir_z)
    basis = [
        coef_zero * jnp.ones_like(dir_x),
        -coef_one * dir_y,
        coef_one * dir_z,
        -coef_one * dir_x,
        coef_two[0] * prod_xy,
        coef_two[1] * prod_yz,
        coef_two[2] * (2.0 * sq_z - sq_x - sq_y),
        coef_two[3] * prod_xz,
        coef_two[4] * (sq_x - sq_y),
        coef_three[0] * dir_y * (3.0 * sq_x - sq_y),
        coef_three[1] * prod_xy * dir_z,
        coef_three[2] * dir_y * (4.0 * sq_z - sq_x - sq_y),
        coef_three[3] * dir_z * (2.0 * sq_z - 3.0 * sq_x - 3.0 * sq_y),
        coef_three[4] * dir_x * (4.0 * sq_z - sq_x - sq_y),
        coef_three[5] * dir_z * (sq_x - sq_y),
        coef_three[6] * dir_x * (sq_x - 3.0 * sq_y),
    ]
    colours = []
    for channel in range(3):
        total = row(11 + 16 * channel) * basis[0]
        for k in range(1, 16):
            total = total + row(11 + 16 * channel + k) * basis[k]
        colours.append(jnp.maximum(total + 0.5, 0.0))
    return [
        mean_x,
        mean_y,
        (-0.5 * LOG2E) * (cov_yy / determinant),
        LOG2E * (cov_xy / determinant),
        (-0.5 * LOG2E) * (cov_xx / determinant),
        log_opacity,
    ] + colours


def pack_kernel(
    cap, gauss_in, send_in, out_ref, gauss_ref, send_ref, table_ref, index_ref, last_ref, sems
):
    copies = [
        pltpu.make_async_copy(send_in, send_ref, sems.at[0]),
        pltpu.make_async_copy(gauss_in, gauss_ref, sems.at[1]),
    ]
    for copy in copies:
        copy.start()
    targets = out_ref.shape[0]
    chunks = gauss_ref.shape[1] // LANES
    spare = LANES - cap
    extra_rows = -(-cap // spare)
    lane = iota((SUBS, LANES), 1)
    sub = iota((SUBS, LANES), 0)
    send_chunks = send_ref.shape[1] // LANES
    copies[0].wait()
    for target in range(targets):
        chunk, shift = divmod(target * cap, LANES)

        def piece(c):
            c = min(c, send_chunks - 1)
            return jnp.broadcast_to(send_ref[0:1, c * LANES : (c + 1) * LANES], (SUBS, LANES))

        index = piece(chunk)
        if shift:
            index = jnp.where(
                lane < LANES - shift,
                pltpu.roll(index, LANES - shift, axis=1),
                pltpu.roll(piece(chunk + 1), LANES - shift, axis=1),
            )
        index_ref[target : target + 1, :] = index[0:1, :]
    copies[1].wait()
    rows = project(lambda k: gauss_ref[k : k + 1, :])
    for k in range(PARAMS):
        table_ref[k : k + 1, :] = rows[k]

    def gather(index, value_of):
        low, high = index & (LANES - 1), index >> 7
        total = jnp.zeros((SUBS, LANES), jnp.float32)
        for c in range(chunks):
            part = lane_take(value_of(slice(c * LANES, (c + 1) * LANES)), low)
            total = jnp.where(high == c, part, total)
        return total

    def octet(o, carry):
        first = pl.multiple_of(o * SUBS, SUBS)
        last = gather(
            index_ref[pl.ds(first, SUBS), :],
            lambda at: jnp.broadcast_to(table_ref[SUBS : SUBS + 1, at], (SUBS, LANES)),
        )
        for r in range(extra_rows):
            last_ref[r, 0:SUBS, :] = pltpu.roll(last, (cap - r * spare) % LANES, axis=1)
        for k in range(SUBS):
            index = index_ref[pl.ds(first + k, SUBS, stride=0), :]
            result = gather(index, lambda at: table_ref[0:SUBS, at])
            for r in range(extra_rows):
                row = last_ref[r, pl.ds(k, SUBS, stride=0), :]
                result = jnp.where((lane >= cap) & (sub == r), row, result)
            out_ref[first + k] = result
        return carry

    lax.fori_loop(0, targets // SUBS, octet, 0)


def sort_kernel(
    cols_here,
    lists_ref,
    basis_in,
    truth_in,
    index_ref,
    meta_ref,
    centre_ref,
    basis_ref,
    truth_ref,
    sems,
):
    copies = [
        pltpu.make_async_copy(basis_in, basis_ref, sems.at[0]),
        pltpu.make_async_copy(truth_in, truth_ref, sems.at[1]),
    ]
    for copy in copies:
        copy.start()
    tiles, length = lists_ref.shape
    lists = lists_ref[...]
    live = jnp.sum((lists >= 0).astype(jnp.float32), axis=1, keepdims=True)
    live = jnp.broadcast_to(live, (tiles, tiles))
    down, across = iota((tiles, tiles), 0), iota((tiles, tiles), 1)
    live_row = jnp.sum(jnp.where(down == across, live, 0.0), axis=0, keepdims=True)
    ahead = (live > live_row) | ((live == live_row) & (down < across))
    rank_row = jnp.sum(ahead.astype(jnp.float32), axis=0, keepdims=True)
    behind = (live_row > live) | ((live_row == live) & (across < down))
    rank = jnp.sum(behind.astype(jnp.float32), axis=1, keepdims=True)
    select = (rank_row == down.astype(jnp.float32)).astype(jnp.float32)
    placed = (rank == across.astype(jnp.float32)).astype(jnp.float32)
    live_sorted = jnp.sum(placed * live, axis=0, keepdims=True)
    tile_sorted = jnp.sum(placed * down.astype(jnp.float32), axis=0, keepdims=True)
    tile_id = tile_sorted.astype(jnp.int32)
    row_of = lax.div(tile_id, cols_here)
    column = (tile_id - row_of * cols_here) * TILE
    busy = jnp.sum((live > (LANES * across).astype(jnp.float32)).astype(jnp.int32), axis=0, keepdims=True)
    meta_ref[0:1, :] = live_sorted.astype(jnp.int32)
    meta_ref[1:2, :] = row_of * (TILE // SUBS * (cols_here * TILE // LANES)) + (column >> 7)
    meta_ref[2:3, :] = column & (LANES - 1)
    meta_ref[4:5, :] = (busy + (2 * SUBS - 1)) >> 4
    tile = jnp.sum(select * across.astype(jnp.float32), axis=1, keepdims=True).astype(jnp.int32)
    tile = jnp.broadcast_to(tile, (tiles, tiles))
    tile_row = lax.div(tile, cols_here)
    tile_col = tile - tile_row * cols_here
    tile_row = tile_row + lax.axis_index("img") * (tiles // cols_here)
    tile_col = tile_col + lax.axis_index("gs") * cols_here
    centre_ref[0] = (tile_col * TILE + TILE // 2).astype(jnp.float32)
    centre_ref[1] = (tile_row * TILE + TILE // 2).astype(jnp.float32)
    high = (lists >> 7).astype(jnp.float32).astype(jnp.bfloat16)
    low = (lists & (LANES - 1)).astype(jnp.float32).astype(jnp.bfloat16)
    select = select.astype(jnp.bfloat16)
    high = jnp.dot(select, high, preferred_element_type=jnp.float32)
    low = jnp.dot(select, low, preferred_element_type=jnp.float32)
    index_ref[...] = high.astype(jnp.int32) * LANES + low.astype(jnp.int32)
    for copy in copies:
        copy.wait()


def basis_matrix():
    local = np.arange(TILE) - 7.5
    kinds = [[(0, local**0), (1, local), (2, local**2)], [(3, local**0), (4, local)]]
    kinds += [[(k, local**0)] for k in range(5, 9)]
    matrix = np.zeros((2 * LANES, len(kinds) * LANES), np.float32)
    for kind, terms in enumerate(kinds):
        for coefficient, values in terms:
            for part in range(3):
                for t in range(SUBS):
                    start = kind * LANES + t * TILE
                    matrix[(coefficient * 3 + part) * SUBS + t, start : start + TILE] = values
    return jnp.asarray(matrix, jnp.bfloat16)


def render_kernel(
    cap,
    meta_ref,
    recv_ref,
    index_ref,
    centre_ref,
    basis_ref,
    truth_ref,
    out_ref,
    near_ref,
    far_ref,
    table_ref,
    rows_a,
    rows_b,
    stacked_a,
    stacked_b,
    image_ref,
):
    wide = out_ref.shape[2] // LANES
    sources = recv_ref.shape[0]
    tiles, list_len = index_ref.shape
    chunks = table_ref.shape[1] // LANES
    spare = LANES - cap
    lane = iota((SUBS, LANES), 1)
    sub = iota((SUBS, LANES), 0)
    for source in range(sources):
        value = recv_ref[source]
        last = jnp.zeros((SUBS, LANES), jnp.float32)
        for r in range(-(-cap // spare)):
            row = jnp.broadcast_to(value[r : r + 1, :], (SUBS, LANES))
            moved = pltpu.roll(row, (r * spare - cap) % LANES, axis=1)
            last = jnp.where((lane >= r * spare) & (lane < (r + 1) * spare), moved, last)
        chunk, shift = divmod(source * cap, LANES)
        here = min(cap, LANES - shift)
        if shift:
            value = pltpu.roll(value, shift, axis=1)
            last = pltpu.roll(last, shift, axis=1)
        for c, start, end, lo in ((chunk, shift, shift + here, 0), (chunk + 1, 0, cap - here, 1)):
            if end > start:
                table_ref[0:SUBS, c * LANES + start : c * LANES + end] = value[:, start:end]
                table_ref[SUBS : SUBS + 1, c * LANES + start : c * LANES + end] = last[0:1, start:end]

    zero = jnp.zeros((SUBS, LANES), jnp.float32)

    def coefficients_of(g, b):
        start = pl.multiple_of(g * SUBS, SUBS)
        index = index_ref[pl.ds(start, SUBS), pl.ds(pl.multiple_of(b * LANES, LANES), LANES)]
        live = index >= 0
        safe = jnp.maximum(index, 0)
        low, high = safe & (LANES - 1), safe >> 7
        params = [zero] * PARAMS
        for c in range(chunks):
            hit = high == c
            for p in range(PARAMS):
                row = table_ref[p : p + 1, c * LANES : (c + 1) * LANES]
                part = lane_take(jnp.broadcast_to(row, (SUBS, LANES)), low)
                params[p] = jnp.where(hit, part, params[p])
        u = params[0] - centre_ref[0, pl.ds(start, SUBS), :]
        v = params[1] - centre_ref[1, pl.ds(start, SUBS), :]
        quad_x, quad_xy, quad_y = params[2:5]
        slope_x = quad_x * u
        slope_y = quad_y * v
        constant = params[5] + slope_x * u + slope_y * v + quad_xy * u * v
        values = [
            jnp.where(live, constant, -1e5),
            jnp.where(live, -2.0 * slope_x - quad_xy * v, 0.0),
            jnp.where(live, quad_x, 0.0),
            jnp.where(live, -2.0 * slope_y - quad_xy * u, 0.0),
            jnp.where(live, quad_xy, 0.0),
            jnp.where(live, quad_y, 0.0),
        ] + params[6:9]
        parts = [part for value in values for part in three_parts(value)]
        parts += [zero] * (2 * LANES // SUBS - len(parts))
        return jnp.concatenate(parts, axis=0).T.astype(jnp.bfloat16)

    up = sub.astype(jnp.float32) + 0.5
    up_squared = up * up
    flip = (SUBS - 1) - sub
    one = jnp.ones((SUBS, LANES), jnp.float32)
    fresh = (one, one) + (zero,) * 6
    groups = tiles // SUBS

    def blend(rows_ref, first, amount, state):
        left_a, left_b, ra, ga, ba, rb, gb, bb = state
        for q in range(amount):
            def row(kind):
                return rows_ref[kind, pl.ds(first + q, SUBS, stride=0), :]

            even = row(0) + up_squared * row(2)
            odd = up * row(1)
            alpha_a = jnp.exp2(even - odd)
            alpha_b = jnp.exp2(even + odd)
            weight_a = left_a * alpha_a
            weight_b = left_b * alpha_b
            left_a = left_a - weight_a
            left_b = left_b - weight_b
            red, green, blue = row(3), row(4), row(5)
            ra, ga, ba = ra + weight_a * red, ga + weight_a * green, ba + weight_a * blue
            rb, gb, bb = rb + weight_b * red, gb + weight_b * green, bb + weight_b * blue
        return left_a, left_b, ra, ga, ba, rb, gb, bb

    def expand(stacked_ref, rows_ref):
        result = jnp.dot(stacked_ref[...], basis_ref[...], preferred_element_type=jnp.float32)
        for kind in range(6):
            rows_ref[kind, 0:LANES, :] = result[:, kind * LANES : (kind + 1) * LANES]

    def following(at):
        g, b = at
        more = (b + 1) * LANES < meta_ref[0, g * SUBS]
        return jnp.where(more, g, jnp.minimum(g + 1, groups - 1)), jnp.where(more, b + 1, 0)

    def finish(g, state):
        halves = [sublane_take(value, flip) for value in state[2:5]] + list(state[5:8])
        for t in range(SUBS):
            place, shift = meta_ref[1, g * SUBS + t], meta_ref[2, g * SUBS + t]
            mask = (lane >= shift) & (lane < shift + TILE)
            for half in range(2):
                for channel in range(3):
                    moved = pltpu.roll(
                        halves[half * 3 + channel], (shift - t * TILE) & (LANES - 1), axis=1
                    )
                    pltpu.store(image_ref.at[channel, place + half * wide], moved, mask=mask)

    def turn(now, ahead, state, rows_now, rows_next, stacked_next, stacked_free):
        g, b = now
        later = following(ahead)
        state = tuple(jnp.where(b == 0, start, value) for start, value in zip(fresh, state))
        state = blend(rows_now, 0, FUSED, state)
        expand(stacked_next, rows_next)
        stacked_free[...] = coefficients_of(*later)
        count = meta_ref[0, g * SUBS] - b * LANES
        rest = (jnp.clip(count - FUSED, 0, LANES - FUSED) + UNROLL - 1) // UNROLL

        def many(s, inner):
            return blend(rows_now, FUSED + s * UNROLL, UNROLL, inner)

        state = lax.fori_loop(0, rest, many, state)

        @pl.when(count <= LANES)
        def _():
            finish(g, state)

        return ahead, later, state

    def two(_, carry):
        now, ahead, state = carry
        now, ahead, state = turn(now, ahead, state, rows_a, rows_b, stacked_b, stacked_a)
        return turn(now, ahead, state, rows_b, rows_a, stacked_a, stacked_b)

    def add_blocks(g, total):
        return total + jnp.maximum((meta_ref[0, g * SUBS] + LANES - 1) // LANES, 1)

    blocks = lax.fori_loop(0, groups, add_blocks, 0)
    start = (jnp.int32(0), jnp.int32(0))
    second = following(start)
    stacked_a[...] = coefficients_of(*start)
    expand(stacked_a, rows_a)
    stacked_b[...] = coefficients_of(*second)
    lax.fori_loop(0, (blocks + 1) // 2, two, (start, second, fresh))

    height = out_ref.shape[1]
    for channel in range(3):
        for r in range(height // SUBS):
            for c in range(wide):
                rows, columns = slice(r * SUBS, (r + 1) * SUBS), slice(c * LANES, (c + 1) * LANES)
                out_ref[channel, rows, columns] = image_ref[channel, r * wide + c]
    sides = [
        jnp.concatenate([out_ref[:, rows, :], truth_ref[:, rows, :]])
        for rows in (slice(0, SUBS), slice(height - SUBS, height))
    ]
    near_ref[...], far_ref[...] = by_parity("img", sides[1], sides[0])


def by_parity(axis, first, second):
    even = lax.axis_index(axis) & 1 == 0
    return jnp.where(even, first, second), jnp.where(even, second, first)


def arrived_sides(axis, near, far):
    index, size = lax.axis_index(axis), lax.axis_size(axis)
    before, after = by_parity(axis, far, near)
    return (
        jnp.where(index == 0, 0.0, before),
        jnp.where(index == size - 1, 0.0, after),
    )


def window():
    offsets = np.arange(11) - 5.0
    weights = np.exp(-offsets * offsets / 4.5)
    return [float(weight) for weight in weights / weights.sum()]


def filtered(load):
    weights = window()
    total = load(5) * weights[5]
    for k in range(5):
        total = total + (load(k) + load(10 - k)) * weights[k]
    return total


def products(image, truth):
    return [image, truth, image * image, truth * truth, image * truth]


def down_kernel(image_ref, truth_ref, out_ref, copy_ref, values_ref, sem):
    copy = pltpu.make_async_copy(image_ref, copy_ref, sem)
    copy.start()
    _, height, width = image_ref.shape
    wide = width // LANES
    for channel in range(3):
        for c in range(wide):
            columns = slice(c * LANES, (c + 1) * LANES)
            parts = products(image_ref[channel, :, columns], truth_ref[channel, :, columns])
            for kind, part in enumerate(parts):
                values_ref[(kind * 3 + channel) * wide + c] = part

    def one(slot, carry):
        for r in range(1, height // SUBS - 1):
            out_ref[slot, r * SUBS : (r + 1) * SUBS, :] = filtered(
                lambda k: values_ref[slot, r * SUBS - 5 + k : r * SUBS + 3 + k, :]
            )
        return carry

    lax.fori_loop(0, out_ref.shape[0], one, 0)
    copy.wait()


def turn_kernel(
    image_ref, truth_ref, near_in, far_in, down_ref, out_ref, near_ref, far_ref, values_ref
):
    _, height, width = image_ref.shape
    wide = width // LANES
    above, below = arrived_sides("img", near_in[...], far_in[...])
    for channel in range(3):
        for c in range(wide):
            columns = slice(c * LANES, (c + 1) * LANES)

            def cut(ref, which, rows):
                return ref[which, rows, columns]

            near, far = slice(0, 2 * SUBS), slice(height - 2 * SUBS, height)
            top = products(
                *(
                    jnp.concatenate([above[k, :, columns], cut(ref, channel, near)])
                    for ref, k in ((image_ref, channel), (truth_ref, channel + 3))
                )
            )
            bottom = products(
                *(
                    jnp.concatenate([cut(ref, channel, far), below[k, :, columns]])
                    for ref, k in ((image_ref, channel), (truth_ref, channel + 3))
                )
            )
            for kind in range(5):
                quantity = kind * 3 + channel
                values_ref[0] = top[kind]
                values_ref[1] = bottom[kind]
                ends = [
                    filtered(lambda k: values_ref[side, 3 + k : 3 + k + SUBS, :]) for side in range(2)
                ]
                middle = down_ref[quantity * wide + c, SUBS : height - SUBS, :]
                turned = jnp.concatenate([ends[0], middle, ends[1]], axis=0).T
                out_ref[quantity, columns, :] = turned


    near_ref[...], far_ref[...] = by_parity(
        "gs", out_ref[:, width - SUBS : width, :], out_ref[:, 0:SUBS, :]
    )


def similarity(parts):
    mean_r, mean_t, square_r, square_t, product = parts
    both, squares = mean_r * mean_t, mean_r * mean_r + mean_t * mean_t
    return (
        (2.0 * both + stable_one)
        * (2.0 * (product - both) + stable_two)
        / ((squares + stable_one) * (square_r + square_t - squares + stable_two))
    )


def across_kernel(turned_ref, out_ref):
    tiles = turned_ref.shape[1] // SUBS
    out_ref[...] = jnp.zeros_like(out_ref)

    def one(channel, carry):
        for r in range(1, tiles - 1):
            parts = [
                filtered(
                    lambda k: turned_ref[
                        kind * 3 + channel, r * SUBS - 5 + k : r * SUBS + 3 + k, :
                    ]
                )
                for kind in range(5)
            ]
            rows = slice(r * SUBS, (r + 1) * SUBS)
            out_ref[rows, :] = out_ref[rows, :] + similarity(parts)
        return carry

    lax.fori_loop(0, 3, one, 0)


def loss_kernel(
    turned_ref, near_in, far_in, sum_ref, image_ref, truth_ref, out_ref, values_ref
):
    length = turned_ref.shape[1]
    before, after = arrived_sides("gs", near_in[...], far_in[...])
    ends = []
    for side in range(2):
        total = None
        for channel in range(3):
            parts = []
            for kind in range(5):
                quantity = kind * 3 + channel
                if side == 0:
                    values_ref[0:SUBS] = before[quantity]
                    values_ref[SUBS : 3 * SUBS] = turned_ref[quantity, 0 : 2 * SUBS, :]
                else:
                    values_ref[0 : 2 * SUBS] = turned_ref[quantity, length - 2 * SUBS : length, :]
                    values_ref[2 * SUBS : 3 * SUBS] = after[quantity]
                parts.append(filtered(lambda k: values_ref[3 + k : 3 + k + SUBS, :]))
            value = similarity(parts)
            total = value if total is None else total + value
        ends.append(total)
    sums = jnp.concatenate([ends[0], sum_ref[SUBS : length - SUBS, :], ends[1]], axis=0)
    for c in range(length // LANES):
        columns = slice(c * LANES, (c + 1) * LANES)
        mean = sums[columns].T * (1.0 / 3.0)
        apart = [jnp.abs(image_ref[k, :, columns] - truth_ref[k, :, columns]) for k in range(3)]
        distance = (apart[0] + apart[1] + apart[2]) * (1.0 / 3.0)
        out_ref[:, columns] = (1.0 - ssim_share) * distance + ssim_share * (1.0 - mean)


def exchanged(near, far, axis, spare):
    axes = ("gs", "img")
    sizes = {name: lax.axis_size(name) for name in axes}
    size = sizes[axis]

    def flat(place):
        return place["gs"] * sizes["img"] + place["img"]

    pairs = [[], []]
    for along in range(size):
        for other in range(sizes[spare]):
            source = {axis: along, spare: other}
            pairs[0].append((flat(source), flat({axis: along ^ 1, spare: other})))
            if 0 < along < size - 1:
                target = {axis: ((along + 1) ^ 1) - 1, spare: other}
            else:
                target = {axis: along, spare: other ^ 1}
            pairs[1].append((flat(source), flat(target)))
    return lax.ppermute(near, axes, pairs[0]), lax.ppermute(far, axes, pairs[1])


def grant(mebibytes):
    return pltpu.CompilerParams(vmem_limit_bytes=mebibytes << 20)


VMEM = pl.BlockSpec(memory_space=pltpu.VMEM)
SMEM = pl.BlockSpec(memory_space=pltpu.SMEM)
ANY = pl.BlockSpec(memory_space=pltpu.HBM)


def on_device(gaussians, send_slots, tile_lists, truth):
    axes = ("gs", "img")
    devices = lax.axis_size(axes)
    cap = send_slots.shape[1] // devices
    count = gaussians.shape[1]
    rows_here, cols_here, list_len = tile_lists.shape
    tiles = rows_here * cols_here
    slots = send_slots.shape[1]
    packed = pl.pallas_call(
        functools.partial(pack_kernel, cap),
        out_shape=jax.ShapeDtypeStruct((devices, SUBS, LANES), jnp.float32),
        in_specs=[ANY, ANY],
        out_specs=VMEM,
        scratch_shapes=[
            pltpu.VMEM(gaussians.shape, jnp.float32),
            pltpu.VMEM(send_slots.shape, jnp.int32),
            pltpu.VMEM((2 * SUBS, count), jnp.float32),
            pltpu.VMEM((devices + SUBS, LANES), jnp.int32),
            pltpu.VMEM((SUBS, 2 * SUBS, LANES), jnp.float32),
            pltpu.SemaphoreType.DMA((2,)),
        ],
        compiler_params=grant(60),
        name="pack",
    )(gaussians, send_slots)
    arrived = lax.all_to_all(packed, axes, split_axis=0, concat_axis=0, tiled=True)
    basis = basis_matrix()
    index, meta, centre, basis, truth = pl.pallas_call(
        functools.partial(sort_kernel, cols_here),
        out_shape=(
            jax.ShapeDtypeStruct((tiles, list_len), jnp.int32),
            jax.ShapeDtypeStruct((SUBS, tiles), jnp.int32),
            jax.ShapeDtypeStruct((2, tiles, LANES), jnp.float32),
            jax.ShapeDtypeStruct(basis.shape, basis.dtype),
            jax.ShapeDtypeStruct(truth.shape, jnp.float32),
        ),
        in_specs=[VMEM, ANY, ANY],
        out_specs=(VMEM,) * 5,
        scratch_shapes=[pltpu.SemaphoreType.DMA((2,))],
        compiler_params=grant(6),
        name="order",
    )(tile_lists.reshape(tiles, list_len), basis, truth)
    height, width = rows_here * TILE, cols_here * TILE
    wide = width // LANES

    def arrays(*shapes):
        return tuple(jax.ShapeDtypeStruct(shape, jnp.float32) for shape in shapes)

    def call(kernel, name, inputs, outputs, scratch):
        return pl.pallas_call(
            kernel,
            out_shape=outputs if len(outputs) > 1 else outputs[0],
            in_specs=[VMEM] * inputs,
            out_specs=(VMEM,) * len(outputs) if len(outputs) > 1 else VMEM,
            scratch_shapes=[pltpu.VMEM(shape, jnp.float32) for shape in scratch],
            compiler_params=grant(9),
            name=name,
        )

    image, near, far = pl.pallas_call(
        functools.partial(render_kernel, cap),
        out_shape=arrays((3, height, width), (6, SUBS, width), (6, SUBS, width)),
        in_specs=[SMEM] + [VMEM] * 5,
        out_specs=(VMEM,) * 3,
        scratch_shapes=[
            pltpu.VMEM((2 * SUBS, -(-slots // LANES) * LANES), jnp.float32),
            pltpu.VMEM((6, LANES + SUBS, LANES), jnp.float32),
            pltpu.VMEM((6, LANES + SUBS, LANES), jnp.float32),
            pltpu.VMEM((LANES, 2 * LANES), jnp.bfloat16),
            pltpu.VMEM((LANES, 2 * LANES), jnp.bfloat16),
            pltpu.VMEM((3, height // SUBS * wide, SUBS, LANES), jnp.float32),
        ],
        compiler_params=grant(12),
        name="render",
    )(meta, arrived, index, centre, basis, truth)
    near, far = exchanged(near, far, "img", "gs")
    sums, rendered = pl.pallas_call(
        down_kernel,
        out_shape=arrays((15 * wide, height, LANES), (3, height, width)),
        in_specs=[VMEM, VMEM],
        out_specs=(VMEM, ANY),
        scratch_shapes=[
            pltpu.VMEM((15 * wide, height, LANES), jnp.float32),
            pltpu.SemaphoreType.DMA,
        ],
        compiler_params=grant(9),
        name="down",
    )(image, truth)
    turned, near, far = call(
        turn_kernel,
        "turn",
        5,
        arrays((15, width, height), (15, SUBS, height), (15, SUBS, height)),
        [(2, 3 * SUBS, LANES)],
    )(image, truth, near, far, sums)
    near, far = exchanged(near, far, "gs", "img")
    similar = call(across_kernel, "across", 1, arrays((width, height)), [])(turned)
    loss = call(loss_kernel, "loss", 6, arrays((height, width)), [(3 * SUBS, height)])(
        turned, near, far, similar, image, truth
    )
    return rendered, loss


def solution(mesh):
    return jax.shard_map(
        on_device,
        mesh=mesh,
        in_specs=(
            P(None, ("gs", "img")),
            P(("gs", "img"), None),
            P("img", "gs", None),
            P(None, "img", "gs"),
        ),
        out_specs=(P(None, "img", "gs"), P("img", "gs")),
        check_vma=False,
    )
```

```python
import functools

import jax
import jax.numpy as jnp
import numpy as np
from jax import lax
from jax.experimental import pallas as pl
from jax.experimental.pallas import tpu as pltpu
from jax.sharding import PartitionSpec as P

TILE = 16
LANES = 128
SUBS = 8
PARAMS = 9
UNROLL = 16
FUSED = 96
SPAN = 256
LOG2E = 1.4426950408889634

coef_zero = 0.28209479177387814
coef_one = 0.4886025119029199
coef_two = [
    1.0925484305920792,
    -1.0925484305920792,
    0.31539156525252005,
    -1.0925484305920792,
    0.5462742152960396,
]
coef_three = [
    -0.5900435899266435,
    2.890611442640554,
    -0.4570457994644658,
    0.3731763325901154,
    -0.4570457994644658,
    1.445305721320277,
    -0.5900435899266435,
]
camera_z = -3000.0
ssim_share = 0.2
stable_one = 0.0001
stable_two = 0.0009


def iota(shape, dim):
    return lax.broadcasted_iota(jnp.int32, shape, dim)


def lane_take(values, index):
    return jnp.take_along_axis(values, index, axis=1, mode="promise_in_bounds")


def sublane_take(values, index):
    return jnp.take_along_axis(values, index, axis=0, mode="promise_in_bounds")


def as_bf16(value):
    return value.astype(jnp.bfloat16).astype(jnp.float32)


def three_parts(value):
    high = as_bf16(value)
    rest = value - high
    middle = as_bf16(rest)
    return high, middle, rest - middle


def project(row):
    mean_x, mean_y, mean_z = row(0), row(1), row(2)
    squared = [jnp.exp(2.0 * row(3 + k)) for k in range(3)]
    quat = [row(6 + k) for k in range(4)]
    norm = jnp.sqrt(quat[0] * quat[0] + quat[1] * quat[1] + quat[2] * quat[2] + quat[3] * quat[3])
    quat_w, quat_x, quat_y, quat_z = [part / norm for part in quat]
    first = [
        1.0 - 2.0 * (quat_y * quat_y + quat_z * quat_z),
        2.0 * (quat_x * quat_y - quat_w * quat_z),
        2.0 * (quat_x * quat_z + quat_w * quat_y),
    ]
    second = [
        2.0 * (quat_x * quat_y + quat_w * quat_z),
        1.0 - 2.0 * (quat_x * quat_x + quat_z * quat_z),
        2.0 * (quat_y * quat_z - quat_w * quat_x),
    ]

    def weighted(left, right):
        return (
            left[0] * right[0] * squared[0]
            + left[1] * right[1] * squared[1]
            + left[2] * right[2] * squared[2]
        )

    cov_xx = weighted(first, first) + 0.3
    cov_xy = weighted(first, second)
    cov_yy = weighted(second, second) + 0.3
    determinant = cov_xx * cov_yy - cov_xy * cov_xy
    log_opacity = -LOG2E * jnp.log(1.0 + jnp.exp(-row(10)))
    delta_z = mean_z - camera_z
    length = jnp.sqrt(mean_x * mean_x + mean_y * mean_y + delta_z * delta_z)
    dir_x, dir_y, dir_z = (mean_x / length, mean_y / length, delta_z / length)
    sq_x, sq_y, sq_z = (dir_x * dir_x, dir_y * dir_y, dir_z * dir_z)
    prod_xy, prod_yz, prod_xz = (dir_x * dir_y, dir_y * dir_z, dir_x * dir_z)
    basis = [
        coef_zero * jnp.ones_like(dir_x),
        -coef_one * dir_y,
        coef_one * dir_z,
        -coef_one * dir_x,
        coef_two[0] * prod_xy,
        coef_two[1] * prod_yz,
        coef_two[2] * (2.0 * sq_z - sq_x - sq_y),
        coef_two[3] * prod_xz,
        coef_two[4] * (sq_x - sq_y),
        coef_three[0] * dir_y * (3.0 * sq_x - sq_y),
        coef_three[1] * prod_xy * dir_z,
        coef_three[2] * dir_y * (4.0 * sq_z - sq_x - sq_y),
        coef_three[3] * dir_z * (2.0 * sq_z - 3.0 * sq_x - 3.0 * sq_y),
        coef_three[4] * dir_x * (4.0 * sq_z - sq_x - sq_y),
        coef_three[5] * dir_z * (sq_x - sq_y),
        coef_three[6] * dir_x * (sq_x - 3.0 * sq_y),
    ]
    colours = []
    for channel in range(3):
        total = row(11 + 16 * channel) * basis[0]
        for k in range(1, 16):
            total = total + row(11 + 16 * channel + k) * basis[k]
        colours.append(jnp.maximum(total + 0.5, 0.0))
    return [log_opacity] + colours + [
        mean_x,
        mean_y,
        (-0.5 * LOG2E) * (cov_yy / determinant),
        LOG2E * (cov_xy / determinant),
        (-0.5 * LOG2E) * (cov_xx / determinant),
    ]


def pack_kernel(
    cap, gauss_in, send_in, out_ref, gauss_ref, send_ref, table_ref, index_ref, last_ref, sems
):
    copies = [
        pltpu.make_async_copy(send_in, send_ref, sems.at[0]),
        pltpu.make_async_copy(gauss_in, gauss_ref, sems.at[1]),
    ]
    for copy in copies:
        copy.start()
    targets = out_ref.shape[0]
    chunks = gauss_ref.shape[1] // LANES
    spare = LANES - cap
    extra_rows = -(-cap // spare)
    lane = iota((SUBS, LANES), 1)
    sub = iota((SUBS, LANES), 0)
    send_chunks = send_ref.shape[1] // LANES
    copies[0].wait()
    for target in range(targets):
        chunk, shift = divmod(target * cap, LANES)

        def piece(c):
            c = min(c, send_chunks - 1)
            return jnp.broadcast_to(send_ref[0:1, c * LANES : (c + 1) * LANES], (SUBS, LANES))

        index = piece(chunk)
        if shift:
            index = jnp.where(
                lane < LANES - shift,
                pltpu.roll(index, LANES - shift, axis=1),
                pltpu.roll(piece(chunk + 1), LANES - shift, axis=1),
            )
        index_ref[target : target + 1, :] = index[0:1, :]
    copies[1].wait()
    rows = project(lambda k: gauss_ref[k : k + 1, :])
    for k in range(PARAMS):
        table_ref[k : k + 1, :] = jnp.where(jnp.abs(rows[k]) < 1e30, rows[k], 0.0)

    def gather(index, value_of):
        low, high = index & (LANES - 1), index >> 7
        total = jnp.zeros((SUBS, LANES), jnp.float32)
        for c in range(chunks):
            part = lane_take(value_of(slice(c * LANES, (c + 1) * LANES)), low)
            total = jnp.where(high == c, part, total)
        return total

    def octet(o, carry):
        first = pl.multiple_of(o * SUBS, SUBS)
        last = gather(
            index_ref[pl.ds(first, SUBS), :],
            lambda at: jnp.broadcast_to(table_ref[SUBS : SUBS + 1, at], (SUBS, LANES)),
        )
        for r in range(extra_rows):
            last_ref[r, 0:SUBS, :] = pltpu.roll(last, (cap - r * spare) % LANES, axis=1)
        for k in range(SUBS):
            index = index_ref[pl.ds(first + k, SUBS, stride=0), :]
            result = gather(index, lambda at: table_ref[0:SUBS, at])
            for r in range(extra_rows):
                row = last_ref[r, pl.ds(k, SUBS, stride=0), :]
                result = jnp.where((lane >= cap) & (sub == r), row, result)
            out_ref[first + k] = result
        return carry

    lax.fori_loop(0, targets // SUBS, octet, 0)


def sort_kernel(
    cols_here,
    lists_ref,
    basis_in,
    truth_in,
    index_ref,
    meta_ref,
    centre_ref,
    basis_ref,
    truth_ref,
    sems,
):
    copies = [
        pltpu.make_async_copy(basis_in, basis_ref, sems.at[0]),
        pltpu.make_async_copy(truth_in, truth_ref, sems.at[1]),
    ]
    for copy in copies:
        copy.start()
    tiles, length = lists_ref.shape
    lists = lists_ref[...]
    live = jnp.sum((lists >= 0).astype(jnp.float32), axis=1, keepdims=True)
    live = jnp.broadcast_to(live, (tiles, tiles))
    down, across = iota((tiles, tiles), 0), iota((tiles, tiles), 1)
    live_row = jnp.sum(jnp.where(down == across, live, 0.0), axis=0, keepdims=True)
    ahead = (live > live_row) | ((live == live_row) & (down < across))
    rank_row = jnp.sum(ahead.astype(jnp.float32), axis=0, keepdims=True)
    behind = (live_row > live) | ((live_row == live) & (across < down))
    rank = jnp.sum(behind.astype(jnp.float32), axis=1, keepdims=True)
    select = (rank_row == down.astype(jnp.float32)).astype(jnp.float32)
    placed = (rank == across.astype(jnp.float32)).astype(jnp.float32)
    live_sorted = jnp.sum(placed * live, axis=0, keepdims=True)
    tile_sorted = jnp.sum(placed * down.astype(jnp.float32), axis=0, keepdims=True)
    tile_id = tile_sorted.astype(jnp.int32)
    row_of = lax.div(tile_id, cols_here)
    column = (tile_id - row_of * cols_here) * TILE
    busy = jnp.sum((live > (LANES * across).astype(jnp.float32)).astype(jnp.int32), axis=0, keepdims=True)
    meta_ref[0:1, :] = live_sorted.astype(jnp.int32)
    meta_ref[1:2, :] = row_of * (TILE // SUBS * (cols_here * TILE // LANES)) + (column >> 7)
    meta_ref[2:3, :] = column & (LANES - 1)
    meta_ref[4:5, :] = (busy + (2 * SUBS - 1)) >> 4
    tile = jnp.sum(select * across.astype(jnp.float32), axis=1, keepdims=True).astype(jnp.int32)
    tile = jnp.broadcast_to(tile, (tiles, tiles))
    tile_row = lax.div(tile, cols_here)
    tile_col = tile - tile_row * cols_here
    tile_row = tile_row + lax.axis_index("img") * (tiles // cols_here)
    tile_col = tile_col + lax.axis_index("gs") * cols_here
    centre_ref[0] = (tile_col * TILE + TILE // 2).astype(jnp.float32)
    centre_ref[1] = (tile_row * TILE + TILE // 2).astype(jnp.float32)
    high = (lists >> 7).astype(jnp.float32).astype(jnp.bfloat16)
    low = (lists & (LANES - 1)).astype(jnp.float32).astype(jnp.bfloat16)
    select = select.astype(jnp.bfloat16)
    high = jnp.dot(select, high, preferred_element_type=jnp.float32)
    low = jnp.dot(select, low, preferred_element_type=jnp.float32)
    index_ref[...] = high.astype(jnp.int32) * LANES + low.astype(jnp.int32)
    for copy in copies:
        copy.wait()


def basis_matrix():
    local = np.arange(TILE) - 7.5
    kinds = [[(0, local**0), (1, local), (2, local**2)], [(3, local**0), (4, local)]]
    kinds += [[(k, local**0)] for k in range(5, 9)]
    matrix = np.zeros((2 * LANES, len(kinds) * LANES), np.float32)
    for kind, terms in enumerate(kinds):
        for coefficient, values in terms:
            for part in range(3):
                for t in range(SUBS):
                    start = kind * LANES + t * TILE
                    matrix[(coefficient * 3 + part) * SUBS + t, start : start + TILE] = values
    return jnp.asarray(matrix, jnp.bfloat16)


def render_kernel(
    cap,
    meta_ref,
    recv_ref,
    index_ref,
    centre_ref,
    basis_ref,
    truth_ref,
    out_ref,
    near_ref,
    far_ref,
    table_ref,
    spread_ref,
    count_ref,
    params_a,
    params_b,
    rows_a,
    rows_b,
    stacked_a,
    stacked_b,
    done_ref,
    image_ref,
):
    wide = out_ref.shape[2] // LANES
    sources = recv_ref.shape[0]
    tiles, list_len = index_ref.shape
    spans = table_ref.shape[1] // SPAN
    chunks = spans * (SPAN // LANES)
    spare = LANES - cap
    lane = iota((SUBS, LANES), 1)
    sub = iota((SUBS, LANES), 0)
    if sources * cap < spans * SPAN:
        last_span = slice((spans - 1) * SPAN, spans * SPAN)
        table_ref[:, last_span] = jnp.zeros((2 * SUBS, SPAN), jnp.float32)
    for source in range(sources):
        value = recv_ref[source]
        last = jnp.zeros((SUBS, LANES), jnp.float32)
        for r in range(-(-cap // spare)):
            row = jnp.broadcast_to(value[r : r + 1, :], (SUBS, LANES))
            moved = pltpu.roll(row, (r * spare - cap) % LANES, axis=1)
            last = jnp.where((lane >= r * spare) & (lane < (r + 1) * spare), moved, last)
        chunk, shift = divmod(source * cap, LANES)
        here = min(cap, LANES - shift)
        if shift:
            value = pltpu.roll(value, shift, axis=1)
            last = pltpu.roll(last, shift, axis=1)
        for c, start, end, lo in ((chunk, shift, shift + here, 0), (chunk + 1, 0, cap - here, 1)):
            if end > start:
                table_ref[0:SUBS, c * LANES + start : c * LANES + end] = value[:, start:end]
                table_ref[SUBS : SUBS + 1, c * LANES + start : c * LANES + end] = last[0:1, start:end]

    zero = jnp.zeros((SUBS, LANES), jnp.float32)

    half = SUBS // 2
    wide_sub = iota((SUBS, SPAN), 0)
    pieces = []
    for c in range(spans):
        value = table_ref[0:SUBS, c * SPAN : (c + 1) * SPAN]
        high = as_bf16(value)
        rest = pltpu.roll(as_bf16(value - high), half, axis=0)
        pieces.append(jnp.where(wide_sub < half, high, rest))
    pieces += [jnp.zeros((SUBS, SPAN), jnp.float32)] * (len(pieces) % 2)
    spread_ref[...] = jnp.concatenate(pieces, axis=0).astype(jnp.bfloat16)
    count_ref[...] = iota((SPAN, LANES), 0).astype(jnp.float32).astype(jnp.bfloat16)
    hot_one = jnp.ones((SPAN, LANES), jnp.bfloat16)
    hot_zero = jnp.zeros((SPAN, LANES), jnp.bfloat16)

    def entries(at):
        g, b = at
        start = pl.multiple_of(g * SUBS, SUBS)
        return start, index_ref[pl.ds(start, SUBS), pl.ds(pl.multiple_of(b * LANES, LANES), LANES)]

    def gather(at, params_ref):
        index = jnp.maximum(entries(at)[1], 0)
        low, high = index & (LANES - 1), index >> 7
        params = [zero] * (PARAMS - half)
        for c in range(chunks):
            hit = high == c
            for p in range(PARAMS - half):
                row = table_ref[half + p : half + p + 1, c * LANES : (c + 1) * LANES]
                part = lane_take(jnp.broadcast_to(row, (SUBS, LANES)), low)
                params[p] = jnp.where(hit, part, params[p])
        for p in range(PARAMS - half):
            params_ref[(SUBS + p) * SUBS : (SUBS + p + 1) * SUBS, :] = params[p]
        low, high = (index & (SPAN - 1)).astype(jnp.float32), index >> 8
        for t in range(0, SUBS, 2):
            hot = []
            for k in range(2):
                row = jnp.broadcast_to(low[t + k : t + k + 1, :], (SPAN, LANES))
                hot.append(jnp.where(row.astype(jnp.bfloat16) == count_ref[...], hot_one, hot_zero))
            found = jnp.dot(
                spread_ref[...], jnp.concatenate(hot, axis=1), preferred_element_type=jnp.float32
            )
            for k in range(2):
                row = jnp.broadcast_to(high[t + k : t + k + 1, :], (SUBS, LANES))
                picked = zero
                for c in range(spans):
                    part = found[c * SUBS : (c + 1) * SUBS, k * LANES : (k + 1) * LANES]
                    picked = jnp.where(row == c, part, picked)
                params_ref[(t + k) * SUBS : (t + k + 1) * SUBS, :] = picked

    def prepare(at, params_ref, stacked_ref):
        start, index = entries(at)
        live = index >= 0
        log_opacity, red, green, blue = (
            params_ref[pl.ds(p, SUBS, stride=SUBS), :]
            + params_ref[pl.ds(p + half, SUBS, stride=SUBS), :]
            for p in range(half)
        )
        mean_x, mean_y, quad_x, quad_xy, quad_y = (
            params_ref[(SUBS + p) * SUBS : (SUBS + p + 1) * SUBS, :] for p in range(PARAMS - half)
        )
        u = mean_x - centre_ref[0, pl.ds(start, SUBS), :]
        v = mean_y - centre_ref[1, pl.ds(start, SUBS), :]
        slope_x = quad_x * u
        slope_y = quad_y * v
        constant = log_opacity + slope_x * u + slope_y * v + quad_xy * u * v
        values = [
            jnp.where(live, constant, -1e5),
            jnp.where(live, -2.0 * slope_x - quad_xy * v, 0.0),
            jnp.where(live, quad_x, 0.0),
            jnp.where(live, -2.0 * slope_y - quad_xy * u, 0.0),
            jnp.where(live, quad_xy, 0.0),
            jnp.where(live, quad_y, 0.0),
            red,
            green,
            blue,
        ]
        parts = [part for value in values for part in three_parts(value)]
        parts += [zero] * (2 * LANES // SUBS - len(parts))
        stacked_ref[...] = jnp.concatenate(parts, axis=0).T.astype(jnp.bfloat16)

    up = sub.astype(jnp.float32) + 0.5
    up_squared = up * up
    flip = (SUBS - 1) - sub
    one = jnp.ones((SUBS, LANES), jnp.float32)
    fresh = (one, one) + (zero,) * 6
    groups = tiles // SUBS

    def blend(rows_ref, first, amount, state):
        left_a, left_b, ra, ga, ba, rb, gb, bb = state
        for q in range(amount):
            def row(kind):
                return rows_ref[kind, pl.ds(first + q, SUBS, stride=0), :]

            even = row(0) + up_squared * row(2)
            odd = up * row(1)
            alpha_a = jnp.exp2(even - odd)
            alpha_b = jnp.exp2(even + odd)
            weight_a = left_a * alpha_a
            weight_b = left_b * alpha_b
            left_a = left_a - weight_a
            left_b = left_b - weight_b
            red, green, blue = row(3), row(4), row(5)
            ra, ga, ba = ra + weight_a * red, ga + weight_a * green, ba + weight_a * blue
            rb, gb, bb = rb + weight_b * red, gb + weight_b * green, bb + weight_b * blue
        return left_a, left_b, ra, ga, ba, rb, gb, bb

    def expand(stacked_ref, rows_ref):
        result = jnp.dot(stacked_ref[...], basis_ref[...], preferred_element_type=jnp.float32)
        for kind in range(6):
            rows_ref[kind, 0:LANES, :] = result[:, kind * LANES : (kind + 1) * LANES]

    def following(at):
        g, b = at
        more = (b + 1) * LANES < meta_ref[0, g * SUBS]
        return jnp.where(more, g, jnp.minimum(g + 1, groups - 1)), jnp.where(more, b + 1, 0)

    def finish(g, state):
        for k in range(6):
            done_ref[g, k] = state[2 + k]

    def place(g, carry):
        halves = [done_ref[g, k] for k in range(6)]
        halves[0:3] = [sublane_take(value, flip) for value in halves[0:3]]
        for t in range(SUBS):
            where, shift = meta_ref[1, g * SUBS + t], meta_ref[2, g * SUBS + t]
            mask = (lane >= shift) & (lane < shift + TILE)
            for side in range(2):
                for channel in range(3):
                    moved = pltpu.roll(
                        halves[side * 3 + channel], (shift - t * TILE) & (LANES - 1), axis=1
                    )
                    pltpu.store(image_ref.at[channel, where + side * wide], moved, mask=mask)
        return carry

    def turn(places, state, rows_now, rows_next, stacked_next, stacked_free, params_now, params_free):
        now, first, second, third = places
        g, b = now
        state = tuple(jnp.where(b == 0, start, value) for start, value in zip(fresh, state))
        state = blend(rows_now, 0, FUSED, state)
        expand(stacked_next, rows_next)
        prepare(second, params_now, stacked_free)
        gather(third, params_free)
        count = meta_ref[0, g * SUBS] - b * LANES
        rest = (jnp.clip(count - FUSED, 0, LANES - FUSED) + UNROLL - 1) // UNROLL

        def many(s, inner):
            return blend(rows_now, FUSED + s * UNROLL, UNROLL, inner)

        state = lax.fori_loop(0, rest, many, state)

        @pl.when(count <= LANES)
        def _():
            finish(g, state)

        return (first, second, third, following(third)), state

    def two(_, carry):
        carry = turn(*carry, rows_a, rows_b, stacked_b, stacked_a, params_a, params_b)
        return turn(*carry, rows_b, rows_a, stacked_a, stacked_b, params_b, params_a)

    def add_blocks(g, total):
        return total + jnp.maximum((meta_ref[0, g * SUBS] + LANES - 1) // LANES, 1)

    blocks = lax.fori_loop(0, groups, add_blocks, 0)
    places = [(jnp.int32(0), jnp.int32(0))]
    for _ in range(3):
        places.append(following(places[-1]))
    gather(places[0], params_a)
    gather(places[1], params_b)
    prepare(places[0], params_a, stacked_a)
    expand(stacked_a, rows_a)
    prepare(places[1], params_b, stacked_b)
    gather(places[2], params_a)
    lax.fori_loop(0, (blocks + 1) // 2, two, (tuple(places), fresh))
    lax.fori_loop(0, groups, place, 0, unroll=4)

    height = out_ref.shape[1]
    for channel in range(3):
        for r in range(height // SUBS):
            for c in range(wide):
                rows, columns = slice(r * SUBS, (r + 1) * SUBS), slice(c * LANES, (c + 1) * LANES)
                out_ref[channel, rows, columns] = image_ref[channel, r * wide + c]
    sides = [
        jnp.concatenate([out_ref[:, rows, :], truth_ref[:, rows, :]])
        for rows in (slice(0, SUBS), slice(height - SUBS, height))
    ]
    near_ref[...], far_ref[...] = by_parity("img", sides[1], sides[0])


def by_parity(axis, first, second):
    even = lax.axis_index(axis) & 1 == 0
    return jnp.where(even, first, second), jnp.where(even, second, first)


def arrived_sides(axis, near, far):
    index, size = lax.axis_index(axis), lax.axis_size(axis)
    before, after = by_parity(axis, far, near)
    return (
        jnp.where(index == 0, 0.0, before),
        jnp.where(index == size - 1, 0.0, after),
    )


def window():
    offsets = np.arange(11) - 5.0
    weights = np.exp(-offsets * offsets / 4.5)
    return [float(weight) for weight in weights / weights.sum()]


def filtered(load):
    weights = window()
    total = load(5) * weights[5]
    for k in range(5):
        total = total + (load(k) + load(10 - k)) * weights[k]
    return total


def products(image, truth):
    return [image, truth, image * image, truth * truth, image * truth]


def down_kernel(image_ref, truth_ref, out_ref, copy_ref, values_ref, sem):
    copy = pltpu.make_async_copy(image_ref, copy_ref, sem)
    copy.start()
    _, height, width = image_ref.shape
    wide = width // LANES
    for channel in range(3):
        for c in range(wide):
            columns = slice(c * LANES, (c + 1) * LANES)
            parts = products(image_ref[channel, :, columns], truth_ref[channel, :, columns])
            for kind, part in enumerate(parts):
                values_ref[(kind * 3 + channel) * wide + c] = part

    def one(slot, carry):
        for r in range(1, height // SUBS - 1):
            out_ref[slot, r * SUBS : (r + 1) * SUBS, :] = filtered(
                lambda k: values_ref[slot, r * SUBS - 5 + k : r * SUBS + 3 + k, :]
            )
        return carry

    lax.fori_loop(0, out_ref.shape[0], one, 0)
    copy.wait()


def turn_kernel(
    image_ref, truth_ref, near_in, far_in, down_ref, out_ref, near_ref, far_ref, values_ref
):
    _, height, width = image_ref.shape
    wide = width // LANES
    above, below = arrived_sides("img", near_in[...], far_in[...])
    for channel in range(3):
        for c in range(wide):
            columns = slice(c * LANES, (c + 1) * LANES)

            def cut(ref, which, rows):
                return ref[which, rows, columns]

            near, far = slice(0, 2 * SUBS), slice(height - 2 * SUBS, height)
            top = products(
                *(
                    jnp.concatenate([above[k, :, columns], cut(ref, channel, near)])
                    for ref, k in ((image_ref, channel), (truth_ref, channel + 3))
                )
            )
            bottom = products(
                *(
                    jnp.concatenate([cut(ref, channel, far), below[k, :, columns]])
                    for ref, k in ((image_ref, channel), (truth_ref, channel + 3))
                )
            )
            for kind in range(5):
                quantity = kind * 3 + channel
                values_ref[0] = top[kind]
                values_ref[1] = bottom[kind]
                ends = [
                    filtered(lambda k: values_ref[side, 3 + k : 3 + k + SUBS, :]) for side in range(2)
                ]
                middle = down_ref[quantity * wide + c, SUBS : height - SUBS, :]
                turned = jnp.concatenate([ends[0], middle, ends[1]], axis=0).T
                out_ref[quantity, columns, :] = turned


    near_ref[...], far_ref[...] = by_parity(
        "gs", out_ref[:, width - SUBS : width, :], out_ref[:, 0:SUBS, :]
    )


def similarity(parts):
    mean_r, mean_t, square_r, square_t, product = parts
    both, squares = mean_r * mean_t, mean_r * mean_r + mean_t * mean_t
    return (
        (2.0 * both + stable_one)
        * (2.0 * (product - both) + stable_two)
        / ((squares + stable_one) * (square_r + square_t - squares + stable_two))
    )


def across_kernel(turned_ref, out_ref):
    tiles = turned_ref.shape[1] // SUBS
    out_ref[...] = jnp.zeros_like(out_ref)

    def one(channel, carry):
        for r in range(1, tiles - 1):
            parts = [
                filtered(
                    lambda k: turned_ref[
                        kind * 3 + channel, r * SUBS - 5 + k : r * SUBS + 3 + k, :
                    ]
                )
                for kind in range(5)
            ]
            rows = slice(r * SUBS, (r + 1) * SUBS)
            out_ref[rows, :] = out_ref[rows, :] + similarity(parts)
        return carry

    lax.fori_loop(0, 3, one, 0)


def loss_kernel(
    turned_ref, near_in, far_in, sum_ref, image_ref, truth_ref, out_ref, values_ref
):
    length = turned_ref.shape[1]
    before, after = arrived_sides("gs", near_in[...], far_in[...])
    ends = []
    for side in range(2):
        total = None
        for channel in range(3):
            parts = []
            for kind in range(5):
                quantity = kind * 3 + channel
                if side == 0:
                    values_ref[0:SUBS] = before[quantity]
                    values_ref[SUBS : 3 * SUBS] = turned_ref[quantity, 0 : 2 * SUBS, :]
                else:
                    values_ref[0 : 2 * SUBS] = turned_ref[quantity, length - 2 * SUBS : length, :]
                    values_ref[2 * SUBS : 3 * SUBS] = after[quantity]
                parts.append(filtered(lambda k: values_ref[3 + k : 3 + k + SUBS, :]))
            value = similarity(parts)
            total = value if total is None else total + value
        ends.append(total)
    sums = jnp.concatenate([ends[0], sum_ref[SUBS : length - SUBS, :], ends[1]], axis=0)
    for c in range(length // LANES):
        columns = slice(c * LANES, (c + 1) * LANES)
        mean = sums[columns].T * (1.0 / 3.0)
        apart = [jnp.abs(image_ref[k, :, columns] - truth_ref[k, :, columns]) for k in range(3)]
        distance = (apart[0] + apart[1] + apart[2]) * (1.0 / 3.0)
        out_ref[:, columns] = (1.0 - ssim_share) * distance + ssim_share * (1.0 - mean)


def exchanged(near, far, axis, spare):
    axes = ("gs", "img")
    sizes = {name: lax.axis_size(name) for name in axes}
    size = sizes[axis]

    def flat(place):
        return place["gs"] * sizes["img"] + place["img"]

    pairs = [[], []]
    for along in range(size):
        for other in range(sizes[spare]):
            source = {axis: along, spare: other}
            pairs[0].append((flat(source), flat({axis: along ^ 1, spare: other})))
            if 0 < along < size - 1:
                target = {axis: ((along + 1) ^ 1) - 1, spare: other}
            else:
                target = {axis: along, spare: other ^ 1}
            pairs[1].append((flat(source), flat(target)))
    return lax.ppermute(near, axes, pairs[0]), lax.ppermute(far, axes, pairs[1])


def grant(mebibytes):
    return pltpu.CompilerParams(vmem_limit_bytes=mebibytes << 20)


VMEM = pl.BlockSpec(memory_space=pltpu.VMEM)
SMEM = pl.BlockSpec(memory_space=pltpu.SMEM)
ANY = pl.BlockSpec(memory_space=pltpu.HBM)


def on_device(gaussians, send_slots, tile_lists, truth):
    axes = ("gs", "img")
    devices = lax.axis_size(axes)
    cap = send_slots.shape[1] // devices
    count = gaussians.shape[1]
    rows_here, cols_here, list_len = tile_lists.shape
    tiles = rows_here * cols_here
    spans = -(-send_slots.shape[1] // SPAN)
    packed = pl.pallas_call(
        functools.partial(pack_kernel, cap),
        out_shape=jax.ShapeDtypeStruct((devices, SUBS, LANES), jnp.float32),
        in_specs=[ANY, ANY],
        out_specs=VMEM,
        scratch_shapes=[
            pltpu.VMEM(gaussians.shape, jnp.float32),
            pltpu.VMEM(send_slots.shape, jnp.int32),
            pltpu.VMEM((2 * SUBS, count), jnp.float32),
            pltpu.VMEM((devices + SUBS, LANES), jnp.int32),
            pltpu.VMEM((SUBS, 2 * SUBS, LANES), jnp.float32),
            pltpu.SemaphoreType.DMA((2,)),
        ],
        compiler_params=grant(60),
        name="pack",
    )(gaussians, send_slots)
    arrived = lax.all_to_all(packed, axes, split_axis=0, concat_axis=0, tiled=True)
    basis = basis_matrix()
    index, meta, centre, basis, truth = pl.pallas_call(
        functools.partial(sort_kernel, cols_here),
        out_shape=(
            jax.ShapeDtypeStruct((tiles, list_len), jnp.int32),
            jax.ShapeDtypeStruct((SUBS, tiles), jnp.int32),
            jax.ShapeDtypeStruct((2, tiles, LANES), jnp.float32),
            jax.ShapeDtypeStruct(basis.shape, basis.dtype),
            jax.ShapeDtypeStruct(truth.shape, jnp.float32),
        ),
        in_specs=[VMEM, ANY, ANY],
        out_specs=(VMEM,) * 5,
        scratch_shapes=[pltpu.SemaphoreType.DMA((2,))],
        compiler_params=grant(6),
        name="order",
    )(tile_lists.reshape(tiles, list_len), basis, truth)
    height, width = rows_here * TILE, cols_here * TILE
    wide = width // LANES

    def arrays(*shapes):
        return tuple(jax.ShapeDtypeStruct(shape, jnp.float32) for shape in shapes)

    def call(kernel, name, inputs, outputs, scratch):
        return pl.pallas_call(
            kernel,
            out_shape=outputs if len(outputs) > 1 else outputs[0],
            in_specs=[VMEM] * inputs,
            out_specs=(VMEM,) * len(outputs) if len(outputs) > 1 else VMEM,
            scratch_shapes=[pltpu.VMEM(shape, jnp.float32) for shape in scratch],
            compiler_params=grant(9),
            name=name,
        )

    image, near, far = pl.pallas_call(
        functools.partial(render_kernel, cap),
        out_shape=arrays((3, height, width), (6, SUBS, width), (6, SUBS, width)),
        in_specs=[SMEM] + [VMEM] * 5,
        out_specs=(VMEM,) * 3,
        scratch_shapes=[
            pltpu.VMEM((2 * SUBS, spans * SPAN), jnp.float32),
            pltpu.VMEM((-(-spans // 2) * 2 * SUBS, SPAN), jnp.bfloat16),
            pltpu.VMEM((SPAN, LANES), jnp.bfloat16),
            pltpu.VMEM(((SUBS + PARAMS) * SUBS, LANES), jnp.float32),
            pltpu.VMEM(((SUBS + PARAMS) * SUBS, LANES), jnp.float32),
            pltpu.VMEM((6, LANES + SUBS, LANES), jnp.float32),
            pltpu.VMEM((6, LANES + SUBS, LANES), jnp.float32),
            pltpu.VMEM((LANES, 2 * LANES), jnp.bfloat16),
            pltpu.VMEM((LANES, 2 * LANES), jnp.bfloat16),
            pltpu.VMEM((tiles // SUBS, 6, SUBS, LANES), jnp.float32),
            pltpu.VMEM((3, height // SUBS * wide, SUBS, LANES), jnp.float32),
        ],
        compiler_params=pltpu.CompilerParams(
            vmem_limit_bytes=12 << 20
        ),
        name="render",
    )(meta, arrived, index, centre, basis, truth)
    near, far = exchanged(near, far, "img", "gs")
    sums, rendered = pl.pallas_call(
        down_kernel,
        out_shape=arrays((15 * wide, height, LANES), (3, height, width)),
        in_specs=[VMEM, VMEM],
        out_specs=(VMEM, ANY),
        scratch_shapes=[
            pltpu.VMEM((15 * wide, height, LANES), jnp.float32),
            pltpu.SemaphoreType.DMA,
        ],
        compiler_params=grant(9),
        name="down",
    )(image, truth)
    turned, near, far = call(
        turn_kernel,
        "turn",
        5,
        arrays((15, width, height), (15, SUBS, height), (15, SUBS, height)),
        [(2, 3 * SUBS, LANES)],
    )(image, truth, near, far, sums)
    near, far = exchanged(near, far, "gs", "img")
    similar = call(across_kernel, "across", 1, arrays((width, height)), [])(turned)
    loss = call(loss_kernel, "loss", 6, arrays((height, width)), [(3 * SUBS, height)])(
        turned, near, far, similar, image, truth
    )
    return rendered, loss


def solution(mesh):
    return jax.shard_map(
        on_device,
        mesh=mesh,
        in_specs=(
            P(None, ("gs", "img")),
            P(("gs", "img"), None),
            P("img", "gs", None),
            P(None, "img", "gs"),
        ),
        out_specs=(P(None, "img", "gs"), P("img", "gs")),
        check_vma=False,
    )
```

```python
import functools

import jax
import jax.numpy as jnp
import numpy as np
from jax import lax
from jax.experimental import pallas as pl
from jax.experimental.pallas import tpu as pltpu
from jax.sharding import PartitionSpec as P

TILE = 16
LANES = 128
SUBS = 8
PARAMS = 9
UNROLL = 16
FUSED = 96
SPAN = 256
LOG2E = 1.4426950408889634

coef_zero = 0.28209479177387814
coef_one = 0.4886025119029199
coef_two = [
    1.0925484305920792,
    -1.0925484305920792,
    0.31539156525252005,
    -1.0925484305920792,
    0.5462742152960396,
]
coef_three = [
    -0.5900435899266435,
    2.890611442640554,
    -0.4570457994644658,
    0.3731763325901154,
    -0.4570457994644658,
    1.445305721320277,
    -0.5900435899266435,
]
camera_z = -3000.0
ssim_share = 0.2
stable_one = 0.0001
stable_two = 0.0009


def iota(shape, dim):
    return lax.broadcasted_iota(jnp.int32, shape, dim)


def lane_take(values, index):
    return jnp.take_along_axis(values, index, axis=1, mode="promise_in_bounds")


def sublane_take(values, index):
    return jnp.take_along_axis(values, index, axis=0, mode="promise_in_bounds")


def as_bf16(value):
    return value.astype(jnp.bfloat16).astype(jnp.float32)


def three_parts(value):
    high = as_bf16(value)
    rest = value - high
    middle = as_bf16(rest)
    return high, middle, rest - middle


def project(row):
    mean_x, mean_y, mean_z = row(0), row(1), row(2)
    squared = [jnp.exp(2.0 * row(3 + k)) for k in range(3)]
    quat = [row(6 + k) for k in range(4)]
    norm = jnp.sqrt(quat[0] * quat[0] + quat[1] * quat[1] + quat[2] * quat[2] + quat[3] * quat[3])
    quat_w, quat_x, quat_y, quat_z = [part / norm for part in quat]
    first = [
        1.0 - 2.0 * (quat_y * quat_y + quat_z * quat_z),
        2.0 * (quat_x * quat_y - quat_w * quat_z),
        2.0 * (quat_x * quat_z + quat_w * quat_y),
    ]
    second = [
        2.0 * (quat_x * quat_y + quat_w * quat_z),
        1.0 - 2.0 * (quat_x * quat_x + quat_z * quat_z),
        2.0 * (quat_y * quat_z - quat_w * quat_x),
    ]

    def weighted(left, right):
        return (
            left[0] * right[0] * squared[0]
            + left[1] * right[1] * squared[1]
            + left[2] * right[2] * squared[2]
        )

    cov_xx = weighted(first, first) + 0.3
    cov_xy = weighted(first, second)
    cov_yy = weighted(second, second) + 0.3
    determinant = cov_xx * cov_yy - cov_xy * cov_xy
    log_opacity = -LOG2E * jnp.log(1.0 + jnp.exp(-row(10)))
    delta_z = mean_z - camera_z
    length = jnp.sqrt(mean_x * mean_x + mean_y * mean_y + delta_z * delta_z)
    dir_x, dir_y, dir_z = (mean_x / length, mean_y / length, delta_z / length)
    sq_x, sq_y, sq_z = (dir_x * dir_x, dir_y * dir_y, dir_z * dir_z)
    prod_xy, prod_yz, prod_xz = (dir_x * dir_y, dir_y * dir_z, dir_x * dir_z)
    basis = [
        coef_zero * jnp.ones_like(dir_x),
        -coef_one * dir_y,
        coef_one * dir_z,
        -coef_one * dir_x,
        coef_two[0] * prod_xy,
        coef_two[1] * prod_yz,
        coef_two[2] * (2.0 * sq_z - sq_x - sq_y),
        coef_two[3] * prod_xz,
        coef_two[4] * (sq_x - sq_y),
        coef_three[0] * dir_y * (3.0 * sq_x - sq_y),
        coef_three[1] * prod_xy * dir_z,
        coef_three[2] * dir_y * (4.0 * sq_z - sq_x - sq_y),
        coef_three[3] * dir_z * (2.0 * sq_z - 3.0 * sq_x - 3.0 * sq_y),
        coef_three[4] * dir_x * (4.0 * sq_z - sq_x - sq_y),
        coef_three[5] * dir_z * (sq_x - sq_y),
        coef_three[6] * dir_x * (sq_x - 3.0 * sq_y),
    ]
    colours = []
    for channel in range(3):
        total = row(11 + 16 * channel) * basis[0]
        for k in range(1, 16):
            total = total + row(11 + 16 * channel + k) * basis[k]
        colours.append(jnp.maximum(total + 0.5, 0.0))
    return [log_opacity] + colours + [
        mean_x,
        mean_y,
        (-0.5 * LOG2E) * (cov_yy / determinant),
        LOG2E * (cov_xy / determinant),
        (-0.5 * LOG2E) * (cov_xx / determinant),
    ]


def pack_kernel(
    cap, gauss_in, send_in, out_ref, gauss_ref, send_ref, table_ref, index_ref, last_ref, sems
):
    copies = [
        pltpu.make_async_copy(send_in, send_ref, sems.at[0]),
        pltpu.make_async_copy(gauss_in, gauss_ref, sems.at[1]),
    ]
    for copy in copies:
        copy.start()
    targets = out_ref.shape[0]
    chunks = gauss_ref.shape[1] // LANES
    spare = LANES - cap
    extra_rows = -(-cap // spare)
    lane = iota((SUBS, LANES), 1)
    sub = iota((SUBS, LANES), 0)
    send_chunks = send_ref.shape[1] // LANES
    copies[0].wait()
    for target in range(targets):
        chunk, shift = divmod(target * cap, LANES)

        def piece(c):
            c = min(c, send_chunks - 1)
            return jnp.broadcast_to(send_ref[0:1, c * LANES : (c + 1) * LANES], (SUBS, LANES))

        index = piece(chunk)
        if shift:
            index = jnp.where(
                lane < LANES - shift,
                pltpu.roll(index, LANES - shift, axis=1),
                pltpu.roll(piece(chunk + 1), LANES - shift, axis=1),
            )
        index_ref[target : target + 1, :] = index[0:1, :]
    copies[1].wait()
    rows = project(lambda k: gauss_ref[k : k + 1, :])
    for k in range(PARAMS):
        table_ref[k : k + 1, :] = jnp.where(jnp.abs(rows[k]) < 1e30, rows[k], 0.0)

    def gather(index, value_of):
        low, high = index & (LANES - 1), index >> 7
        total = jnp.zeros((SUBS, LANES), jnp.float32)
        for c in range(chunks):
            part = lane_take(value_of(slice(c * LANES, (c + 1) * LANES)), low)
            total = jnp.where(high == c, part, total)
        return total

    def octet(o, carry):
        first = pl.multiple_of(o * SUBS, SUBS)
        last = gather(
            index_ref[pl.ds(first, SUBS), :],
            lambda at: jnp.broadcast_to(table_ref[SUBS : SUBS + 1, at], (SUBS, LANES)),
        )
        for r in range(extra_rows):
            last_ref[r, 0:SUBS, :] = pltpu.roll(last, (cap - r * spare) % LANES, axis=1)
        for k in range(SUBS):
            index = index_ref[pl.ds(first + k, SUBS, stride=0), :]
            result = gather(index, lambda at: table_ref[0:SUBS, at])
            for r in range(extra_rows):
                row = last_ref[r, pl.ds(k, SUBS, stride=0), :]
                result = jnp.where((lane >= cap) & (sub == r), row, result)
            out_ref[first + k] = result
        return carry

    lax.fori_loop(0, targets // SUBS, octet, 0)


def sort_kernel(
    cols_here,
    lists_ref,
    basis_in,
    truth_in,
    index_ref,
    meta_ref,
    centre_ref,
    basis_ref,
    truth_ref,
    sems,
):
    copies = [
        pltpu.make_async_copy(basis_in, basis_ref, sems.at[0]),
        pltpu.make_async_copy(truth_in, truth_ref, sems.at[1]),
    ]
    for copy in copies:
        copy.start()
    tiles, length = lists_ref.shape
    lists = lists_ref[...]
    live = jnp.sum((lists >= 0).astype(jnp.float32), axis=1, keepdims=True)
    live = jnp.broadcast_to(live, (tiles, tiles))
    down, across = iota((tiles, tiles), 0), iota((tiles, tiles), 1)
    live_row = jnp.sum(jnp.where(down == across, live, 0.0), axis=0, keepdims=True)
    ahead = (live > live_row) | ((live == live_row) & (down < across))
    rank_row = jnp.sum(ahead.astype(jnp.float32), axis=0, keepdims=True)
    behind = (live_row > live) | ((live_row == live) & (across < down))
    rank = jnp.sum(behind.astype(jnp.float32), axis=1, keepdims=True)
    select = (rank_row == down.astype(jnp.float32)).astype(jnp.float32)
    placed = (rank == across.astype(jnp.float32)).astype(jnp.float32)
    live_sorted = jnp.sum(placed * live, axis=0, keepdims=True)
    tile_sorted = jnp.sum(placed * down.astype(jnp.float32), axis=0, keepdims=True)
    tile_id = tile_sorted.astype(jnp.int32)
    row_of = lax.div(tile_id, cols_here)
    column = (tile_id - row_of * cols_here) * TILE
    busy = jnp.sum((live > (LANES * across).astype(jnp.float32)).astype(jnp.int32), axis=0, keepdims=True)
    meta_ref[0:1, :] = live_sorted.astype(jnp.int32)
    meta_ref[1:2, :] = row_of * (TILE // SUBS * (cols_here * TILE // LANES)) + (column >> 7)
    meta_ref[2:3, :] = column & (LANES - 1)
    meta_ref[4:5, :] = (busy + (2 * SUBS - 1)) >> 4
    tile = jnp.sum(select * across.astype(jnp.float32), axis=1, keepdims=True).astype(jnp.int32)
    tile = jnp.broadcast_to(tile, (tiles, tiles))
    tile_row = lax.div(tile, cols_here)
    tile_col = tile - tile_row * cols_here
    tile_row = tile_row + lax.axis_index("img") * (tiles // cols_here)
    tile_col = tile_col + lax.axis_index("gs") * cols_here
    centre_ref[0] = (tile_col * TILE + TILE // 2).astype(jnp.float32)
    centre_ref[1] = (tile_row * TILE + TILE // 2).astype(jnp.float32)
    high = (lists >> 7).astype(jnp.float32).astype(jnp.bfloat16)
    low = (lists & (LANES - 1)).astype(jnp.float32).astype(jnp.bfloat16)
    select = select.astype(jnp.bfloat16)
    high = jnp.dot(select, high, preferred_element_type=jnp.float32)
    low = jnp.dot(select, low, preferred_element_type=jnp.float32)
    index_ref[...] = high.astype(jnp.int32) * LANES + low.astype(jnp.int32)
    for copy in copies:
        copy.wait()


def basis_matrix():
    local = np.arange(TILE) - 7.5
    kinds = [[(0, local**0), (1, local), (2, local**2)], [(3, local**0), (4, local)]]
    kinds += [[(k, local**0)] for k in range(5, 9)]
    matrix = np.zeros((2 * LANES, len(kinds) * LANES), np.float32)
    for kind, terms in enumerate(kinds):
        for coefficient, values in terms:
            for part in range(3):
                for t in range(SUBS):
                    start = kind * LANES + t * TILE
                    matrix[(coefficient * 3 + part) * SUBS + t, start : start + TILE] = values
    return jnp.asarray(matrix, jnp.bfloat16)


def render_kernel(
    cap,
    meta_ref,
    recv_ref,
    index_ref,
    centre_ref,
    basis_ref,
    truth_ref,
    out_ref,
    near_ref,
    far_ref,
    table_ref,
    spread_ref,
    count_ref,
    params_a,
    params_b,
    rows_a,
    rows_b,
    stacked_a,
    stacked_b,
    done_ref,
    image_ref,
):
    wide = out_ref.shape[2] // LANES
    sources = recv_ref.shape[0]
    tiles, list_len = index_ref.shape
    spans = table_ref.shape[1] // SPAN
    chunks = spans * (SPAN // LANES)
    spare = LANES - cap
    lane = iota((SUBS, LANES), 1)
    sub = iota((SUBS, LANES), 0)
    if sources * cap < spans * SPAN:
        last_span = slice((spans - 1) * SPAN, spans * SPAN)
        table_ref[:, last_span] = jnp.zeros((2 * SUBS, SPAN), jnp.float32)
    for source in range(sources):
        value = recv_ref[source]
        last = jnp.zeros((SUBS, LANES), jnp.float32)
        for r in range(-(-cap // spare)):
            row = jnp.broadcast_to(value[r : r + 1, :], (SUBS, LANES))
            moved = pltpu.roll(row, (r * spare - cap) % LANES, axis=1)
            last = jnp.where((lane >= r * spare) & (lane < (r + 1) * spare), moved, last)
        chunk, shift = divmod(source * cap, LANES)
        here = min(cap, LANES - shift)
        if shift:
            value = pltpu.roll(value, shift, axis=1)
            last = pltpu.roll(last, shift, axis=1)
        for c, start, end, lo in ((chunk, shift, shift + here, 0), (chunk + 1, 0, cap - here, 1)):
            if end > start:
                table_ref[0:SUBS, c * LANES + start : c * LANES + end] = value[:, start:end]
                table_ref[SUBS : SUBS + 1, c * LANES + start : c * LANES + end] = last[0:1, start:end]

    zero = jnp.zeros((SUBS, LANES), jnp.float32)

    half = SUBS // 2
    wide_sub = iota((SUBS, SPAN), 0)
    pieces = []
    for c in range(spans):
        value = table_ref[0:SUBS, c * SPAN : (c + 1) * SPAN]
        high = as_bf16(value)
        rest = pltpu.roll(as_bf16(value - high), half, axis=0)
        pieces.append(jnp.where(wide_sub < half, high, rest))
    pieces += [jnp.zeros((SUBS, SPAN), jnp.float32)] * (len(pieces) % 2)
    spread_ref[...] = jnp.concatenate(pieces, axis=0).astype(jnp.bfloat16)
    count_ref[...] = iota((SPAN, LANES), 0).astype(jnp.float32).astype(jnp.bfloat16)
    hot_one = jnp.ones((SPAN, LANES), jnp.bfloat16)
    hot_zero = jnp.zeros((SPAN, LANES), jnp.bfloat16)

    def entries(at):
        g, b = at
        start = pl.multiple_of(g * SUBS, SUBS)
        return start, index_ref[pl.ds(start, SUBS), pl.ds(pl.multiple_of(b * LANES, LANES), LANES)]

    def gather(at, params_ref):
        index = jnp.maximum(entries(at)[1], 0)
        low, high = index & (LANES - 1), index >> 7
        params = [zero] * (PARAMS - half)
        for c in range(chunks):
            hit = high == c
            for p in range(PARAMS - half):
                row = table_ref[half + p : half + p + 1, c * LANES : (c + 1) * LANES]
                part = lane_take(jnp.broadcast_to(row, (SUBS, LANES)), low)
                params[p] = jnp.where(hit, part, params[p])
        for p in range(PARAMS - half):
            params_ref[(SUBS + p) * SUBS : (SUBS + p + 1) * SUBS, :] = params[p]
        low, high = (index & (SPAN - 1)).astype(jnp.float32), index >> 8
        for t in range(0, SUBS, 2):
            hot = []
            for k in range(2):
                row = jnp.broadcast_to(low[t + k : t + k + 1, :], (SPAN, LANES))
                hot.append(jnp.where(row.astype(jnp.bfloat16) == count_ref[...], hot_one, hot_zero))
            found = jnp.dot(
                spread_ref[...], jnp.concatenate(hot, axis=1), preferred_element_type=jnp.float32
            )
            for k in range(2):
                row = jnp.broadcast_to(high[t + k : t + k + 1, :], (SUBS, LANES))
                picked = zero
                for c in range(spans):
                    part = found[c * SUBS : (c + 1) * SUBS, k * LANES : (k + 1) * LANES]
                    picked = jnp.where(row == c, part, picked)
                params_ref[(t + k) * SUBS : (t + k + 1) * SUBS, :] = picked

    def prepare(at, params_ref, stacked_ref):
        start, index = entries(at)
        live = index >= 0
        log_opacity, red, green, blue = (
            params_ref[pl.ds(p, SUBS, stride=SUBS), :]
            + params_ref[pl.ds(p + half, SUBS, stride=SUBS), :]
            for p in range(half)
        )
        mean_x, mean_y, quad_x, quad_xy, quad_y = (
            params_ref[(SUBS + p) * SUBS : (SUBS + p + 1) * SUBS, :] for p in range(PARAMS - half)
        )
        u = mean_x - centre_ref[0, pl.ds(start, SUBS), :]
        v = mean_y - centre_ref[1, pl.ds(start, SUBS), :]
        slope_x = quad_x * u
        slope_y = quad_y * v
        constant = log_opacity + slope_x * u + slope_y * v + quad_xy * u * v
        values = [
            jnp.where(live, constant, -1e5),
            jnp.where(live, -2.0 * slope_x - quad_xy * v, 0.0),
            jnp.where(live, quad_x, 0.0),
            jnp.where(live, -2.0 * slope_y - quad_xy * u, 0.0),
            jnp.where(live, quad_xy, 0.0),
            jnp.where(live, quad_y, 0.0),
            red,
            green,
            blue,
        ]
        parts = [part for value in values for part in three_parts(value)]
        parts += [zero] * (2 * LANES // SUBS - len(parts))
        stacked_ref[...] = jnp.concatenate(parts, axis=0).T.astype(jnp.bfloat16)

    up = sub.astype(jnp.float32) + 0.5
    up_squared = up * up
    flip = (SUBS - 1) - sub
    one = jnp.ones((SUBS, LANES), jnp.float32)
    fresh = (one, one) + (zero,) * 6
    groups = tiles // SUBS

    def blend(rows_ref, first, amount, state):
        left_a, left_b, ra, ga, ba, rb, gb, bb = state
        for q in range(amount):
            def row(kind):
                return rows_ref[kind, pl.ds(first + q, SUBS, stride=0), :]

            even = row(0) + up_squared * row(2)
            odd = up * row(1)
            alpha_a = jnp.exp2(even - odd)
            alpha_b = jnp.exp2(even + odd)
            weight_a = left_a * alpha_a
            weight_b = left_b * alpha_b
            left_a = left_a - weight_a
            left_b = left_b - weight_b
            red, green, blue = row(3), row(4), row(5)
            ra, ga, ba = ra + weight_a * red, ga + weight_a * green, ba + weight_a * blue
            rb, gb, bb = rb + weight_b * red, gb + weight_b * green, bb + weight_b * blue
        return left_a, left_b, ra, ga, ba, rb, gb, bb

    def expand(stacked_ref, rows_ref):
        result = jnp.dot(stacked_ref[...], basis_ref[...], preferred_element_type=jnp.float32)
        for kind in range(6):
            rows_ref[kind, 0:LANES, :] = result[:, kind * LANES : (kind + 1) * LANES]

    def following(at):
        g, b = at
        more = (b + 1) * LANES < meta_ref[0, g * SUBS]
        return jnp.where(more, g, jnp.minimum(g + 1, groups - 1)), jnp.where(more, b + 1, 0)

    def finish(g, state):
        for k in range(6):
            done_ref[g, k] = state[2 + k]

    def place(g):
        halves = [done_ref[g, k] for k in range(6)]
        halves[0:3] = [sublane_take(value, flip) for value in halves[0:3]]
        for t in range(SUBS):
            where, shift = meta_ref[1, g * SUBS + t], meta_ref[2, g * SUBS + t]
            mask = (lane >= shift) & (lane < shift + TILE)
            for side in range(2):
                for channel in range(3):
                    moved = pltpu.roll(
                        halves[side * 3 + channel], (shift - t * TILE) & (LANES - 1), axis=1
                    )
                    pltpu.store(image_ref.at[channel, where + side * wide], moved, mask=mask)

    def turn(places, ready, state, rows_now, rows_next, stacked_next, stacked_free, params_now, params_free):
        now, first, second, third = places
        g, b = now
        state = tuple(jnp.where(b == 0, start, value) for start, value in zip(fresh, state))
        state = blend(rows_now, 0, FUSED, state)
        expand(stacked_next, rows_next)
        prepare(second, params_now, stacked_free)
        gather(third, params_free)
        place(ready)
        count = meta_ref[0, g * SUBS] - b * LANES
        rest = (jnp.clip(count - FUSED, 0, LANES - FUSED) + UNROLL - 1) // UNROLL

        def many(s, inner):
            return blend(rows_now, FUSED + s * UNROLL, UNROLL, inner)

        state = lax.fori_loop(0, rest, many, state)

        @pl.when(count <= LANES)
        def _():
            finish(g, state)

        ready = jnp.where(count <= LANES, g, ready)
        return (first, second, third, following(third)), ready, state

    def two(_, carry):
        carry = turn(*carry, rows_a, rows_b, stacked_b, stacked_a, params_a, params_b)
        return turn(*carry, rows_b, rows_a, stacked_a, stacked_b, params_b, params_a)

    def add_blocks(g, total):
        return total + jnp.maximum((meta_ref[0, g * SUBS] + LANES - 1) // LANES, 1)

    blocks = lax.fori_loop(0, groups, add_blocks, 0)
    places = [(jnp.int32(0), jnp.int32(0))]
    for _ in range(3):
        places.append(following(places[-1]))
    gather(places[0], params_a)
    gather(places[1], params_b)
    prepare(places[0], params_a, stacked_a)
    expand(stacked_a, rows_a)
    prepare(places[1], params_b, stacked_b)
    gather(places[2], params_a)
    lax.fori_loop(0, (blocks + 1) // 2, two, (tuple(places), jnp.int32(0), fresh))
    place(groups - 1)

    height = out_ref.shape[1]
    for channel in range(3):
        for r in range(height // SUBS):
            for c in range(wide):
                rows, columns = slice(r * SUBS, (r + 1) * SUBS), slice(c * LANES, (c + 1) * LANES)
                out_ref[channel, rows, columns] = image_ref[channel, r * wide + c]
    sides = [
        jnp.concatenate([out_ref[:, rows, :], truth_ref[:, rows, :]])
        for rows in (slice(0, SUBS), slice(height - SUBS, height))
    ]
    near_ref[...], far_ref[...] = by_parity("img", sides[1], sides[0])


def by_parity(axis, first, second):
    even = lax.axis_index(axis) & 1 == 0
    return jnp.where(even, first, second), jnp.where(even, second, first)


def arrived_sides(axis, near, far):
    index, size = lax.axis_index(axis), lax.axis_size(axis)
    before, after = by_parity(axis, far, near)
    return (
        jnp.where(index == 0, 0.0, before),
        jnp.where(index == size - 1, 0.0, after),
    )


def window():
    offsets = np.arange(11) - 5.0
    weights = np.exp(-offsets * offsets / 4.5)
    return [float(weight) for weight in weights / weights.sum()]


def filtered(load):
    weights = window()
    total = load(5) * weights[5]
    for k in range(5):
        total = total + (load(k) + load(10 - k)) * weights[k]
    return total


def products(image, truth):
    return [image, truth, image * image, truth * truth, image * truth]


def down_kernel(image_ref, truth_ref, out_ref, copy_ref, values_ref, sem):
    copy = pltpu.make_async_copy(image_ref, copy_ref, sem)
    copy.start()
    _, height, width = image_ref.shape
    wide = width // LANES
    for channel in range(3):
        for c in range(wide):
            columns = slice(c * LANES, (c + 1) * LANES)
            parts = products(image_ref[channel, :, columns], truth_ref[channel, :, columns])
            for kind, part in enumerate(parts):
                values_ref[(kind * 3 + channel) * wide + c] = part

    def one(slot, carry):
        for r in range(1, height // SUBS - 1):
            out_ref[slot, r * SUBS : (r + 1) * SUBS, :] = filtered(
                lambda k: values_ref[slot, r * SUBS - 5 + k : r * SUBS + 3 + k, :]
            )
        return carry

    lax.fori_loop(0, out_ref.shape[0], one, 0)
    copy.wait()


def turn_kernel(
    image_ref, truth_ref, near_in, far_in, down_ref, out_ref, near_ref, far_ref, values_ref
):
    _, height, width = image_ref.shape
    wide = width // LANES
    above, below = arrived_sides("img", near_in[...], far_in[...])
    for channel in range(3):
        for c in range(wide):
            columns = slice(c * LANES, (c + 1) * LANES)

            def cut(ref, which, rows):
                return ref[which, rows, columns]

            near, far = slice(0, 2 * SUBS), slice(height - 2 * SUBS, height)
            top = products(
                *(
                    jnp.concatenate([above[k, :, columns], cut(ref, channel, near)])
                    for ref, k in ((image_ref, channel), (truth_ref, channel + 3))
                )
            )
            bottom = products(
                *(
                    jnp.concatenate([cut(ref, channel, far), below[k, :, columns]])
                    for ref, k in ((image_ref, channel), (truth_ref, channel + 3))
                )
            )
            for kind in range(5):
                quantity = kind * 3 + channel
                values_ref[0] = top[kind]
                values_ref[1] = bottom[kind]
                ends = [
                    filtered(lambda k: values_ref[side, 3 + k : 3 + k + SUBS, :]) for side in range(2)
                ]
                middle = down_ref[quantity * wide + c, SUBS : height - SUBS, :]
                turned = jnp.concatenate([ends[0], middle, ends[1]], axis=0).T
                out_ref[quantity, columns, :] = turned


    near_ref[...], far_ref[...] = by_parity(
        "gs", out_ref[:, width - SUBS : width, :], out_ref[:, 0:SUBS, :]
    )


def similarity(parts):
    mean_r, mean_t, square_r, square_t, product = parts
    both, squares = mean_r * mean_t, mean_r * mean_r + mean_t * mean_t
    return (
        (2.0 * both + stable_one)
        * (2.0 * (product - both) + stable_two)
        / ((squares + stable_one) * (square_r + square_t - squares + stable_two))
    )


def across_kernel(turned_ref, image_ref, truth_ref, out_ref, sum_ref):
    length = turned_ref.shape[1]
    sum_ref[...] = jnp.zeros_like(sum_ref)

    def one(channel, carry):
        for r in range(1, length // SUBS - 1):
            parts = [
                filtered(
                    lambda k: turned_ref[
                        kind * 3 + channel, r * SUBS - 5 + k : r * SUBS + 3 + k, :
                    ]
                )
                for kind in range(5)
            ]
            rows = slice(r * SUBS, (r + 1) * SUBS)
            sum_ref[rows, :] = sum_ref[rows, :] + similarity(parts)
        return carry

    lax.fori_loop(0, 3, one, 0)
    for c in range(length // LANES):
        columns = slice(c * LANES, (c + 1) * LANES)
        mean = sum_ref[columns, :].T * (1.0 / 3.0)
        apart = [jnp.abs(image_ref[k, :, columns] - truth_ref[k, :, columns]) for k in range(3)]
        distance = (apart[0] + apart[1] + apart[2]) * (1.0 / 3.0)
        out_ref[:, columns] = (1.0 - ssim_share) * distance + ssim_share * (1.0 - mean)


def loss_kernel(turned_ref, near_in, far_in, partial_ref, out_ref, values_ref):
    length, height = turned_ref.shape[1:]
    before, after = arrived_sides("gs", near_in[...], far_in[...])
    ends = []
    for side in range(2):
        total = None
        for channel in range(3):
            parts = []
            for kind in range(5):
                quantity = kind * 3 + channel
                slot = quantity * 2 + side
                if side == 0:
                    values_ref[slot, 0:SUBS, :] = before[quantity]
                    values_ref[slot, SUBS : 3 * SUBS, :] = turned_ref[quantity, 0 : 2 * SUBS, :]
                else:
                    values_ref[slot, 0 : 2 * SUBS, :] = turned_ref[
                        quantity, length - 2 * SUBS : length, :
                    ]
                    values_ref[slot, 2 * SUBS : 3 * SUBS, :] = after[quantity]
                parts.append(filtered(lambda k: values_ref[slot, 3 + k : 3 + k + SUBS, :]))
            value = similarity(parts)
            total = value if total is None else total + value
        ends.append(total * (ssim_share / 3.0))
    wide = length // LANES
    blank = jnp.zeros((SUBS, height), jnp.float32)
    for c in range(wide):
        columns = slice(c * LANES, (c + 1) * LANES)
        blocks = [blank] * (LANES // SUBS)
        if c == 0:
            blocks[0] = ends[0]
        if c == wide - 1:
            blocks[-1] = ends[1]
        out_ref[:, columns] = partial_ref[:, columns] - jnp.concatenate(blocks, axis=0).T


def exchanged(near, far, axis, spare):
    axes = ("gs", "img")
    sizes = {name: lax.axis_size(name) for name in axes}
    size = sizes[axis]

    def flat(place):
        return place["gs"] * sizes["img"] + place["img"]

    pairs = [[], []]
    for along in range(size):
        for other in range(sizes[spare]):
            source = {axis: along, spare: other}
            pairs[0].append((flat(source), flat({axis: along ^ 1, spare: other})))
            if 0 < along < size - 1:
                target = {axis: ((along + 1) ^ 1) - 1, spare: other}
            else:
                target = {axis: along, spare: other ^ 1}
            pairs[1].append((flat(source), flat(target)))
    return lax.ppermute(near, axes, pairs[0]), lax.ppermute(far, axes, pairs[1])


def grant(mebibytes):
    return pltpu.CompilerParams(vmem_limit_bytes=mebibytes << 20)


VMEM = pl.BlockSpec(memory_space=pltpu.VMEM)
SMEM = pl.BlockSpec(memory_space=pltpu.SMEM)
ANY = pl.BlockSpec(memory_space=pltpu.HBM)


def on_device(gaussians, send_slots, tile_lists, truth):
    axes = ("gs", "img")
    devices = lax.axis_size(axes)
    cap = send_slots.shape[1] // devices
    count = gaussians.shape[1]
    rows_here, cols_here, list_len = tile_lists.shape
    tiles = rows_here * cols_here
    spans = -(-send_slots.shape[1] // SPAN)
    packed = pl.pallas_call(
        functools.partial(pack_kernel, cap),
        out_shape=jax.ShapeDtypeStruct((devices, SUBS, LANES), jnp.float32),
        in_specs=[ANY, ANY],
        out_specs=VMEM,
        scratch_shapes=[
            pltpu.VMEM(gaussians.shape, jnp.float32),
            pltpu.VMEM(send_slots.shape, jnp.int32),
            pltpu.VMEM((2 * SUBS, count), jnp.float32),
            pltpu.VMEM((devices + SUBS, LANES), jnp.int32),
            pltpu.VMEM((SUBS, 2 * SUBS, LANES), jnp.float32),
            pltpu.SemaphoreType.DMA((2,)),
        ],
        compiler_params=grant(60),
        name="pack",
    )(gaussians, send_slots)
    arrived = lax.all_to_all(packed, axes, split_axis=0, concat_axis=0, tiled=True)
    basis = basis_matrix()
    index, meta, centre, basis, truth = pl.pallas_call(
        functools.partial(sort_kernel, cols_here),
        out_shape=(
            jax.ShapeDtypeStruct((tiles, list_len), jnp.int32),
            jax.ShapeDtypeStruct((SUBS, tiles), jnp.int32),
            jax.ShapeDtypeStruct((2, tiles, LANES), jnp.float32),
            jax.ShapeDtypeStruct(basis.shape, basis.dtype),
            jax.ShapeDtypeStruct(truth.shape, jnp.float32),
        ),
        in_specs=[VMEM, ANY, ANY],
        out_specs=(VMEM,) * 5,
        scratch_shapes=[pltpu.SemaphoreType.DMA((2,))],
        compiler_params=grant(6),
        name="order",
    )(tile_lists.reshape(tiles, list_len), basis, truth)
    height, width = rows_here * TILE, cols_here * TILE
    wide = width // LANES

    def arrays(*shapes):
        return tuple(jax.ShapeDtypeStruct(shape, jnp.float32) for shape in shapes)

    def call(kernel, name, inputs, outputs, scratch):
        return pl.pallas_call(
            kernel,
            out_shape=outputs if len(outputs) > 1 else outputs[0],
            in_specs=[VMEM] * inputs,
            out_specs=(VMEM,) * len(outputs) if len(outputs) > 1 else VMEM,
            scratch_shapes=[pltpu.VMEM(shape, jnp.float32) for shape in scratch],
            compiler_params=grant(9),
            name=name,
        )

    image, near, far = pl.pallas_call(
        functools.partial(render_kernel, cap),
        out_shape=arrays((3, height, width), (6, SUBS, width), (6, SUBS, width)),
        in_specs=[SMEM] + [VMEM] * 5,
        out_specs=(VMEM,) * 3,
        scratch_shapes=[
            pltpu.VMEM((2 * SUBS, spans * SPAN), jnp.float32),
            pltpu.VMEM((-(-spans // 2) * 2 * SUBS, SPAN), jnp.bfloat16),
            pltpu.VMEM((SPAN, LANES), jnp.bfloat16),
            pltpu.VMEM(((SUBS + PARAMS) * SUBS, LANES), jnp.float32),
            pltpu.VMEM(((SUBS + PARAMS) * SUBS, LANES), jnp.float32),
            pltpu.VMEM((6, LANES + SUBS, LANES), jnp.float32),
            pltpu.VMEM((6, LANES + SUBS, LANES), jnp.float32),
            pltpu.VMEM((LANES, 2 * LANES), jnp.bfloat16),
            pltpu.VMEM((LANES, 2 * LANES), jnp.bfloat16),
            pltpu.VMEM((tiles // SUBS, 6, SUBS, LANES), jnp.float32),
            pltpu.VMEM((3, height // SUBS * wide, SUBS, LANES), jnp.float32),
        ],
        compiler_params=pltpu.CompilerParams(
            vmem_limit_bytes=12 << 20
        ),
        name="render",
    )(meta, arrived, index, centre, basis, truth)
    near, far = exchanged(near, far, "img", "gs")
    sums, rendered = pl.pallas_call(
        down_kernel,
        out_shape=arrays((15 * wide, height, LANES), (3, height, width)),
        in_specs=[VMEM, VMEM],
        out_specs=(VMEM, ANY),
        scratch_shapes=[
            pltpu.VMEM((15 * wide, height, LANES), jnp.float32),
            pltpu.SemaphoreType.DMA,
        ],
        compiler_params=grant(9),
        name="down",
    )(image, truth)
    turned, near, far = call(
        turn_kernel,
        "turn",
        5,
        arrays((15, width, height), (15, SUBS, height), (15, SUBS, height)),
        [(2, 3 * SUBS, LANES)],
    )(image, truth, near, far, sums)
    near, far = exchanged(near, far, "gs", "img")
    partial = call(across_kernel, "across", 3, arrays((height, width)), [(width, height)])(
        turned, image, truth
    )
    loss = call(loss_kernel, "loss", 4, arrays((height, width)), [(30, 3 * SUBS, height)])(
        turned, near, far, partial
    )
    return rendered, loss


def solution(mesh):
    return jax.shard_map(
        on_device,
        mesh=mesh,
        in_specs=(
            P(None, ("gs", "img")),
            P(("gs", "img"), None),
            P("img", "gs", None),
            P(None, "img", "gs"),
        ),
        out_specs=(P(None, "img", "gs"), P("img", "gs")),
        check_vma=False,
    )
```

```python
import functools

import jax
import jax.numpy as jnp
import numpy as np
from jax import lax
from jax.experimental import pallas as pl
from jax.experimental.pallas import tpu as pltpu
from jax.sharding import PartitionSpec as P

TILE = 16
LANES = 128
SUBS = 8
PARAMS = 9
UNROLL = 16
FUSED = 96
SPAN = 256
LOG2E = 1.4426950408889634

coef_zero = 0.28209479177387814
coef_one = 0.4886025119029199
coef_two = [
    1.0925484305920792,
    -1.0925484305920792,
    0.31539156525252005,
    -1.0925484305920792,
    0.5462742152960396,
]
coef_three = [
    -0.5900435899266435,
    2.890611442640554,
    -0.4570457994644658,
    0.3731763325901154,
    -0.4570457994644658,
    1.445305721320277,
    -0.5900435899266435,
]
camera_z = -3000.0
ssim_share = 0.2
stable_one = 0.0001
stable_two = 0.0009


def iota(shape, dim):
    return lax.broadcasted_iota(jnp.int32, shape, dim)


def lane_take(values, index):
    return jnp.take_along_axis(values, index, axis=1, mode="promise_in_bounds")


def sublane_take(values, index):
    return jnp.take_along_axis(values, index, axis=0, mode="promise_in_bounds")


def as_bf16(value):
    return value.astype(jnp.bfloat16).astype(jnp.float32)


def three_parts(value):
    high = as_bf16(value)
    rest = value - high
    middle = as_bf16(rest)
    return high, middle, rest - middle


def project(row):
    mean_x, mean_y, mean_z = row(0), row(1), row(2)
    squared = [jnp.exp(2.0 * row(3 + k)) for k in range(3)]
    quat = [row(6 + k) for k in range(4)]
    norm = jnp.sqrt(quat[0] * quat[0] + quat[1] * quat[1] + quat[2] * quat[2] + quat[3] * quat[3])
    quat_w, quat_x, quat_y, quat_z = [part / norm for part in quat]
    first = [
        1.0 - 2.0 * (quat_y * quat_y + quat_z * quat_z),
        2.0 * (quat_x * quat_y - quat_w * quat_z),
        2.0 * (quat_x * quat_z + quat_w * quat_y),
    ]
    second = [
        2.0 * (quat_x * quat_y + quat_w * quat_z),
        1.0 - 2.0 * (quat_x * quat_x + quat_z * quat_z),
        2.0 * (quat_y * quat_z - quat_w * quat_x),
    ]

    def weighted(left, right):
        return (
            left[0] * right[0] * squared[0]
            + left[1] * right[1] * squared[1]
            + left[2] * right[2] * squared[2]
        )

    cov_xx = weighted(first, first) + 0.3
    cov_xy = weighted(first, second)
    cov_yy = weighted(second, second) + 0.3
    determinant = cov_xx * cov_yy - cov_xy * cov_xy
    log_opacity = -LOG2E * jnp.log(1.0 + jnp.exp(-row(10)))
    delta_z = mean_z - camera_z
    length = jnp.sqrt(mean_x * mean_x + mean_y * mean_y + delta_z * delta_z)
    dir_x, dir_y, dir_z = (mean_x / length, mean_y / length, delta_z / length)
    sq_x, sq_y, sq_z = (dir_x * dir_x, dir_y * dir_y, dir_z * dir_z)
    prod_xy, prod_yz, prod_xz = (dir_x * dir_y, dir_y * dir_z, dir_x * dir_z)
    basis = [
        coef_zero * jnp.ones_like(dir_x),
        -coef_one * dir_y,
        coef_one * dir_z,
        -coef_one * dir_x,
        coef_two[0] * prod_xy,
        coef_two[1] * prod_yz,
        coef_two[2] * (2.0 * sq_z - sq_x - sq_y),
        coef_two[3] * prod_xz,
        coef_two[4] * (sq_x - sq_y),
        coef_three[0] * dir_y * (3.0 * sq_x - sq_y),
        coef_three[1] * prod_xy * dir_z,
        coef_three[2] * dir_y * (4.0 * sq_z - sq_x - sq_y),
        coef_three[3] * dir_z * (2.0 * sq_z - 3.0 * sq_x - 3.0 * sq_y),
        coef_three[4] * dir_x * (4.0 * sq_z - sq_x - sq_y),
        coef_three[5] * dir_z * (sq_x - sq_y),
        coef_three[6] * dir_x * (sq_x - 3.0 * sq_y),
    ]
    colours = []
    for channel in range(3):
        total = row(11 + 16 * channel) * basis[0]
        for k in range(1, 16):
            total = total + row(11 + 16 * channel + k) * basis[k]
        colours.append(jnp.maximum(total + 0.5, 0.0))
    return [log_opacity] + colours + [
        mean_x,
        mean_y,
        (-0.5 * LOG2E) * (cov_yy / determinant),
        LOG2E * (cov_xy / determinant),
        (-0.5 * LOG2E) * (cov_xx / determinant),
    ]


def pack_kernel(
    cap, gauss_in, send_in, out_ref, gauss_ref, send_ref, table_ref, index_ref, last_ref, sems
):
    copies = [
        pltpu.make_async_copy(send_in, send_ref, sems.at[0]),
        pltpu.make_async_copy(gauss_in, gauss_ref, sems.at[1]),
    ]
    for copy in copies:
        copy.start()
    targets = out_ref.shape[0]
    chunks = gauss_ref.shape[1] // LANES
    spare = LANES - cap
    extra_rows = -(-cap // spare)
    lane = iota((SUBS, LANES), 1)
    sub = iota((SUBS, LANES), 0)
    send_chunks = send_ref.shape[1] // LANES
    copies[0].wait()
    for target in range(targets):
        chunk, shift = divmod(target * cap, LANES)

        def piece(c):
            c = min(c, send_chunks - 1)
            return jnp.broadcast_to(send_ref[0:1, c * LANES : (c + 1) * LANES], (SUBS, LANES))

        index = piece(chunk)
        if shift:
            index = jnp.where(
                lane < LANES - shift,
                pltpu.roll(index, LANES - shift, axis=1),
                pltpu.roll(piece(chunk + 1), LANES - shift, axis=1),
            )
        index_ref[target : target + 1, :] = index[0:1, :]
    copies[1].wait()
    rows = project(lambda k: gauss_ref[k : k + 1, :])
    for k in range(PARAMS):
        table_ref[k : k + 1, :] = jnp.where(jnp.abs(rows[k]) < 1e30, rows[k], 0.0)

    def gather(index, value_of):
        low, high = index & (LANES - 1), index >> 7
        total = jnp.zeros((SUBS, LANES), jnp.float32)
        for c in range(chunks):
            part = lane_take(value_of(slice(c * LANES, (c + 1) * LANES)), low)
            total = jnp.where(high == c, part, total)
        return total

    def octet(o, carry):
        first = pl.multiple_of(o * SUBS, SUBS)
        last = gather(
            index_ref[pl.ds(first, SUBS), :],
            lambda at: jnp.broadcast_to(table_ref[SUBS : SUBS + 1, at], (SUBS, LANES)),
        )
        for r in range(extra_rows):
            last_ref[r, 0:SUBS, :] = pltpu.roll(last, (cap - r * spare) % LANES, axis=1)
        for k in range(SUBS):
            index = index_ref[pl.ds(first + k, SUBS, stride=0), :]
            result = gather(index, lambda at: table_ref[0:SUBS, at])
            for r in range(extra_rows):
                row = last_ref[r, pl.ds(k, SUBS, stride=0), :]
                result = jnp.where((lane >= cap) & (sub == r), row, result)
            out_ref[first + k] = result
        return carry

    lax.fori_loop(0, targets // SUBS, octet, 0)


def sort_kernel(
    cols_here,
    lists_ref,
    basis_in,
    truth_in,
    index_ref,
    meta_ref,
    centre_ref,
    basis_ref,
    truth_ref,
    sems,
):
    copies = [
        pltpu.make_async_copy(basis_in, basis_ref, sems.at[0]),
        pltpu.make_async_copy(truth_in, truth_ref, sems.at[1]),
    ]
    for copy in copies:
        copy.start()
    tiles, length = lists_ref.shape
    lists = lists_ref[...]
    live = jnp.sum((lists >= 0).astype(jnp.float32), axis=1, keepdims=True)
    live = jnp.broadcast_to(live, (tiles, tiles))
    down, across = iota((tiles, tiles), 0), iota((tiles, tiles), 1)
    live_row = jnp.sum(jnp.where(down == across, live, 0.0), axis=0, keepdims=True)
    ahead = (live > live_row) | ((live == live_row) & (down < across))
    rank_row = jnp.sum(ahead.astype(jnp.float32), axis=0, keepdims=True)
    behind = (live_row > live) | ((live_row == live) & (across < down))
    rank = jnp.sum(behind.astype(jnp.float32), axis=1, keepdims=True)
    select = (rank_row == down.astype(jnp.float32)).astype(jnp.float32)
    placed = (rank == across.astype(jnp.float32)).astype(jnp.float32)
    live_sorted = jnp.sum(placed * live, axis=0, keepdims=True)
    tile_sorted = jnp.sum(placed * down.astype(jnp.float32), axis=0, keepdims=True)
    tile_id = tile_sorted.astype(jnp.int32)
    row_of = lax.div(tile_id, cols_here)
    column = (tile_id - row_of * cols_here) * TILE
    busy = jnp.sum((live > (LANES * across).astype(jnp.float32)).astype(jnp.int32), axis=0, keepdims=True)
    meta_ref[0:1, :] = live_sorted.astype(jnp.int32)
    meta_ref[1:2, :] = row_of * (TILE // SUBS * (cols_here * TILE // LANES)) + (column >> 7)
    meta_ref[2:3, :] = column & (LANES - 1)
    meta_ref[4:5, :] = (busy + (2 * SUBS - 1)) >> 4
    tile = jnp.sum(select * across.astype(jnp.float32), axis=1, keepdims=True).astype(jnp.int32)
    tile = jnp.broadcast_to(tile, (tiles, tiles))
    tile_row = lax.div(tile, cols_here)
    tile_col = tile - tile_row * cols_here
    tile_row = tile_row + lax.axis_index("img") * (tiles // cols_here)
    tile_col = tile_col + lax.axis_index("gs") * cols_here
    centre_ref[0] = (tile_col * TILE + TILE // 2).astype(jnp.float32)
    centre_ref[1] = (tile_row * TILE + TILE // 2).astype(jnp.float32)
    high = (lists >> 7).astype(jnp.float32).astype(jnp.bfloat16)
    low = (lists & (LANES - 1)).astype(jnp.float32).astype(jnp.bfloat16)
    select = select.astype(jnp.bfloat16)
    high = jnp.dot(select, high, preferred_element_type=jnp.float32)
    low = jnp.dot(select, low, preferred_element_type=jnp.float32)
    index_ref[...] = high.astype(jnp.int32) * LANES + low.astype(jnp.int32)
    for copy in copies:
        copy.wait()


def basis_matrix():
    local = np.arange(TILE) - 7.5
    kinds = [[(0, local**0), (1, local), (2, local**2)], [(3, local**0), (4, local)]]
    kinds += [[(k, local**0)] for k in range(5, 9)]
    matrix = np.zeros((2 * LANES, len(kinds) * LANES), np.float32)
    for kind, terms in enumerate(kinds):
        for coefficient, values in terms:
            for part in range(3):
                for t in range(SUBS):
                    start = kind * LANES + t * TILE
                    matrix[(coefficient * 3 + part) * SUBS + t, start : start + TILE] = values
    return jnp.asarray(matrix, jnp.bfloat16)


def render_kernel(
    cap,
    meta_ref,
    recv_ref,
    index_ref,
    centre_ref,
    basis_ref,
    truth_ref,
    out_ref,
    near_ref,
    far_ref,
    table_ref,
    spread_ref,
    count_ref,
    params_a,
    params_b,
    rows_a,
    rows_b,
    stacked_a,
    stacked_b,
    done_ref,
    image_ref,
):
    wide = out_ref.shape[2] // LANES
    sources = recv_ref.shape[0]
    tiles, list_len = index_ref.shape
    spans = table_ref.shape[1] // SPAN
    chunks = spans * (SPAN // LANES)
    spare = LANES - cap
    lane = iota((SUBS, LANES), 1)
    sub = iota((SUBS, LANES), 0)
    if sources * cap < spans * SPAN:
        last_span = slice((spans - 1) * SPAN, spans * SPAN)
        table_ref[:, last_span] = jnp.zeros((2 * SUBS, SPAN), jnp.float32)
    for source in range(sources):
        value = recv_ref[source]
        last = jnp.zeros((SUBS, LANES), jnp.float32)
        for r in range(-(-cap // spare)):
            row = jnp.broadcast_to(value[r : r + 1, :], (SUBS, LANES))
            moved = pltpu.roll(row, (r * spare - cap) % LANES, axis=1)
            last = jnp.where((lane >= r * spare) & (lane < (r + 1) * spare), moved, last)
        chunk, shift = divmod(source * cap, LANES)
        here = min(cap, LANES - shift)
        if shift:
            value = pltpu.roll(value, shift, axis=1)
            last = pltpu.roll(last, shift, axis=1)
        for c, start, end, lo in ((chunk, shift, shift + here, 0), (chunk + 1, 0, cap - here, 1)):
            if end > start:
                table_ref[0:SUBS, c * LANES + start : c * LANES + end] = value[:, start:end]
                table_ref[SUBS : SUBS + 1, c * LANES + start : c * LANES + end] = last[0:1, start:end]

    zero = jnp.zeros((SUBS, LANES), jnp.float32)

    half = SUBS // 2
    wide_sub = iota((SUBS, SPAN), 0)
    pieces = []
    for c in range(spans):
        value = table_ref[0:SUBS, c * SPAN : (c + 1) * SPAN]
        high = as_bf16(value)
        rest = pltpu.roll(as_bf16(value - high), half, axis=0)
        pieces.append(jnp.where(wide_sub < half, high, rest))
    pieces += [jnp.zeros((SUBS, SPAN), jnp.float32)] * (len(pieces) % 2)
    spread_ref[...] = jnp.concatenate(pieces, axis=0).astype(jnp.bfloat16)
    count_ref[...] = iota((SPAN, LANES), 0).astype(jnp.float32).astype(jnp.bfloat16)
    hot_one = jnp.ones((SPAN, LANES), jnp.bfloat16)
    hot_zero = jnp.zeros((SPAN, LANES), jnp.bfloat16)

    def entries(at):
        g, b = at
        start = pl.multiple_of(g * SUBS, SUBS)
        return start, index_ref[pl.ds(start, SUBS), pl.ds(pl.multiple_of(b * LANES, LANES), LANES)]

    def gather(at, params_ref):
        index = jnp.maximum(entries(at)[1], 0)
        low, high = index & (LANES - 1), index >> 7
        params = [zero] * (PARAMS - half)
        for c in range(chunks):
            hit = high == c
            for p in range(PARAMS - half):
                row = table_ref[half + p : half + p + 1, c * LANES : (c + 1) * LANES]
                part = lane_take(jnp.broadcast_to(row, (SUBS, LANES)), low)
                params[p] = jnp.where(hit, part, params[p])
        for p in range(PARAMS - half):
            params_ref[(SUBS + p) * SUBS : (SUBS + p + 1) * SUBS, :] = params[p]
        low, high = (index & (SPAN - 1)).astype(jnp.float32), index >> 8
        for t in range(0, SUBS, 2):
            hot = []
            for k in range(2):
                row = jnp.broadcast_to(low[t + k : t + k + 1, :], (SPAN, LANES))
                hot.append(jnp.where(row.astype(jnp.bfloat16) == count_ref[...], hot_one, hot_zero))
            found = jnp.dot(
                spread_ref[...], jnp.concatenate(hot, axis=1), preferred_element_type=jnp.float32
            )
            for k in range(2):
                row = jnp.broadcast_to(high[t + k : t + k + 1, :], (SUBS, LANES))
                picked = zero
                for c in range(spans):
                    part = found[c * SUBS : (c + 1) * SUBS, k * LANES : (k + 1) * LANES]
                    picked = jnp.where(row == c, part, picked)
                params_ref[(t + k) * SUBS : (t + k + 1) * SUBS, :] = picked

    def prepare(at, params_ref, stacked_ref):
        start, index = entries(at)
        live = index >= 0
        log_opacity, red, green, blue = (
            params_ref[pl.ds(p, SUBS, stride=SUBS), :]
            + params_ref[pl.ds(p + half, SUBS, stride=SUBS), :]
            for p in range(half)
        )
        mean_x, mean_y, quad_x, quad_xy, quad_y = (
            params_ref[(SUBS + p) * SUBS : (SUBS + p + 1) * SUBS, :] for p in range(PARAMS - half)
        )
        u = mean_x - centre_ref[0, pl.ds(start, SUBS), :]
        v = mean_y - centre_ref[1, pl.ds(start, SUBS), :]
        slope_x = quad_x * u
        slope_y = quad_y * v
        constant = log_opacity + slope_x * u + slope_y * v + quad_xy * u * v
        values = [
            jnp.where(live, constant, -1e5),
            jnp.where(live, -2.0 * slope_x - quad_xy * v, 0.0),
            jnp.where(live, quad_x, 0.0),
            jnp.where(live, -2.0 * slope_y - quad_xy * u, 0.0),
            jnp.where(live, quad_xy, 0.0),
            jnp.where(live, quad_y, 0.0),
            red,
            green,
            blue,
        ]
        parts = [part for value in values for part in three_parts(value)]
        parts += [zero] * (2 * LANES // SUBS - len(parts))
        stacked_ref[...] = jnp.concatenate(parts, axis=0).T.astype(jnp.bfloat16)

    up = sub.astype(jnp.float32) + 0.5
    up_squared = up * up
    flip = (SUBS - 1) - sub
    one = jnp.ones((SUBS, LANES), jnp.float32)
    fresh = (one, one) + (zero,) * 6
    groups = tiles // SUBS

    def blend(rows_ref, first, amount, state):
        left_a, left_b, ra, ga, ba, rb, gb, bb = state
        for q in range(amount):
            def row(kind):
                return rows_ref[kind, pl.ds(first + q, SUBS, stride=0), :]

            even = row(0) + up_squared * row(2)
            odd = up * row(1)
            alpha_a = jnp.exp2(even - odd)
            alpha_b = jnp.exp2(even + odd)
            weight_a = left_a * alpha_a
            weight_b = left_b * alpha_b
            left_a = left_a - weight_a
            left_b = left_b - weight_b
            red, green, blue = row(3), row(4), row(5)
            ra, ga, ba = ra + weight_a * red, ga + weight_a * green, ba + weight_a * blue
            rb, gb, bb = rb + weight_b * red, gb + weight_b * green, bb + weight_b * blue
        return left_a, left_b, ra, ga, ba, rb, gb, bb

    def expand(stacked_ref, rows_ref):
        result = jnp.dot(stacked_ref[...], basis_ref[...], preferred_element_type=jnp.float32)
        for kind in range(6):
            rows_ref[kind, 0:LANES, :] = result[:, kind * LANES : (kind + 1) * LANES]

    def following(at):
        g, b = at
        more = (b + 1) * LANES < meta_ref[0, g * SUBS]
        return jnp.where(more, g, jnp.minimum(g + 1, groups - 1)), jnp.where(more, b + 1, 0)

    def finish(g, state):
        for k in range(6):
            done_ref[g, k] = state[2 + k]

    def place(g):
        halves = [done_ref[g, k] for k in range(6)]
        halves[0:3] = [sublane_take(value, flip) for value in halves[0:3]]
        for t in range(SUBS):
            where, shift = meta_ref[1, g * SUBS + t], meta_ref[2, g * SUBS + t]
            mask = (lane >= shift) & (lane < shift + TILE)
            for side in range(2):
                for channel in range(3):
                    moved = pltpu.roll(
                        halves[side * 3 + channel], (shift - t * TILE) & (LANES - 1), axis=1
                    )
                    pltpu.store(image_ref.at[channel, where + side * wide], moved, mask=mask)

    def turn(places, ready, state, rows_now, rows_next, stacked_next, stacked_free, params_now, params_free):
        now, first, second, third = places
        g, b = now
        state = tuple(jnp.where(b == 0, start, value) for start, value in zip(fresh, state))
        state = blend(rows_now, 0, FUSED, state)
        expand(stacked_next, rows_next)
        prepare(second, params_now, stacked_free)
        gather(third, params_free)
        place(ready)
        count = meta_ref[0, g * SUBS] - b * LANES
        rest = (jnp.clip(count - FUSED, 0, LANES - FUSED) + UNROLL - 1) // UNROLL

        def many(s, inner):
            return blend(rows_now, FUSED + s * UNROLL, UNROLL, inner)

        state = lax.fori_loop(0, rest, many, state)

        @pl.when(count <= LANES)
        def _():
            finish(g, state)

        ready = jnp.where(count <= LANES, g, ready)
        return (first, second, third, following(third)), ready, state

    def two(_, carry):
        carry = turn(*carry, rows_a, rows_b, stacked_b, stacked_a, params_a, params_b)
        return turn(*carry, rows_b, rows_a, stacked_a, stacked_b, params_b, params_a)

    def add_blocks(g, total):
        return total + jnp.maximum((meta_ref[0, g * SUBS] + LANES - 1) // LANES, 1)

    blocks = lax.fori_loop(0, groups, add_blocks, 0)
    places = [(jnp.int32(0), jnp.int32(0))]
    for _ in range(3):
        places.append(following(places[-1]))
    gather(places[0], params_a)
    gather(places[1], params_b)
    prepare(places[0], params_a, stacked_a)
    expand(stacked_a, rows_a)
    prepare(places[1], params_b, stacked_b)
    gather(places[2], params_a)
    lax.fori_loop(0, (blocks + 1) // 2, two, (tuple(places), jnp.int32(0), fresh))
    place(groups - 1)

    height = out_ref.shape[1]
    for channel in range(3):
        for r in range(height // SUBS):
            for c in range(wide):
                rows, columns = slice(r * SUBS, (r + 1) * SUBS), slice(c * LANES, (c + 1) * LANES)
                out_ref[channel, rows, columns] = image_ref[channel, r * wide + c]
    sides = [
        jnp.concatenate([out_ref[:, rows, :], truth_ref[:, rows, :]])
        for rows in (slice(0, SUBS), slice(height - SUBS, height))
    ]
    near_ref[...], far_ref[...] = by_parity("img", sides[1], sides[0])


def by_parity(axis, first, second):
    even = lax.axis_index(axis) & 1 == 0
    return jnp.where(even, first, second), jnp.where(even, second, first)


def arrived_sides(axis, near, far):
    index, size = lax.axis_index(axis), lax.axis_size(axis)
    before, after = by_parity(axis, far, near)
    return (
        jnp.where(index == 0, 0.0, before),
        jnp.where(index == size - 1, 0.0, after),
    )


def window():
    offsets = np.arange(11) - 5.0
    weights = np.exp(-offsets * offsets / 4.5)
    return [float(weight) for weight in weights / weights.sum()]


def filtered(load):
    weights = window()
    total = load(5) * weights[5]
    for k in range(5):
        total = total + (load(k) + load(10 - k)) * weights[k]
    return total


def products(image, truth):
    return [image, truth, image * image, truth * truth, image * truth]


def down_kernel(image_ref, truth_ref, out_ref, copy_ref, values_ref, sem):
    copy = pltpu.make_async_copy(image_ref, copy_ref, sem)
    copy.start()
    _, height, width = image_ref.shape
    wide = width // LANES
    for channel in range(3):
        for c in range(wide):
            columns = slice(c * LANES, (c + 1) * LANES)
            parts = products(image_ref[channel, :, columns], truth_ref[channel, :, columns])
            for kind, part in enumerate(parts):
                values_ref[(kind * 3 + channel) * wide + c] = part

    def one(slot, carry):
        for r in range(1, height // SUBS - 1):
            out_ref[slot, r * SUBS : (r + 1) * SUBS, :] = filtered(
                lambda k: values_ref[slot, r * SUBS - 5 + k : r * SUBS + 3 + k, :]
            )
        return carry

    lax.fori_loop(0, out_ref.shape[0], one, 0)
    copy.wait()


def turn_kernel(
    image_ref, truth_ref, near_in, far_in, down_ref, out_ref, near_ref, far_ref, values_ref
):
    _, height, width = image_ref.shape
    wide = width // LANES
    above, below = arrived_sides("img", near_in[...], far_in[...])
    for channel in range(3):
        for c in range(wide):
            columns = slice(c * LANES, (c + 1) * LANES)

            def cut(ref, which, rows):
                return ref[which, rows, columns]

            near, far = slice(0, 2 * SUBS), slice(height - 2 * SUBS, height)
            top = products(
                *(
                    jnp.concatenate([above[k, :, columns], cut(ref, channel, near)])
                    for ref, k in ((image_ref, channel), (truth_ref, channel + 3))
                )
            )
            bottom = products(
                *(
                    jnp.concatenate([cut(ref, channel, far), below[k, :, columns]])
                    for ref, k in ((image_ref, channel), (truth_ref, channel + 3))
                )
            )
            for kind in range(5):
                quantity = kind * 3 + channel
                values_ref[0] = top[kind]
                values_ref[1] = bottom[kind]
                ends = [
                    filtered(lambda k: values_ref[side, 3 + k : 3 + k + SUBS, :]) for side in range(2)
                ]
                middle = down_ref[quantity * wide + c, SUBS : height - SUBS, :]
                turned = jnp.concatenate([ends[0], middle, ends[1]], axis=0).T
                out_ref[quantity, columns, :] = turned


    for quantity in range(15):
        rows = slice(quantity * 5, quantity * 5 + 5)
        near_ref[rows, :], far_ref[rows, :] = by_parity(
            "gs", out_ref[quantity, width - 5 : width, :], out_ref[quantity, 0:5, :]
        )


def similarity(parts):
    mean_r, mean_t, square_r, square_t, product = parts
    both, squares = mean_r * mean_t, mean_r * mean_r + mean_t * mean_t
    return (
        (2.0 * both + stable_one)
        * (2.0 * (product - both) + stable_two)
        / ((squares + stable_one) * (square_r + square_t - squares + stable_two))
    )


def across_kernel(turned_ref, image_ref, truth_ref, out_ref, sum_ref):
    length = turned_ref.shape[1]
    sum_ref[...] = jnp.zeros_like(sum_ref)

    def one(channel, carry):
        for r in range(1, length // SUBS - 1):
            parts = [
                filtered(
                    lambda k: turned_ref[
                        kind * 3 + channel, r * SUBS - 5 + k : r * SUBS + 3 + k, :
                    ]
                )
                for kind in range(5)
            ]
            rows = slice(r * SUBS, (r + 1) * SUBS)
            sum_ref[rows, :] = sum_ref[rows, :] + similarity(parts)
        return carry

    lax.fori_loop(0, 3, one, 0)
    for c in range(length // LANES):
        columns = slice(c * LANES, (c + 1) * LANES)
        mean = sum_ref[columns, :].T * (1.0 / 3.0)
        apart = [jnp.abs(image_ref[k, :, columns] - truth_ref[k, :, columns]) for k in range(3)]
        distance = (apart[0] + apart[1] + apart[2]) * (1.0 / 3.0)
        out_ref[:, columns] = (1.0 - ssim_share) * distance + ssim_share * (1.0 - mean)


def loss_kernel(turned_ref, near_in, far_in, partial_ref, out_ref, values_ref):
    length, height = turned_ref.shape[1:]
    before, after = arrived_sides("gs", near_in[...], far_in[...])
    ends = []
    for side in range(2):
        total = None
        for channel in range(3):
            parts = []
            for kind in range(5):
                quantity = kind * 3 + channel
                slot = quantity * 2 + side
                if side == 0:
                    values_ref[slot, 3:SUBS, :] = before[quantity * 5 : quantity * 5 + 5]
                    values_ref[slot, SUBS : 3 * SUBS, :] = turned_ref[quantity, 0 : 2 * SUBS, :]
                else:
                    values_ref[slot, 0 : 2 * SUBS, :] = turned_ref[
                        quantity, length - 2 * SUBS : length, :
                    ]
                    values_ref[slot, 2 * SUBS : 2 * SUBS + 5, :] = after[
                        quantity * 5 : quantity * 5 + 5
                    ]
                parts.append(filtered(lambda k: values_ref[slot, 3 + k : 3 + k + SUBS, :]))
            value = similarity(parts)
            total = value if total is None else total + value
        ends.append(total * (ssim_share / 3.0))
    wide = length // LANES
    blank = jnp.zeros((SUBS, height), jnp.float32)
    for c in range(wide):
        columns = slice(c * LANES, (c + 1) * LANES)
        blocks = [blank] * (LANES // SUBS)
        if c == 0:
            blocks[0] = ends[0]
        if c == wide - 1:
            blocks[-1] = ends[1]
        out_ref[:, columns] = partial_ref[:, columns] - jnp.concatenate(blocks, axis=0).T


def exchanged(near, far, axis, spare):
    axes = ("gs", "img")
    sizes = {name: lax.axis_size(name) for name in axes}
    size = sizes[axis]

    def flat(place):
        return place["gs"] * sizes["img"] + place["img"]

    pairs = [[], []]
    for along in range(size):
        for other in range(sizes[spare]):
            source = {axis: along, spare: other}
            pairs[0].append((flat(source), flat({axis: along ^ 1, spare: other})))
            if 0 < along < size - 1:
                target = {axis: ((along + 1) ^ 1) - 1, spare: other}
            else:
                target = {axis: along, spare: other ^ 1}
            pairs[1].append((flat(source), flat(target)))
    return lax.ppermute(near, axes, pairs[0]), lax.ppermute(far, axes, pairs[1])


def grant(mebibytes):
    return pltpu.CompilerParams(vmem_limit_bytes=mebibytes << 20)


VMEM = pl.BlockSpec(memory_space=pltpu.VMEM)
SMEM = pl.BlockSpec(memory_space=pltpu.SMEM)
ANY = pl.BlockSpec(memory_space=pltpu.HBM)


def on_device(gaussians, send_slots, tile_lists, truth):
    axes = ("gs", "img")
    devices = lax.axis_size(axes)
    cap = send_slots.shape[1] // devices
    count = gaussians.shape[1]
    rows_here, cols_here, list_len = tile_lists.shape
    tiles = rows_here * cols_here
    spans = -(-send_slots.shape[1] // SPAN)
    packed = pl.pallas_call(
        functools.partial(pack_kernel, cap),
        out_shape=jax.ShapeDtypeStruct((devices, SUBS, LANES), jnp.float32),
        in_specs=[ANY, ANY],
        out_specs=VMEM,
        scratch_shapes=[
            pltpu.VMEM(gaussians.shape, jnp.float32),
            pltpu.VMEM(send_slots.shape, jnp.int32),
            pltpu.VMEM((2 * SUBS, count), jnp.float32),
            pltpu.VMEM((devices + SUBS, LANES), jnp.int32),
            pltpu.VMEM((SUBS, 2 * SUBS, LANES), jnp.float32),
            pltpu.SemaphoreType.DMA((2,)),
        ],
        compiler_params=grant(60),
        name="pack",
    )(gaussians, send_slots)
    arrived = lax.all_to_all(packed, axes, split_axis=0, concat_axis=0, tiled=True)
    basis = basis_matrix()
    index, meta, centre, basis, truth = pl.pallas_call(
        functools.partial(sort_kernel, cols_here),
        out_shape=(
            jax.ShapeDtypeStruct((tiles, list_len), jnp.int32),
            jax.ShapeDtypeStruct((SUBS, tiles), jnp.int32),
            jax.ShapeDtypeStruct((2, tiles, LANES), jnp.float32),
            jax.ShapeDtypeStruct(basis.shape, basis.dtype),
            jax.ShapeDtypeStruct(truth.shape, jnp.float32),
        ),
        in_specs=[VMEM, ANY, ANY],
        out_specs=(VMEM,) * 5,
        scratch_shapes=[pltpu.SemaphoreType.DMA((2,))],
        compiler_params=grant(6),
        name="order",
    )(tile_lists.reshape(tiles, list_len), basis, truth)
    height, width = rows_here * TILE, cols_here * TILE
    wide = width // LANES

    def arrays(*shapes):
        return tuple(jax.ShapeDtypeStruct(shape, jnp.float32) for shape in shapes)

    def call(kernel, name, inputs, outputs, scratch):
        return pl.pallas_call(
            kernel,
            out_shape=outputs if len(outputs) > 1 else outputs[0],
            in_specs=[VMEM] * inputs,
            out_specs=(VMEM,) * len(outputs) if len(outputs) > 1 else VMEM,
            scratch_shapes=[pltpu.VMEM(shape, jnp.float32) for shape in scratch],
            compiler_params=grant(9),
            name=name,
        )

    image, near, far = pl.pallas_call(
        functools.partial(render_kernel, cap),
        out_shape=arrays((3, height, width), (6, SUBS, width), (6, SUBS, width)),
        in_specs=[SMEM] + [VMEM] * 5,
        out_specs=(VMEM,) * 3,
        scratch_shapes=[
            pltpu.VMEM((2 * SUBS, spans * SPAN), jnp.float32),
            pltpu.VMEM((-(-spans // 2) * 2 * SUBS, SPAN), jnp.bfloat16),
            pltpu.VMEM((SPAN, LANES), jnp.bfloat16),
            pltpu.VMEM(((SUBS + PARAMS) * SUBS, LANES), jnp.float32),
            pltpu.VMEM(((SUBS + PARAMS) * SUBS, LANES), jnp.float32),
            pltpu.VMEM((6, LANES + SUBS, LANES), jnp.float32),
            pltpu.VMEM((6, LANES + SUBS, LANES), jnp.float32),
            pltpu.VMEM((LANES, 2 * LANES), jnp.bfloat16),
            pltpu.VMEM((LANES, 2 * LANES), jnp.bfloat16),
            pltpu.VMEM((tiles // SUBS, 6, SUBS, LANES), jnp.float32),
            pltpu.VMEM((3, height // SUBS * wide, SUBS, LANES), jnp.float32),
        ],
        compiler_params=pltpu.CompilerParams(
            vmem_limit_bytes=12 << 20
        ),
        name="render",
    )(meta, arrived, index, centre, basis, truth)
    near, far = exchanged(near, far, "img", "gs")
    sums, rendered = pl.pallas_call(
        down_kernel,
        out_shape=arrays((15 * wide, height, LANES), (3, height, width)),
        in_specs=[VMEM, VMEM],
        out_specs=(VMEM, ANY),
        scratch_shapes=[
            pltpu.VMEM((15 * wide, height, LANES), jnp.float32),
            pltpu.SemaphoreType.DMA,
        ],
        compiler_params=grant(9),
        name="down",
    )(image, truth)
    turned, near, far = call(
        turn_kernel,
        "turn",
        5,
        arrays((15, width, height), (10 * SUBS, height), (10 * SUBS, height)),
        [(2, 3 * SUBS, LANES)],
    )(image, truth, near, far, sums)
    near, far = exchanged(near, far, "gs", "img")
    partial = call(across_kernel, "across", 3, arrays((height, width)), [(width, height)])(
        turned, image, truth
    )
    loss = call(loss_kernel, "loss", 4, arrays((height, width)), [(30, 3 * SUBS, height)])(
        turned, near, far, partial
    )
    return rendered, loss


def solution(mesh):
    return jax.shard_map(
        on_device,
        mesh=mesh,
        in_specs=(
            P(None, ("gs", "img")),
            P(("gs", "img"), None),
            P("img", "gs", None),
            P(None, "img", "gs"),
        ),
        out_specs=(P(None, "img", "gs"), P("img", "gs")),
        check_vma=False,
    )
```
